32 devices in a mesh: mem: 4 (over x, core), tile: 8 (over z, y).
Axes of the slice: x: 2, y: 2, z: 4, core: 2. Of those that a mesh axis runs over, the one named last changes fastest.
Arguments:
- increment: float32 [70, 128, 256], P(None, 'tile')
- previous: float32 [70, 128, 256], P(None, 'tile'), may hold values from -6 to 6
- beta_prev: float32 [1], replicated, may hold values from 0.5 to 1.5
- members: bfloat16 [8, 70, 128, 256], P('mem', None, 'tile'), may hold values from -6 to 6
- band_widths: int32 [70], replicated, may hold values from 1 to 8, as said below
- diffusion_steps: int32 [8], replicated, may hold values from 1 to 4, as said below
Outputs:
- next_vector: float32 [70, 128, 256], P(None, 'tile')
- coefficients: float32 [2], replicated
The draws below stay inside these ranges and needn't reach their ends.
Inputs may be any that keep to these rules, and one draw needn't show every extreme that they name: `band_widths`: every level's band width lies in the range and some level has exactly 8. `diffusion_steps`: every tile's iteration count lies in the range and some tile has exactly 4.
All inputs are finite; a program needn't handle non-finite values.
Results may differ from the reference program's by a relative error of at most 0.0003.
Values sent between devices are 32-bit elements; how exact they have to be, the bound alone decides.
No kernel may reach another device: no remote copies, remote signals or barrier semaphores. Data moves between devices by JAX's collectives and lax.ppermute only.
A program may use at most 64 MiB of HBM per device.

```python
import math
import jax
import jax.numpy as jnp
from jax import lax

LEV = 70
HY = 16
NX = 256
DIFF = 4
BAND = 8
MEMBERS = 8
TILES = 8
NY = 128


def draw_band_widths(key, part):
    widths = jax.random.randint(key, (LEV,), 1, BAND + 1, dtype=jnp.int32)
    where_top = jax.random.randint(jax.random.fold_in(key, 7), (), 0, LEV, dtype=jnp.int32)
    return widths.at[where_top].set(BAND)


def draw_diffusion_steps(key, part):
    counts = jax.random.randint(key, (TILES,), 1, DIFF + 1, dtype=jnp.int32)
    where_top = jax.random.randint(jax.random.fold_in(key, 11), (), 0, TILES, dtype=jnp.int32)
    return counts.at[where_top].set(DIFF)


def draw_increment(key, part):
    key_base = jax.random.fold_in(key, 1)
    key_lev = jax.random.fold_in(key, 2)
    key_col = jax.random.fold_in(key, 3)
    level_scale = jnp.exp(jax.random.uniform(key_lev, (LEV, 1, 1), jnp.float32, 0.0, math.log(3.0)))
    column_scale = jnp.exp(jax.random.uniform(key_col, (1, 1, NX), jnp.float32, 0.0, math.log(3.0)))
    row_frac = jnp.arange(NY, dtype=jnp.float32)[None, :, None] / max(NY - 1, 1)
    base = jax.random.normal(key_base, (LEV, NY, NX), jnp.float32)
    row_scale = jnp.exp(row_frac * math.log(3.0))
    return (base * level_scale * row_scale * column_scale).astype(jnp.float32)


def steps_of(stream_key, dims, pieces, smallest, high):
    factor_of, own = 1.0, jax.random.fold_in(stream_key, 6)
    for dim, parts in pieces:
        steps = jnp.exp(jax.random.uniform(jax.random.fold_in(own, dim), (parts,), jnp.float32, smallest / len(pieces), high / len(pieces)))
        factor_of = factor_of * jnp.repeat(steps, dims[dim] // parts).reshape([-1 if axis == dim else 1 for axis in range(len(dims))])
    return factor_of


def gaussian(key, dims, scale, most, cuts=(), kind=jnp.bfloat16):
    entries = jax.random.normal(key, dims, jnp.float32) * scale
    if len(cuts) > 0:
        entries = steps_of(key, dims, cuts, -0.22, 0.18) * entries
    return jnp.clip(entries, min=-most, max=most).astype(kind)


def setup_inputs(seed: int = 0) -> dict:
    key_list = jax.random.split(jax.random.key(seed), 7)
    return {
        "increment": draw_increment(jax.random.fold_in(key_list[6], 71), 0),
        "previous": gaussian(key_list[1], (LEV, NY, NX), 1.0, 6.0, ((1, 8),), jnp.float32),
        "beta_prev": jnp.clip(jax.random.uniform(key_list[2], (1,), jnp.float32, 0.5, 1.5), 0.5, 1.5),
        "members": gaussian(key_list[3], (MEMBERS, LEV, NY, NX), 1.0, 6.0, ((0, 4), (2, 8))),
        "band_widths": draw_band_widths(jax.random.fold_in(key_list[6], 71), 0),
        "diffusion_steps": draw_diffusion_steps(jax.random.fold_in(key_list[6], 71), 0),
    }


def vertical_matrix(band_widths):
    levels = jnp.arange(band_widths.shape[0], dtype=jnp.int32)
    apart = levels[:, None] - levels[None, :]
    band_float = band_widths.astype(jnp.float32)
    limit = jnp.minimum(band_widths[:, None], band_widths[None, :])
    weight = jnp.exp(-apart.astype(jnp.float32) ** 2 / (band_float[:, None] * band_float[None, :]))
    return jnp.where(jnp.abs(apart) <= limit, weight, jnp.float32(0.0))

def reference(increment, previous, beta_prev, members, band_widths, diffusion_steps):
    vertical = vertical_matrix(band_widths)
    row_counts = jnp.repeat(diffusion_steps, HY)[None, :, None]

    def one_member(summed, member):
        member_f = member.astype(jnp.float32)
        localized = jnp.einsum('ij,jyx->iyx', vertical, member_f * increment, precision=lax.Precision.HIGHEST)
        for sweep_index in range(DIFF):
            padded = jnp.pad(localized, ((0, 0), (1, 1), (1, 1)))
            laplace = padded[:, 2:, 1:-1] + padded[:, :-2, 1:-1] + padded[:, 1:-1, 2:] + padded[:, 1:-1, :-2] - 4.0 * localized
            localized = jnp.where(sweep_index < row_counts, localized + 0.24 * laplace, localized)
        return (summed + member_f * localized, None)
    summed, _ = lax.scan(one_member, jnp.zeros(increment.shape, jnp.float32), members)
    image = increment + summed * (1.0 / (MEMBERS - 1))
    alpha_value = jnp.sum(increment * image) / jnp.sum(increment * increment)
    residual = image - alpha_value * increment - beta_prev[0] * previous
    scale_value = jnp.sqrt(jnp.sum(residual * residual) / (LEV * NY * NX) + 1e-06)
    return (residual / scale_value, jnp.stack([alpha_value, scale_value]).astype(jnp.float32))
```

```python
import functools

import jax
import jax.numpy as jnp
from jax import lax
from jax.experimental import pallas as pl
from jax.experimental.pallas import tpu as pltpu
from jax.sharding import PartitionSpec as P

DIFF = 4
RATE = 0.24
F32 = jnp.float32
VMEM_LIMIT = 48 * 1024 * 1024


def up_to(value, unit):
    return -(-value // unit) * unit


def vmem():
    return pl.BlockSpec(memory_space=pltpu.VMEM)


def smem():
    return pl.BlockSpec(memory_space=pltpu.SMEM)


def grid_row(tile, row, rows):
    return jnp.where(tile % 2 == 0, row, rows - 1 - row)


def put_flat(ref, value):
    for piece in range(ref.shape[0]):
        ref[piece, : value.shape[0], :] = value[:, piece * 128 : (piece + 1) * 128]


def strided(ref, start, count, stride):
    pieces = [ref[piece, pl.ds(start, count, stride=stride), :] for piece in range(ref.shape[0])]
    return jnp.concatenate(pieces, axis=1)


def sweep_counts(steps_ref, tile, tiles):
    even = tile % 2 == 0
    near = jnp.where(even, tile + 1, tile - 1)
    far = jnp.where(even, tile - 1, tile + 1)

    def count(index):
        inside = (index >= 0) & (index < tiles)
        return jnp.where(inside, steps_ref[jnp.clip(index, 0, tiles - 1)], 0)

    return count(tile), count(near), count(far)


def coefficient(sweep, count):
    return jnp.where(sweep < count, F32(RATE), F32(0.0))


def build_vertical(bands_ref, pad_ref, levels):
    pad_ref[...] = jnp.ones(pad_ref.shape, F32)
    pad_ref[0:1, 0:levels] = bands_ref[...].astype(F32)
    across = jnp.broadcast_to(pad_ref[0:1, :], (128, 128))
    down = across.T
    i = lax.broadcasted_iota(jnp.int32, (128, 128), 0)
    j = lax.broadcasted_iota(jnp.int32, (128, 128), 1)
    apart = (i - j).astype(F32)
    weight = jnp.exp(-(apart * apart) / (down * across))
    keep = (jnp.abs(apart) <= jnp.minimum(down, across)) & (i < levels) & (j < levels)
    full = jnp.where(keep, weight, F32(0.0))[: up_to(levels, 8), : up_to(levels, 16)]
    high = full.astype(jnp.bfloat16)
    return high, (full - high.astype(F32)).astype(jnp.bfloat16)


def apply_vertical(vertical, field):
    v_high, v_low = vertical
    high = field.astype(jnp.bfloat16)
    low = (field - high.astype(F32)).astype(jnp.bfloat16)
    dot = functools.partial(jnp.dot, preferred_element_type=F32)
    return dot(v_high, high) + dot(v_high, low) + dot(v_low, high)


def left_of(field):
    lane = lax.broadcasted_iota(jnp.int32, field.shape, field.ndim - 1)
    return jnp.where(lane == 0, F32(0.0), pltpu.roll(field, 1, field.ndim - 1))


def right_of(field):
    width = field.shape[-1]
    lane = lax.broadcasted_iota(jnp.int32, field.shape, field.ndim - 1)
    return jnp.where(lane == width - 1, F32(0.0), pltpu.roll(field, width - 1, field.ndim - 1))


def edge_kernel(rows, levels, bands_ref, members_ref, inc_ref, near_ref, far_ref, prod_ref, pad_ref):
    tile = lax.axis_index("tile")
    vertical = build_vertical(bands_ref, pad_ref, levels)
    deep = up_to(levels, 16)
    total = rows * levels
    width = inc_ref.shape[-1]
    for m in range(members_ref.shape[0]):
        put_flat(prod_ref.at[m], members_ref[m].astype(F32) * inc_ref[...])
        prod_ref[m, :, total:, :] = jnp.zeros((width // 128, prod_ref.shape[2] - total, 128), F32)
    for out_ref, base, sign in ((near_ref, rows - 1, -1), (far_ref, 0, 1)):
        for m in range(members_ref.shape[0]):
            for q in range(DIFF):
                row = grid_row(tile, base + sign * q, rows)
                field = strided(prod_ref.at[m], row, deep, rows)
                out_ref[m, q] = apply_vertical(vertical, field)


def own_kernel(
    rows, levels, tiles,
    bands_ref, steps_ref, members_ref, inc_ref, prev_ref,
    mine_ref, theirs_ref, cov_near_ref, cov_far_ref, mem_near_ref, mem_far_ref, inc_t_ref, prev_t_ref,
    prod_ref, memf_ref, one_ref, two_ref, pad_ref,
):
    tile = lax.axis_index("tile")
    half = lax.axis_index("mem") % 2
    counts = sweep_counts(steps_ref, tile, tiles)
    vertical = build_vertical(bands_ref, pad_ref, levels)
    deep, tall = up_to(levels, 16), up_to(levels, 8)
    total = rows * levels
    width = inc_ref.shape[-1]
    blank = jnp.zeros((width // 128, prod_ref.shape[1] - total, 128), F32)
    prod_ref[:, total:, :] = blank
    memf_ref[:, total:, :] = blank

    def transpose_to(ref):
        def body(row, _):
            ref[row] = strided(prod_ref, grid_row(tile, row, rows), tall, rows)
            return 0

        lax.fori_loop(0, rows, body, 0)

    put_flat(prod_ref, inc_ref[...])
    transpose_to(inc_t_ref)
    put_flat(prod_ref, prev_ref[...])
    transpose_to(prev_t_ref)
    zero = jnp.zeros((tall, width), F32)
    two_ref[0] = zero
    two_ref[rows + 5] = zero
    for m in range(members_ref.shape[0]):
        as_float = members_ref[m].astype(F32)
        put_flat(memf_ref, as_float)
        put_flat(prod_ref, as_float * inc_ref[...])
        for index in (0, 1, 2, rows + 3, rows + 4, rows + 5):
            one_ref[index] = zero

        def localize(row, _):
            field = strided(prod_ref, grid_row(tile, row, rows), deep, rows)
            one_ref[row + 3] = apply_vertical(vertical, field)
            return 0

        lax.fori_loop(0, rows, localize, 0)
        source, target = one_ref, two_ref
        for sweep in range(DIFF):
            own, near, far = (coefficient(sweep, count) for count in counts)

            def diffuse(index, _, source=source, target=target, own=own, near=near, far=far):
                rate = jnp.where(index < 3, far, jnp.where(index < rows + 3, own, near))
                here = source[index]
                around = source[index - 1] + source[index + 1] + left_of(here) + right_of(here)
                target[index] = here + rate * (around - 4.0 * here)
                return 0

            lax.fori_loop(1, rows + 5, diffuse, 0)
            source, target = target, source

        def member_row(row):
            return strided(memf_ref, grid_row(tile, row, rows), tall, rows)

        def add_to(ref, index, value):
            if m == 0:
                ref[index] = value
            else:
                ref[index] = ref[index] + value

        for q in range(DIFF):
            far_row, near_row = member_row(q), member_row(rows - 1 - q)
            mem_far_ref[m, q] = far_row
            mem_near_ref[m, q] = near_row
            add_to(cov_far_ref, q, far_row * source[q + 3])
            add_to(cov_near_ref, q, near_row * source[rows + 2 - q])
        part = (rows - 2 * DIFF) // 2
        for q in range(part):
            for ref, which in ((mine_ref, half), (theirs_ref, 1 - half)):
                row = DIFF + which * part + q
                add_to(ref, q, member_row(row) * source[row + 3])


def halo_kernel(near, tiles, steps_ref, halo_ref, mem_ref, cov_ref, out_ref):
    own_count, near_count, far_count = sweep_counts(steps_ref, lax.axis_index("tile"), tiles)
    own = [coefficient(k, own_count) for k in range(DIFF)]
    other = [coefficient(k, near_count if near else far_count) for k in range(DIFF)]

    def chunk(index, _):
        at = pl.ds(pl.multiple_of(index * 8, 8), 8)
        sums = [cov_ref[q, at, :] for q in range(DIFF)]
        for m in range(halo_ref.shape[0]):
            field = [None] * DIFF + [halo_ref[m, q, at, :] for q in range(DIFF)]
            for k in range(DIFF):
                new = list(field)
                for p in range(DIFF - 1 - k, 2 * DIFF - 1 - k):
                    rate = own[k] if p < DIFF else other[k]
                    around = field[p + 1]
                    if field[p] is not None:
                        here = field[p]
                        around = around + left_of(here) + right_of(here) - 4.0 * here
                        if p > 0 and field[p - 1] is not None:
                            around = around + field[p - 1]
                        new[p] = here + rate * around
                    else:
                        new[p] = rate * around
                field = new
            for q in range(DIFF):
                sums[q] = sums[q] + mem_ref[m, q, at, :] * field[DIFF - 1 - q]
        for q in range(DIFF):
            out_ref[q, at, :] = sums[q]
        return 0

    lax.fori_loop(0, halo_ref.shape[2] // 8, chunk, 0)


def reduced(value):
    return jnp.sum(value, axis=(0, 1), keepdims=True).reshape(1, 1)


def ratio(top, bottom):
    some = bottom != 0.0
    return jnp.where(some, top / jnp.where(some, bottom, F32(1.0)), F32(0.0))


def weighted(cov, inverse, prev, beta):
    return inverse * cov - beta * prev


def bulk_kernel(
    rows, inverse, halves,
    beta_ref, first_ref, second_ref, near_a_ref, near_b_ref, inc_ref, prev_ref, w_ref, sums_ref,
):
    beta = beta_ref[0]
    part = (rows - 2 * DIFF) // 2
    zero = jnp.zeros(inc_ref.shape[1:], F32)
    own_half = lax.axis_index("mem") % 2

    def rows_of():
        for q in range(part):
            yield DIFF + q, lambda q=q: jnp.where(own_half == 0, first_ref[q], second_ref[q])
        for q in range(part):
            yield DIFF + part + q, lambda q=q: jnp.where(own_half == 0, second_ref[q], first_ref[q])
        for q in range(DIFF):
            yield rows - 1 - q, lambda q=q: near_a_ref[q] + near_b_ref[q]

    square, cross = zero, zero
    for row, cov in rows_of():
        inc = inc_ref[row]
        scaled = inverse * cov()
        square = square + inc * inc
        cross = cross + inc * scaled
        w_ref[row - DIFF] = scaled - beta * prev_ref[row]
    square, cross = reduced(square), reduced(cross)
    pivot = ratio(cross, square)
    mixed, rest = zero, zero
    for row in range(DIFF, rows):
        inc = inc_ref[row]
        apart = w_ref[row - DIFF] - pivot * inc
        mixed = mixed + apart * inc
        rest = rest + apart * apart
    store_sums(sums_ref, square, cross, reduced(mixed), reduced(rest), pivot)


def store_sums(ref, *values):
    sub = lax.broadcasted_iota(jnp.int32, ref.shape, 0)
    out = jnp.zeros(ref.shape, F32)
    for index, value in enumerate(values):
        out = jnp.where(sub == index, value, out)
    ref[...] = out


def load_sums(ref):
    return [ref[index : index + 1, :] for index in range(5)]


def last_kernel(inverse, beta_ref, sums_ref, cov_a_ref, cov_b_ref, inc_ref, prev_ref, w_ref, out_ref):
    beta = beta_ref[0]
    square0, cross0, mixed0, rest0, pivot0 = [value[:, 0:1] for value in load_sums(sums_ref)]
    zero = jnp.zeros(inc_ref.shape[1:], F32)
    square, cross, mixed, rest = zero, zero, zero, zero
    for q in range(DIFF):
        inc = inc_ref[q]
        scaled = inverse * (cov_a_ref[q] + cov_b_ref[q])
        value = scaled - beta * prev_ref[q]
        w_ref[q] = value
        apart = value - pivot0 * inc
        square = square + inc * inc
        cross = cross + inc * scaled
        mixed = mixed + apart * inc
        rest = rest + apart * apart
    store_sums(
        out_ref,
        square0 + reduced(square), cross0 + reduced(cross), mixed0 + reduced(mixed), rest0 + reduced(rest), pivot0,
    )


def merged(parts):
    square = sum(part[0] for part in parts)
    cross = sum(part[1] for part in parts)
    pivot = ratio(cross, square)
    mixed, rest = F32(0.0), F32(0.0)
    for part in parts:
        shift = part[4] - pivot
        mixed = mixed + part[2] + shift * part[0]
        rest = rest + part[3] + 2.0 * shift * part[2] + shift * shift * part[0]
    return square, cross, mixed, rest, pivot


def merge_kernel(*refs):
    store_sums(refs[-1], *merged([load_sums(ref) for ref in refs[:-1]]))


def final_kernel(rows, levels, cells, count, *refs):
    sums_refs = refs[:count]
    w_far_ref, w_rest_ref, inc_ref, out_ref, coef_ref, flat_ref = refs[count:]
    tile = lax.axis_index("tile")
    _, _, _, rest, pivot = merged([load_sums(ref) for ref in sums_refs])
    scale = jnp.sqrt(rest / cells + 1e-6)
    coef_ref[...] = jnp.concatenate([1.0 + pivot, scale], axis=0)
    over = (1.0 / scale)[:, 0:1]
    pivot = pivot[:, 0:1]
    for row in range(rows):
        w = w_far_ref[row] if row < DIFF else w_rest_ref[row - DIFF]
        value = (w - pivot * inc_ref[row]) * over
        for piece in range(flat_ref.shape[0]):
            part = value[:levels, piece * 128 : (piece + 1) * 128]
            flat_ref[piece, pl.ds(grid_row(tile, row, rows), levels, stride=rows), :] = part
    for piece in range(flat_ref.shape[0]):
        out_ref[:, piece * 128 : (piece + 1) * 128] = flat_ref[piece]


def call(kernel, ins, outs, scratch=(), cost=None):
    specs = [smem() if kind == "s" else vmem() for kind, _ in ins]
    return pl.pallas_call(
        kernel,
        out_shape=tuple(jax.ShapeDtypeStruct(shape, F32) for shape in outs),
        in_specs=specs,
        out_specs=tuple(vmem() for _ in outs),
        scratch_shapes=scratch,
        compiler_params=pltpu.CompilerParams(vmem_limit_bytes=VMEM_LIMIT),
        cost_estimate=None
        if cost is None
        else pl.CostEstimate(flops=cost[0], bytes_accessed=cost[1], transcendentals=0),
    )(*(value for _, value in ins))


def flipped(axis, bit):
    count = lax.axis_size(axis)
    return [(i, i ^ bit) for i in range(count)]


def rotated(axis, digit, radix, by):
    count = lax.axis_size(axis)

    def target(i):
        value = i // digit % radix
        return i + ((value + by) % radix - value) * digit

    return [(i, target(i)) for i in range(count)]


def radices(count):
    out = [] if count % 2 else [2]
    rest = count // 2 if out else count
    factor = 4
    while rest > 1:
        while factor > 1 and rest % factor:
            factor -= 1
        if factor == 1:
            factor = rest
        out.append(factor)
        rest //= factor
        factor = min(factor, 4)
    return out


def per_device(increment, previous, beta_prev, members, band_widths, diffusion_steps):
    levels, rows, width = increment.shape
    tiles, mems = lax.axis_size("tile"), lax.axis_size("mem")
    owned = members.shape[0]
    tall, deep = up_to(levels, 8), up_to(levels, 16)
    inverse = 1.0 / (owned * mems - 1)
    cells = levels * rows * tiles * width
    inc = increment.reshape(levels * rows, width)
    prev = previous.reshape(levels * rows, width)
    mem = members.reshape(owned, levels * rows, width)
    bands = band_widths.reshape(1, levels)
    edge = (owned, DIFF, tall, width)
    part = (rows - 2 * DIFF) // 2
    near_pairs = [(i, i ^ 1) for i in range(tiles) if i ^ 1 < tiles]
    far_pairs = [pair for i in range(1, tiles - 1, 2) for pair in ((i, i + 1), (i + 1, i))]
    pad = pltpu.VMEM((8, 128), F32)

    near_edge, far_edge = call(
        functools.partial(edge_kernel, rows, levels),
        [("v", bands), ("v", mem), ("v", inc)],
        [edge, edge],
        [pltpu.VMEM((owned, width // 128, deep * rows, 128), F32), pad],
    )
    near_halo = lax.ppermute(near_edge, "tile", near_pairs)
    far_halo = lax.ppermute(far_edge, "tile", far_pairs)

    piece, four = (part, tall, width), (DIFF, tall, width)
    mine, theirs, cov_near, cov_far, mem_near, mem_far, inc_t, prev_t = call(
        functools.partial(own_kernel, rows, levels, tiles),
        [("v", bands), ("s", diffusion_steps), ("v", mem), ("v", inc), ("v", prev)],
        [piece, piece, four, four, edge, edge, (rows, tall, width), (rows, tall, width)],
        [pltpu.VMEM((width // 128, deep * rows, 128), F32)] * 2 + [pltpu.VMEM((rows + 6, tall, width), F32)] * 2 + [pad],
        (200_000_000, 10_000_000),
    )
    bits = [1 << k for k in range(1, mems.bit_length() - 1)]
    mine = mine + lax.ppermute(theirs, "mem", flipped("mem", 1))
    for bit in bits:
        mine = mine + lax.ppermute(mine, "mem", flipped("mem", bit))
    other = lax.ppermute(mine, "mem", flipped("mem", 1))

    def edge_sum(near, halo, mem_rows, cov):
        (value,) = call(
            functools.partial(halo_kernel, near, tiles),
            [("s", diffusion_steps), ("v", halo), ("v", mem_rows), ("v", cov)],
            [four],
        )
        for bit in [1] + bits[:-1]:
            value = value + lax.ppermute(value, "mem", flipped("mem", bit))
        return value, lax.ppermute(value, "mem", flipped("mem", bits[-1]))

    near_a, near_b = edge_sum(True, near_halo, mem_near, cov_near)
    w_rest, sums = call(
        functools.partial(bulk_kernel, rows, inverse, None),
        [("s", beta_prev), ("v", mine), ("v", other), ("v", near_a), ("v", near_b), ("v", inc_t), ("v", prev_t)],
        [(rows - DIFF, tall, width), (8, 128)],
    )
    far_a, far_b = edge_sum(False, far_halo, mem_far, cov_far)
    w_far, sums = call(
        functools.partial(last_kernel, inverse),
        [("s", beta_prev), ("v", sums), ("v", far_a), ("v", far_b), ("v", inc_t[:DIFF]), ("v", prev_t[:DIFF])],
        [four, (8, 128)],
    )
    digit = 1
    stages = radices(tiles)
    for index, radix in enumerate(stages):
        parts = [sums] + [lax.ppermute(sums, "tile", rotated("tile", digit, radix, by)) for by in range(1, radix)]
        if index < len(stages) - 1:
            (sums,) = call(merge_kernel, [("v", value) for value in parts], [(8, 128)])
        digit *= radix
    out, coefficients = call(
        functools.partial(final_kernel, rows, levels, cells, len(parts)),
        [("v", value) for value in parts] + [("v", w_far), ("v", w_rest), ("v", inc_t)],
        [(levels * rows, width), (2, 128)],
        [pltpu.VMEM((width // 128, levels * rows, 128), F32)],
    )
    return out.reshape(levels, rows, width), coefficients[:, 0]


def solution(mesh):
    in_specs = (
        P(None, "tile", None),
        P(None, "tile", None),
        P(),
        P("mem", None, "tile", None),
        P(),
        P(),
    )
    out_specs = (P(None, "tile", None), P())
    return jax.shard_map(
        per_device, mesh=mesh, in_specs=in_specs, out_specs=out_specs, check_vma=False
    )
```

```python
import functools

import jax
import jax.numpy as jnp
import ml_dtypes
import numpy as np
from jax import lax
from jax.experimental import pallas as pl
from jax.experimental.pallas import tpu as pltpu
from jax.sharding import PartitionSpec as P

DIFF = 4
RATE = 0.24
F32 = jnp.float32
VMEM_LIMIT = 32 * 1024 * 1024
EDGE_LIMIT = 60 * 1024 * 1024


def up_to(value, unit):
    return -(-value // unit) * unit


def grid_row(tile, row, rows):
    return jnp.where(tile % 2 == 0, row, rows - 1 - row)


def put_flat(ref, value):
    for piece in range(ref.shape[0]):
        ref[piece, : value.shape[0], :] = value[:, piece * 128 : (piece + 1) * 128]


def strided(ref, start, count, stride):
    pieces = [ref[piece, pl.ds(start, count, stride=stride), :] for piece in range(ref.shape[0])]
    return jnp.concatenate(pieces, axis=1)


def sweep_counts(steps_ref, tile, tiles):
    even = tile % 2 == 0
    near = jnp.where(even, tile + 1, tile - 1)
    far = jnp.where(even, tile - 1, tile + 1)

    def count(index):
        inside = (index >= 0) & (index < tiles)
        return jnp.where(inside, steps_ref[jnp.clip(index, 0, tiles - 1)], 0)

    return count(tile), count(near), count(far)


def coefficient(sweep, count):
    return jnp.where(sweep < count, F32(RATE), F32(0.0))


def build_vertical(bands_ref, pad_ref, levels):
    pad_ref[...] = jnp.ones(pad_ref.shape, F32)
    pad_ref[0:1, 0:levels] = bands_ref[...].astype(F32)
    across = jnp.broadcast_to(pad_ref[0:1, :], (128, 128))
    down = across.T
    i = lax.broadcasted_iota(jnp.int32, (128, 128), 0)
    j = lax.broadcasted_iota(jnp.int32, (128, 128), 1)
    apart = (i - j).astype(F32)
    weight = jnp.exp(-(apart * apart) / (down * across))
    keep = (jnp.abs(apart) <= jnp.minimum(down, across)) & (i < levels) & (j < levels)
    full = jnp.where(keep, weight, F32(0.0))[: up_to(levels, 8), : up_to(levels, 16)]
    high = full.astype(jnp.bfloat16)
    return high, (full - high.astype(F32)).astype(jnp.bfloat16)


def apply_vertical(vertical, field):
    v_high, v_low = vertical
    high = field.astype(jnp.bfloat16)
    low = (field - high.astype(F32)).astype(jnp.bfloat16)
    dot = functools.partial(jnp.dot, preferred_element_type=F32)
    return dot(v_high, high) + dot(v_high, low) + dot(v_low, high)


def sine_matrix(width):
    mode = np.arange(1, width + 1)
    full = np.sqrt(2.0 / (width + 1)) * np.sin(np.pi * np.outer(mode, mode) / (width + 1))
    high = full.astype(ml_dtypes.bfloat16)
    low = (full - high.astype(np.float64)).astype(ml_dtypes.bfloat16)
    waves = np.broadcast_to(2.0 * np.cos(np.pi * mode / (width + 1)), (8, width)).astype(np.float32)
    return jnp.asarray(high), jnp.asarray(low), jnp.asarray(waves)


def transform(field, s_high, s_low):
    high = field.astype(jnp.bfloat16)
    low = (field - high.astype(F32)).astype(jnp.bfloat16)
    dot = functools.partial(jnp.dot, preferred_element_type=F32)
    return dot(high, s_high) + dot(low, s_high) + dot(high, s_low)


def advance(field, rates, bases):
    new = {}
    for p, rate in rates.items():
        near = [field[p + d] for d in (-1, 1) if p + d in field]
        value = None
        if near:
            value = rate * (near[0] + near[1] if len(near) == 2 else near[0])
        if p in field:
            here = bases[p] * field[p]
            value = here if value is None else here + value
        if value is not None:
            new[p] = value
    return new


def base_of(rate, waves):
    return (1.0 - 4.0 * rate) + rate * waves


def edge_kernel(
    near, rows, levels, cuts,
    bands_hbm, members_hbm, inc_hbm, s_high_hbm, s_low_hbm, *refs,
):
    out_refs = refs[: len(cuts)]
    bands_ref, mem_ref, inc_ref, s_high_ref, s_low_ref, prod_ref, pad_ref, sems = refs[len(cuts) :]
    tile = lax.axis_index("tile")
    high_end = (tile % 2 == 0) == near
    start = pl.multiple_of(jnp.where(high_end, rows - 8, 0), 8)
    owned = members_hbm.shape[0]
    pairs = [(bands_hbm, bands_ref), (inc_hbm.at[:, pl.ds(start, 8), :], inc_ref)]
    pairs += [(members_hbm.at[m, :, pl.ds(start, 8), :], mem_ref.at[m]) for m in range(owned)]
    pairs += [(s_high_hbm, s_high_ref), (s_low_hbm, s_low_ref)]
    copies = [pltpu.make_async_copy(source, target, sems.at[k]) for k, (source, target) in enumerate(pairs)]
    for copy in copies:
        copy.start()
    width = inc_ref.shape[-1]
    deep, tall = up_to(levels, 16), up_to(levels, 8)
    for piece in range(width // 128):
        prod_ref[piece, levels * 8 :, :] = jnp.zeros((prod_ref.shape[1] - levels * 8, 128), F32)
    copies[0].wait()
    vertical = build_vertical(bands_ref, pad_ref, levels)
    copies[1].wait()
    for m in range(owned):
        copies[2 + m].wait()
        product = mem_ref[m].astype(F32) * inc_ref[...]
        put_flat(prod_ref, product.reshape(levels * 8, width))
        local = []
        for q in range(DIFF):
            row = jnp.where(high_end, 7 - q, q)
            local.append(apply_vertical(vertical, strided(prod_ref, row, deep, 8)))
        if m == 0:
            copies[2 + owned].wait()
            copies[3 + owned].wait()
        waves = transform(jnp.concatenate(local, axis=0), s_high_ref[...], s_low_ref[...])
        for q in range(DIFF):
            for (low, high), out_ref in zip(cuts, out_refs):
                for piece in range(width // 128):
                    part = waves[q * tall + low : q * tall + high, piece * 128 : (piece + 1) * 128]
                    out_ref[m, piece, pl.ds(q, high - low, stride=DIFF), :] = part


def own_kernel(
    rows, levels, tiles,
    bands_ref, steps_ref, members_ref, inc_ref, prev_ref, s_high_ref, s_low_ref, waves_ref,
    mine_ref, theirs_ref, cov_near_ref, cov_far_ref, mem_near_ref, mem_far_ref, inc_t_ref, prev_t_ref,
    prod_ref, memf_ref, spec_ref, acc_ref, base_ref, pad_ref,
):
    tile = lax.axis_index("tile")
    half = lax.axis_index("mem") % 2
    counts = sweep_counts(steps_ref, tile, tiles)
    vertical = build_vertical(bands_ref, pad_ref, levels)
    deep, tall = up_to(levels, 16), up_to(levels, 8)
    total = rows * levels
    width = inc_ref.shape[-1]
    for ref in (prod_ref, memf_ref):
        for piece in range(width // 128):
            ref[piece, total:, :] = jnp.zeros((ref.shape[1] - total, 128), F32)

    def row_of(ref, row, count):
        return strided(ref, grid_row(tile, row, rows), count, rows)

    for source, target in ((inc_ref, inc_t_ref), (prev_ref, prev_t_ref)):
        put_flat(prod_ref, source[...])
        for row in range(rows):
            target[row] = row_of(prod_ref, row, tall)
    rate = [[coefficient(k, count) for count in counts] for k in range(DIFF)]
    for k in range(DIFF):
        for side in range(3):
            base_ref[k, side] = base_of(rate[k][side], waves_ref[...])

    def side_of(p):
        return 2 if p < 0 else 1 if p >= rows else 0

    for m in range(members_ref.shape[0]):
        as_float = members_ref[m].astype(F32)
        put_flat(memf_ref, as_float)
        put_flat(prod_ref, transform(as_float * inc_ref[...], s_high_ref[...], s_low_ref[...]))
        for row in range(rows):
            spec_ref[row] = apply_vertical(vertical, row_of(prod_ref, row, deep))

        def chunk(index, _):
            at = pl.ds(pl.multiple_of(index * 8, 8), 8)
            field = {p: spec_ref[p, at, :] for p in range(rows)}
            for k in range(DIFF):
                out = min(k + 1, DIFF - 1 - k)
                kept = range(-out, rows + out)
                bases = {p: base_ref[k, side_of(p)] for p in kept}
                field = advance(field, {p: rate[k][side_of(p)] for p in kept}, bases)
            for p in range(rows):
                spec_ref[p, at, :] = field[p]
            return 0

        lax.fori_loop(0, tall // 8, chunk, 0)
        group = 4
        for first in range(0, rows, group):
            block = spec_ref[first : first + group].reshape(group * tall, width)
            block = transform(block, s_high_ref[...], s_low_ref[...])
            for k in range(group):
                row = first + k
                member = row_of(memf_ref, row, tall)
                if row < DIFF:
                    mem_far_ref[m, row] = member
                if row >= rows - DIFF:
                    mem_near_ref[m, rows - 1 - row] = member
                value = member * block[k * tall : (k + 1) * tall]
                acc_ref[row] = value if m == 0 else acc_ref[row] + value
    part = (rows - 2 * DIFF) // 2
    for q in range(DIFF):
        cov_far_ref[q] = acc_ref[q]
        cov_near_ref[q] = acc_ref[rows - 1 - q]
    for q in range(part):
        mine_ref[q] = acc_ref[DIFF + half * part + q]
        theirs_ref[q] = acc_ref[DIFF + (1 - half) * part + q]


def halo_kernel(
    near, tiles, cut,
    steps_ref, halo_ref, mem_ref, cov_ref, s_high_ref, s_low_ref, waves_ref, out_ref, spec_ref, base_ref,
):
    counts = sweep_counts(steps_ref, lax.axis_index("tile"), tiles)
    owned, width = halo_ref.shape[0], cov_ref.shape[-1]
    low, high = cut
    count, tall = high - low, up_to(high - low, 8)
    rate = [[coefficient(k, counts[0]), coefficient(k, counts[1 if near else 2])] for k in range(DIFF)]
    for k in range(DIFF):
        for side in range(2):
            base_ref[k, side] = base_of(rate[k][side], waves_ref[...])
    for m in range(owned):
        for at in range(0, count, 8):
            size = min(8, count - at)
            field = {q: strided(halo_ref.at[m], q + DIFF * at, size, DIFF) for q in range(DIFF)}
            for k in range(DIFF):
                kept = range(-1 - k, DIFF - 1 - k)
                bases = {p: base_ref[k, 0 if p < 0 else 1][:size] for p in kept}
                field = advance(field, {p: rate[k][0 if p < 0 else 1] for p in kept}, bases)
            for q in range(DIFF):
                spec_ref[q, at : at + size, :] = field[-1 - q]
        if count < tall:
            for q in range(DIFF):
                spec_ref[q, count:, :] = jnp.zeros((tall - count, width), F32)
        block = spec_ref[...].reshape(DIFF * tall, width)
        block = transform(block, s_high_ref[...], s_low_ref[...])
        for q in range(DIFF):
            value = mem_ref[m, q, low : low + tall, :] * block[q * tall : (q + 1) * tall]
            out_ref[q] = value + (cov_ref[q, low : low + tall, :] if m == 0 else out_ref[q])


def reduced(value):
    return jnp.sum(value, axis=(0, 1), keepdims=True)


def folded(value):
    return jnp.sum(value.reshape(value.shape[0] // 8, 8, value.shape[1]), axis=0)


def ratio(top, bottom):
    some = bottom != 0.0
    return jnp.where(some, top / jnp.where(some, bottom, F32(1.0)), F32(0.0))


def put_row(ref, row, rows, low, value):
    for piece in range(ref.shape[0]):
        part = value[:, piece * 128 : (piece + 1) * 128]
        ref[piece, pl.ds(row + low * rows, value.shape[0], stride=rows), :] = part


def bulk_kernel(
    rows, levels, inverse, cut,
    beta_ref, mine_ref, other_ref, near_a_ref, near_b_ref, far_a_ref, far_b_ref, inc_ref, prev_ref,
    w_ref, sums_ref, keep_ref,
):
    beta = beta_ref[0]
    tile = lax.axis_index("tile")
    part = (rows - 2 * DIFF) // 2
    own_half = lax.axis_index("mem") % 2
    zero = jnp.zeros((8, inc_ref.shape[-1]), F32)

    def covariance(row):
        if row < DIFF:
            return far_a_ref[row] + far_b_ref[row]
        if row >= rows - DIFF:
            q = rows - 1 - row
            return near_a_ref[q] + near_b_ref[q]
        which, q = divmod(row - DIFF, part)
        return jnp.where(own_half == which, mine_ref[q], other_ref[q])

    square, cross = zero, zero
    for row in range(rows):
        high = cut if row < DIFF else inc_ref.shape[1]
        inc = inc_ref[row, :high]
        scaled = inverse * covariance(row)
        square = square + folded(inc * inc)
        cross = cross + folded(inc * scaled)
        value = scaled - beta * prev_ref[row, :high]
        keep_ref[row, :high] = value
        put_row(w_ref, grid_row(tile, row, rows), rows, 0, value[: min(high, levels)])
    square, cross = reduced(square), reduced(cross)
    pivot = ratio(cross, square)
    mixed, rest = zero, zero
    for row in range(rows):
        high = cut if row < DIFF else inc_ref.shape[1]
        inc = inc_ref[row, :high]
        apart = keep_ref[row, :high] - pivot * inc
        mixed = mixed + folded(apart * inc)
        rest = rest + folded(apart * apart)
    store_sums(sums_ref, square, cross, reduced(mixed), reduced(rest), pivot)


def store_sums(ref, *values):
    sub = lax.broadcasted_iota(jnp.int32, ref.shape, 0)
    out = jnp.zeros(ref.shape, F32)
    for index, value in enumerate(values):
        out = jnp.where(sub == index, value, out)
    ref[...] = out


def load_sums(ref):
    return [ref[index : index + 1, :] for index in range(5)]


def last_kernel(inverse, cut, beta_ref, sums_ref, cov_a_ref, cov_b_ref, inc_ref, prev_ref, w_ref, out_ref):
    beta = beta_ref[0]
    square0, cross0, mixed0, rest0, pivot0 = [value[:, 0:1] for value in load_sums(sums_ref)]
    zero = jnp.zeros((8, inc_ref.shape[-1]), F32)
    square, cross, mixed, rest = zero, zero, zero, zero
    for q in range(DIFF):
        inc = inc_ref[q, cut:]
        scaled = inverse * (cov_a_ref[q] + cov_b_ref[q])
        value = scaled - beta * prev_ref[q, cut:]
        w_ref[q] = value
        apart = value - pivot0 * inc
        square = square + folded(inc * inc)
        cross = cross + folded(inc * scaled)
        mixed = mixed + folded(apart * inc)
        rest = rest + folded(apart * apart)
    store_sums(
        out_ref,
        square0 + reduced(square), cross0 + reduced(cross), mixed0 + reduced(mixed), rest0 + reduced(rest), pivot0,
    )


def merged(parts):
    square = sum(part[0] for part in parts)
    cross = sum(part[1] for part in parts)
    pivot = ratio(cross, square)
    mixed, rest = F32(0.0), F32(0.0)
    for part in parts:
        shift = part[4] - pivot
        mixed = mixed + part[2] + shift * part[0]
        rest = rest + part[3] + 2.0 * shift * part[2] + shift * shift * part[0]
    return square, cross, mixed, rest, pivot


def merge_kernel(*refs):
    store_sums(refs[-1], *merged([load_sums(ref) for ref in refs[:-1]]))


def final_kernel(rows, levels, cells, cut, count, *refs):
    sums_refs = refs[:count]
    w_far_ref, w_ref, inc_ref, out_hbm, coef_ref, out_ref, end_ref, sems = refs[count:]
    tile = lax.axis_index("tile")
    _, _, _, rest, pivot = merged([load_sums(ref) for ref in sums_refs])
    scale = jnp.sqrt(rest / cells + 1e-6)
    lane = lax.broadcasted_iota(jnp.int32, scale.shape, 1)
    coef_ref[...] = jnp.where(lane == 0, 1.0 + pivot, scale)[:, :2]
    over = 1.0 / scale
    total, edge = rows * levels, rows * cut
    end_ref[...] = w_ref[:, edge:, :]
    for q in range(DIFF):
        put_row(end_ref, grid_row(tile, q, rows), rows, 0, w_far_ref[q, : levels - cut])
    bounds = [0, edge // 16 * 8, edge, total]
    copies = []
    for k in range(3):
        low, high = bounds[k], bounds[k + 1]
        for piece in range(w_ref.shape[0]):
            lanes = slice(piece * 128, (piece + 1) * 128)
            w = end_ref[piece] if k == 2 else w_ref[piece, low:high, :]
            out_ref[low:high, lanes] = (w - pivot * inc_ref[low:high, lanes]) * over
        copies.append(pltpu.make_async_copy(out_ref.at[low:high], out_hbm.at[low:high], sems.at[k]))
        copies[-1].start()
    for copy in copies:
        copy.wait()


def call(kernel, ins, outs, scratch=(), cost=None, limit=VMEM_LIMIT):
    spaces = {"s": pltpu.SMEM, "v": pltpu.VMEM, "h": pl.ANY}
    outs = [out if isinstance(out[0], str) else ("v", out) for out in outs]
    estimate = None
    if cost is not None:
        estimate = pl.CostEstimate(flops=cost[0], bytes_accessed=cost[1], transcendentals=0)
    return pl.pallas_call(
        kernel,
        out_shape=tuple(jax.ShapeDtypeStruct(shape, F32) for _, shape in outs),
        in_specs=[pl.BlockSpec(memory_space=spaces[kind]) for kind, _ in ins],
        out_specs=tuple(pl.BlockSpec(memory_space=spaces[kind]) for kind, _ in outs),
        scratch_shapes=scratch,
        compiler_params=pltpu.CompilerParams(vmem_limit_bytes=limit),
        cost_estimate=estimate,
    )(*(value for _, value in ins))


def flipped(axis, bit):
    count = lax.axis_size(axis)
    return [(i, i ^ bit) for i in range(count)]


def rotated(axis, digit, radix, by):
    count = lax.axis_size(axis)

    def target(i):
        value = i // digit % radix
        return i + ((value + by) % radix - value) * digit

    return [(i, target(i)) for i in range(count)]


def radices(count):
    out = [] if count % 2 else [2]
    rest = count // 2 if out else count
    factor = 4
    while rest > 1:
        while factor > 1 and rest % factor:
            factor -= 1
        if factor == 1:
            factor = rest
        out.append(factor)
        rest //= factor
        factor = min(factor, 4)
    return out


def per_device(increment, previous, beta_prev, members, band_widths, diffusion_steps):
    levels, rows, width = increment.shape
    tiles, mems = lax.axis_size("tile"), lax.axis_size("mem")
    owned = members.shape[0]
    tall, deep = up_to(levels, 8), up_to(levels, 16)
    cut = up_to(2 * levels // 3, 8)
    inverse = 1.0 / (owned * mems - 1)
    cells = levels * rows * tiles * width
    lanes = width // 128
    inc = increment.reshape(levels * rows, width)
    prev = previous.reshape(levels * rows, width)
    mem = members.reshape(owned, levels * rows, width)
    bands = band_widths.reshape(1, levels)
    s_high, s_low, waves = sine_matrix(width)
    edge = (owned, DIFF, tall, width)
    part = (rows - 2 * DIFF) // 2
    near_pairs = [(i, i ^ 1) for i in range(tiles) if i ^ 1 < tiles]
    far_pairs = [pair for i in range(1, tiles - 1, 2) for pair in ((i, i + 1), (i + 1, i))]
    pad = pltpu.VMEM((8, 128), F32)

    def edges(near, cuts):
        return call(
            functools.partial(edge_kernel, near, rows, levels, cuts),
            [("h", bands), ("h", members), ("h", increment), ("h", s_high), ("h", s_low)],
            [(owned, lanes, DIFF * (high - low), 128) for low, high in cuts],
            [
                pltpu.VMEM((1, levels), jnp.int32),
                pltpu.VMEM((owned, levels, 8, width), jnp.bfloat16),
                pltpu.VMEM((levels, 8, width), F32),
                pltpu.VMEM((width, width), jnp.bfloat16),
                pltpu.VMEM((width, width), jnp.bfloat16),
                pltpu.VMEM((lanes, deep * 8, 128), F32),
                pad,
                pltpu.SemaphoreType.DMA((owned + 4,)),
            ],
            limit=EDGE_LIMIT if near else VMEM_LIMIT,
        )

    near_cut, far_cuts = (0, levels), [(0, cut), (cut, levels)]
    (near_edge,) = edges(True, [near_cut])
    near_halo = lax.ppermute(near_edge, "tile", near_pairs)
    far_edges = edges(False, far_cuts)
    far_halos = [lax.ppermute(value, "tile", far_pairs) for value in far_edges]

    piece, four = (part, tall, width), (DIFF, tall, width)
    mine, theirs, cov_near, cov_far, mem_near, mem_far, inc_t, prev_t = call(
        functools.partial(own_kernel, rows, levels, tiles),
        [("v", bands), ("s", diffusion_steps), ("v", mem), ("v", inc), ("v", prev)]
        + [("v", s_high), ("v", s_low), ("v", waves)],
        [piece, piece, four, four, edge, edge, (rows, tall, width), (rows, tall, width)],
        [pltpu.VMEM((lanes, deep * rows, 128), F32)] * 2
        + [pltpu.VMEM((rows, tall, width), F32)] * 2
        + [pltpu.VMEM((DIFF, 3, 8, width), F32), pad],
        (200_000_000, 10_000_000),
    )
    bits = [1 << k for k in range(1, mems.bit_length() - 1)]
    mine = mine + lax.ppermute(theirs, "mem", flipped("mem", 1))
    for bit in bits:
        mine = mine + lax.ppermute(mine, "mem", flipped("mem", bit))
    other = lax.ppermute(mine, "mem", flipped("mem", 1))

    def edge_sum(near, span, halo, mem_rows, cov):
        size = up_to(span[1] - span[0], 8)
        (value,) = call(
            functools.partial(halo_kernel, near, tiles, span),
            [("s", diffusion_steps), ("v", halo), ("v", mem_rows), ("v", cov)]
            + [("v", s_high), ("v", s_low), ("v", waves)],
            [(DIFF, size, width)],
            [pltpu.VMEM((DIFF, size, width), F32), pltpu.VMEM((DIFF, 2, 8, width), F32)],
        )
        for bit in [1] + bits[:-1]:
            value = value + lax.ppermute(value, "mem", flipped("mem", bit))
        return value, lax.ppermute(value, "mem", flipped("mem", bits[-1]))

    near_sums = edge_sum(True, near_cut, near_halo, mem_near, cov_near)
    far_sums = edge_sum(False, far_cuts[0], far_halos[0], mem_far, cov_far)
    w_rest, sums = call(
        functools.partial(bulk_kernel, rows, levels, inverse, cut),
        [("s", beta_prev), ("v", mine), ("v", other)]
        + [("v", value) for value in near_sums + far_sums]
        + [("v", inc_t), ("v", prev_t)],
        [(lanes, levels * rows, 128), (8, 128)],
        [pltpu.VMEM((rows, tall, width), F32)],
    )
    last_sums = edge_sum(False, far_cuts[1], far_halos[1], mem_far, cov_far)
    w_far, sums = call(
        functools.partial(last_kernel, inverse, cut),
        [("s", beta_prev), ("v", sums)] + [("v", value) for value in last_sums] + [("v", inc_t), ("v", prev_t)],
        [(DIFF, tall - cut, width), (8, 128)],
    )
    digit = 1
    stages = radices(tiles)
    for index, radix in enumerate(stages):
        parts = [sums] + [lax.ppermute(sums, "tile", rotated("tile", digit, radix, by)) for by in range(1, radix)]
        if index < len(stages) - 1:
            (sums,) = call(merge_kernel, [("v", value) for value in parts], [(8, 128)])
        digit *= radix
    out, coefficients = call(
        functools.partial(final_kernel, rows, levels, cells, cut, len(parts)),
        [("v", value) for value in parts] + [("v", w_far), ("v", w_rest), ("v", inc)],
        [("h", (levels * rows, width)), (1, 2)],
        [
            pltpu.VMEM((levels * rows, width), F32),
            pltpu.VMEM((lanes, (levels - cut) * rows, 128), F32),
            pltpu.SemaphoreType.DMA((3,)),
        ],
    )
    return out.reshape(levels, rows, width), coefficients.reshape(2)


def solution(mesh):
    in_specs = (
        P(None, "tile", None),
        P(None, "tile", None),
        P(),
        P("mem", None, "tile", None),
        P(),
        P(),
    )
    out_specs = (P(None, "tile", None), P())
    return jax.shard_map(
        per_device, mesh=mesh, in_specs=in_specs, out_specs=out_specs, check_vma=False
    )
```

```python
import functools

import jax
import jax.numpy as jnp
import ml_dtypes
import numpy as np
from jax import lax
from jax.experimental import pallas as pl
from jax.experimental.pallas import tpu as pltpu
from jax.sharding import PartitionSpec as P

DIFF = 4
RATE = 0.24
F32 = jnp.float32
VMEM_LIMIT = 32 * 1024 * 1024
EDGE_LIMIT = 60 * 1024 * 1024


def up_to(value, unit):
    return -(-value // unit) * unit


def grid_row(tile, row, rows):
    return jnp.where(tile % 2 == 0, row, rows - 1 - row)


def put_flat(ref, value):
    for piece in range(ref.shape[0]):
        ref[piece, : value.shape[0], :] = value[:, piece * 128 : (piece + 1) * 128]


def strided(ref, start, count, stride):
    pieces = [ref[piece, pl.ds(start, count, stride=stride), :] for piece in range(ref.shape[0])]
    return jnp.concatenate(pieces, axis=1)


def sweep_counts(steps_ref, tile, tiles):
    even = tile % 2 == 0
    near = jnp.where(even, tile + 1, tile - 1)
    far = jnp.where(even, tile - 1, tile + 1)

    def count(index):
        inside = (index >= 0) & (index < tiles)
        return jnp.where(inside, steps_ref[jnp.clip(index, 0, tiles - 1)], 0)

    return count(tile), count(near), count(far)


def coefficient(sweep, count):
    return jnp.where(sweep < count, F32(RATE), F32(0.0))


def build_vertical(bands_ref, pad_ref, levels):
    pad_ref[...] = jnp.ones(pad_ref.shape, F32)
    pad_ref[0:1, 0:levels] = bands_ref[...].astype(F32)
    across = jnp.broadcast_to(pad_ref[0:1, :], (128, 128))
    down = across.T
    i = lax.broadcasted_iota(jnp.int32, (128, 128), 0)
    j = lax.broadcasted_iota(jnp.int32, (128, 128), 1)
    apart = (i - j).astype(F32)
    weight = jnp.exp(-(apart * apart) / (down * across))
    keep = (jnp.abs(apart) <= jnp.minimum(down, across)) & (i < levels) & (j < levels)
    full = jnp.where(keep, weight, F32(0.0))[: up_to(levels, 8), : up_to(levels, 16)]
    high = full.astype(jnp.bfloat16)
    return high, (full - high.astype(F32)).astype(jnp.bfloat16)


def apply_vertical(vertical, field):
    v_high, v_low = vertical
    high = field.astype(jnp.bfloat16)
    low = (field - high.astype(F32)).astype(jnp.bfloat16)
    dot = functools.partial(jnp.dot, preferred_element_type=F32)
    return dot(v_high, high) + dot(v_high, low) + dot(v_low, high)


def sine_matrix(width):
    mode = np.arange(1, width + 1)
    full = np.sqrt(2.0 / (width + 1)) * np.sin(np.pi * np.outer(mode, mode) / (width + 1))
    high = full.astype(ml_dtypes.bfloat16)
    low = (full - high.astype(np.float64)).astype(ml_dtypes.bfloat16)
    waves = np.broadcast_to(2.0 * np.cos(np.pi * mode / (width + 1)), (8, width)).astype(np.float32)
    return jnp.asarray(high), jnp.asarray(low), jnp.asarray(waves)


def transform(field, s_high, s_low):
    high = field.astype(jnp.bfloat16)
    low = (field - high.astype(F32)).astype(jnp.bfloat16)
    dot = functools.partial(jnp.dot, preferred_element_type=F32)
    return dot(high, s_high) + dot(low, s_high) + dot(high, s_low)


def advance(field, rates, bases):
    new = {}
    for p, rate in rates.items():
        near = [field[p + d] for d in (-1, 1) if p + d in field]
        value = None
        if near:
            value = rate * (near[0] + near[1] if len(near) == 2 else near[0])
        if p in field:
            here = bases[p] * field[p]
            value = here if value is None else here + value
        if value is not None:
            new[p] = value
    return new


def base_of(rate, waves):
    return (1.0 - 4.0 * rate) + rate * waves


def edge_kernel(
    near, rows, levels,
    bands_hbm, members_hbm, inc_hbm, s_high_hbm, s_low_hbm, out_ref,
    bands_ref, mem_ref, inc_ref, s_high_ref, s_low_ref, prod_ref, pad_ref, sems,
):
    tile = lax.axis_index("tile")
    high_end = (tile % 2 == 0) == near
    start = pl.multiple_of(jnp.where(high_end, rows - 8, 0), 8)
    owned = members_hbm.shape[0]
    pairs = [(bands_hbm, bands_ref), (inc_hbm.at[:, pl.ds(start, 8), :], inc_ref)]
    pairs += [(members_hbm.at[m, :, pl.ds(start, 8), :], mem_ref.at[m]) for m in range(owned)]
    pairs += [(s_high_hbm, s_high_ref), (s_low_hbm, s_low_ref)]
    copies = [pltpu.make_async_copy(source, target, sems.at[k]) for k, (source, target) in enumerate(pairs)]
    for copy in copies:
        copy.start()
    width = inc_ref.shape[-1]
    deep, tall = up_to(levels, 16), up_to(levels, 8)
    for piece in range(width // 128):
        prod_ref[piece, levels * 8 :, :] = jnp.zeros((prod_ref.shape[1] - levels * 8, 128), F32)
    copies[0].wait()
    vertical = build_vertical(bands_ref, pad_ref, levels)
    copies[1].wait()
    for m in range(owned):
        copies[2 + m].wait()
        product = mem_ref[m].astype(F32) * inc_ref[...]
        put_flat(prod_ref, product.reshape(levels * 8, width))
        local = []
        for q in range(DIFF):
            row = jnp.where(high_end, 7 - q, q)
            local.append(apply_vertical(vertical, strided(prod_ref, row, deep, 8)))
        if m == 0:
            copies[2 + owned].wait()
            copies[3 + owned].wait()
        waves = transform(jnp.concatenate(local, axis=0), s_high_ref[...], s_low_ref[...])
        for q in range(DIFF):
            for piece in range(width // 128):
                part = waves[q * tall : q * tall + levels, piece * 128 : (piece + 1) * 128]
                out_ref[m, piece, pl.ds(q, levels, stride=DIFF), :] = part


def own_kernel(
    rows, levels, tiles,
    bands_ref, steps_ref, members_ref, inc_ref, prev_ref, s_high_ref, s_low_ref, waves_ref,
    mine_ref, theirs_ref, cov_near_ref, cov_far_ref, mem_near_ref, mem_far_ref, inc_t_ref, prev_t_ref,
    prod_ref, memf_ref, spec_ref, acc_ref, base_ref, pad_ref,
):
    tile = lax.axis_index("tile")
    half = lax.axis_index("mem") % 2
    counts = sweep_counts(steps_ref, tile, tiles)
    vertical = build_vertical(bands_ref, pad_ref, levels)
    deep, tall = up_to(levels, 16), up_to(levels, 8)
    total = rows * levels
    width = inc_ref.shape[-1]
    for ref in (prod_ref, memf_ref):
        for piece in range(width // 128):
            ref[piece, total:, :] = jnp.zeros((ref.shape[1] - total, 128), F32)

    def row_of(ref, row, count):
        return strided(ref, grid_row(tile, row, rows), count, rows)

    for source, target in ((inc_ref, inc_t_ref), (prev_ref, prev_t_ref)):
        put_flat(prod_ref, source[...])
        for row in range(rows):
            target[row] = row_of(prod_ref, row, tall)
    rate = [[coefficient(k, count) for count in counts] for k in range(DIFF)]
    for k in range(DIFF):
        for side in range(3):
            base_ref[k, side] = base_of(rate[k][side], waves_ref[...])

    def side_of(p):
        return 2 if p < 0 else 1 if p >= rows else 0

    for m in range(members_ref.shape[0]):
        as_float = members_ref[m].astype(F32)
        put_flat(memf_ref, as_float)
        put_flat(prod_ref, transform(as_float * inc_ref[...], s_high_ref[...], s_low_ref[...]))
        for row in range(rows):
            spec_ref[row] = apply_vertical(vertical, row_of(prod_ref, row, deep))

        def chunk(index, _):
            at = pl.ds(pl.multiple_of(index * 8, 8), 8)
            field = {p: spec_ref[p, at, :] for p in range(rows)}
            for k in range(DIFF):
                out = min(k + 1, DIFF - 1 - k)
                kept = range(-out, rows + out)
                bases = {p: base_ref[k, side_of(p)] for p in kept}
                field = advance(field, {p: rate[k][side_of(p)] for p in kept}, bases)
            for p in range(rows):
                spec_ref[p, at, :] = field[p]
            return 0

        lax.fori_loop(0, tall // 8, chunk, 0)
        group = 4
        for first in range(0, rows, group):
            block = spec_ref[first : first + group].reshape(group * tall, width)
            block = transform(block, s_high_ref[...], s_low_ref[...])
            for k in range(group):
                row = first + k
                member = row_of(memf_ref, row, tall)
                if row < DIFF:
                    mem_far_ref[m, row] = member
                if row >= rows - DIFF:
                    mem_near_ref[m, rows - 1 - row] = member
                value = member * block[k * tall : (k + 1) * tall]
                acc_ref[row] = value if m == 0 else acc_ref[row] + value
    part = (rows - 2 * DIFF) // 2
    for q in range(DIFF):
        cov_far_ref[q] = acc_ref[q]
        cov_near_ref[q] = acc_ref[rows - 1 - q]
    for q in range(part):
        mine_ref[q] = acc_ref[DIFF + half * part + q]
        theirs_ref[q] = acc_ref[DIFF + (1 - half) * part + q]


def halo_kernel(
    near, levels, tiles,
    steps_ref, halo_ref, mem_ref, cov_ref, s_high_ref, s_low_ref, waves_ref, *refs,
):
    out_refs, (spec_ref, base_ref) = refs[:-2], refs[-2:]
    counts = sweep_counts(steps_ref, lax.axis_index("tile"), tiles)
    owned, tall, width = halo_ref.shape[0], cov_ref.shape[1], cov_ref.shape[2]
    rate = [[coefficient(k, counts[0]), coefficient(k, counts[1 if near else 2])] for k in range(DIFF)]
    for k in range(DIFF):
        for side in range(2):
            base_ref[k, side] = base_of(rate[k][side], waves_ref[...])
    sums = [cov_ref[q] for q in range(DIFF)]
    for m in range(owned):
        for at in range(0, levels, 8):
            size = min(8, levels - at)
            field = {q: strided(halo_ref.at[m], q + DIFF * at, size, DIFF) for q in range(DIFF)}
            for k in range(DIFF):
                kept = range(-1 - k, DIFF - 1 - k)
                bases = {p: base_ref[k, 0 if p < 0 else 1][:size] for p in kept}
                field = advance(field, {p: rate[k][0 if p < 0 else 1] for p in kept}, bases)
            for q in range(DIFF):
                spec_ref[q, at : at + size, :] = field[-1 - q]
        if levels < tall:
            for q in range(DIFF):
                spec_ref[q, levels:, :] = jnp.zeros((tall - levels, width), F32)
        block = spec_ref[...].reshape(DIFF * tall, width)
        block = transform(block, s_high_ref[...], s_low_ref[...])
        for q in range(DIFF):
            sums[q] = sums[q] + mem_ref[m, q] * block[q * tall : (q + 1) * tall]
    if len(out_refs) == 1:
        for q in range(DIFF):
            out_refs[0][q] = sums[q]
        return
    part = DIFF // 2
    half = lax.axis_index("mem") % 2
    for q in range(DIFF):

        @pl.when(half == q // part)
        def _(q=q):
            out_refs[0][q % part] = sums[q]

        @pl.when(half != q // part)
        def _(q=q):
            out_refs[1][q % part] = sums[q]


def reduced(value):
    return jnp.sum(value, axis=(0, 1), keepdims=True)


def folded(value):
    return jnp.sum(value.reshape(value.shape[0] // 8, 8, value.shape[1]), axis=0)


def ratio(top, bottom):
    some = bottom != 0.0
    return jnp.where(some, top / jnp.where(some, bottom, F32(1.0)), F32(0.0))


def put_row(ref, row, rows, value):
    for piece in range(ref.shape[0]):
        part = value[:, piece * 128 : (piece + 1) * 128]
        ref[piece, pl.ds(row, value.shape[0], stride=rows), :] = part


def bulk_kernel(
    rows, levels, inverse,
    beta_ref, mine_ref, other_ref, near_a_ref, near_b_ref, inc_ref, prev_ref,
    w_ref, sums_ref, keep_ref,
):
    beta = beta_ref[0]
    tile = lax.axis_index("tile")
    part = (rows - 2 * DIFF) // 2
    own_half = lax.axis_index("mem") % 2
    zero = jnp.zeros((8, inc_ref.shape[-1]), F32)

    def covariance(row):
        if row >= rows - DIFF:
            q = rows - 1 - row
            return near_a_ref[q] + near_b_ref[q]
        which, q = divmod(row - DIFF, part)
        return jnp.where(own_half == which, mine_ref[q], other_ref[q])

    square, cross = zero, zero
    for row in range(DIFF, rows):
        inc = inc_ref[row]
        scaled = inverse * covariance(row)
        square = square + folded(inc * inc)
        cross = cross + folded(inc * scaled)
        value = scaled - beta * prev_ref[row]
        keep_ref[row - DIFF] = value
        put_row(w_ref, grid_row(tile, row, rows), rows, value[:levels])
    square, cross = reduced(square), reduced(cross)
    pivot = ratio(cross, square)
    mixed, rest = zero, zero
    for row in range(DIFF, rows):
        inc = inc_ref[row]
        apart = keep_ref[row - DIFF] - pivot * inc
        mixed = mixed + folded(apart * inc)
        rest = rest + folded(apart * apart)
    store_sums(sums_ref, square, cross, reduced(mixed), reduced(rest), pivot)


def store_sums(ref, *values):
    sub = lax.broadcasted_iota(jnp.int32, ref.shape, 0)
    out = jnp.zeros(ref.shape, F32)
    for index, value in enumerate(values):
        out = jnp.where(sub == index, value, out)
    ref[...] = out


def load_sums(ref):
    return [ref[index : index + 1, :] for index in range(5)]


def last_kernel(inverse, beta_ref, sums_ref, mine_ref, other_ref, inc_ref, prev_ref, w_ref, out_ref):
    own_half = lax.axis_index("mem") % 2
    part = DIFF // 2
    beta = beta_ref[0]
    square0, cross0, mixed0, rest0, pivot0 = [value[:, 0:1] for value in load_sums(sums_ref)]
    zero = jnp.zeros((8, inc_ref.shape[-1]), F32)
    square, cross, mixed, rest = zero, zero, zero, zero
    for q in range(DIFF):
        inc = inc_ref[q]
        which, index = divmod(q, part)
        scaled = inverse * jnp.where(own_half == which, mine_ref[index], other_ref[index])
        value = scaled - beta * prev_ref[q]
        w_ref[q] = value
        apart = value - pivot0 * inc
        square = square + folded(inc * inc)
        cross = cross + folded(inc * scaled)
        mixed = mixed + folded(apart * inc)
        rest = rest + folded(apart * apart)
    store_sums(
        out_ref,
        square0 + reduced(square), cross0 + reduced(cross), mixed0 + reduced(mixed), rest0 + reduced(rest), pivot0,
    )


def merged(parts):
    square = sum(part[0] for part in parts)
    cross = sum(part[1] for part in parts)
    pivot = ratio(cross, square)
    mixed, rest = F32(0.0), F32(0.0)
    for part in parts:
        shift = part[4] - pivot
        mixed = mixed + part[2] + shift * part[0]
        rest = rest + part[3] + 2.0 * shift * part[2] + shift * shift * part[0]
    return square, cross, mixed, rest, pivot


def merge_kernel(*refs):
    store_sums(refs[-1], *merged([load_sums(ref) for ref in refs[:-1]]))


def final_kernel(rows, levels, cells, count, *refs):
    sums_refs = refs[:count]
    w_far_ref, w_ref, inc_t_ref, inc_ref, out_hbm, coef_ref, out_ref, sems = refs[count:]
    tile = lax.axis_index("tile")
    _, _, _, rest, pivot = merged([load_sums(ref) for ref in sums_refs])
    scale = jnp.sqrt(rest / cells + 1e-6)
    lane = lax.broadcasted_iota(jnp.int32, scale.shape, 1)
    coef_ref[...] = jnp.where(lane == 0, 1.0 + pivot, scale)[:, :2]
    over = 1.0 / scale
    wide_pivot, wide_over = (jnp.concatenate([value] * w_ref.shape[0], axis=1) for value in (pivot, over))
    step = up_to(up_to(levels, 8) // 4, 8)
    copies = []
    for low in range(0, levels, step):
        high = min(levels, low + step)
        span = slice(low * rows, high * rows)
        for piece in range(w_ref.shape[0]):
            lanes = slice(piece * 128, (piece + 1) * 128)
            out_ref[piece, span, :] = (w_ref[piece, span, :] - pivot * inc_ref[span, lanes]) * over
        for q in range(DIFF):
            value = (w_far_ref[q, low:high] - wide_pivot * inc_t_ref[q, low:high]) * wide_over
            put_row(out_ref, grid_row(tile, q, rows) + low * rows, rows, value)
        for piece in range(w_ref.shape[0]):
            lanes = slice(piece * 128, (piece + 1) * 128)
            source, target = out_ref.at[piece, span, :], out_hbm.at[span, lanes]
            copies.append(pltpu.make_async_copy(source, target, sems.at[len(copies)]))
            copies[-1].start()
    for copy in copies:
        copy.wait()


def call(kernel, ins, outs, scratch=(), cost=None, limit=VMEM_LIMIT):
    spaces = {"s": pltpu.SMEM, "v": pltpu.VMEM, "h": pltpu.HBM}
    outs = [out if isinstance(out[0], str) else ("v", out) for out in outs]
    estimate = None
    if cost is not None:
        estimate = pl.CostEstimate(flops=cost[0], bytes_accessed=cost[1], transcendentals=0)
    return pl.pallas_call(
        kernel,
        out_shape=tuple(jax.ShapeDtypeStruct(shape, F32) for _, shape in outs),
        in_specs=[pl.BlockSpec(memory_space=spaces[kind]) for kind, _ in ins],
        out_specs=tuple(pl.BlockSpec(memory_space=spaces[kind]) for kind, _ in outs),
        scratch_shapes=scratch,
        compiler_params=pltpu.CompilerParams(vmem_limit_bytes=limit),
        cost_estimate=estimate,
    )(*(value for _, value in ins))


def flipped(axis, bit):
    count = lax.axis_size(axis)
    return [(i, i ^ bit) for i in range(count)]


def rotated(axis, digit, radix, by):
    count = lax.axis_size(axis)

    def target(i):
        value = i // digit % radix
        return i + ((value + by) % radix - value) * digit

    return [(i, target(i)) for i in range(count)]


def radices(count):
    out = [] if count % 2 else [2]
    rest = count // 2 if out else count
    factor = 4
    while rest > 1:
        while factor > 1 and rest % factor:
            factor -= 1
        if factor == 1:
            factor = rest
        out.append(factor)
        rest //= factor
        factor = min(factor, 4)
    return out


def per_device(increment, previous, beta_prev, members, band_widths, diffusion_steps):
    levels, rows, width = increment.shape
    tiles, mems = lax.axis_size("tile"), lax.axis_size("mem")
    owned = members.shape[0]
    tall, deep = up_to(levels, 8), up_to(levels, 16)
    inverse = 1.0 / (owned * mems - 1)
    cells = levels * rows * tiles * width
    lanes = width // 128
    inc = increment.reshape(levels * rows, width)
    prev = previous.reshape(levels * rows, width)
    bands = band_widths.reshape(1, levels)
    s_high, s_low, waves = sine_matrix(width)
    edge = (owned, DIFF, tall, width)
    part = (rows - 2 * DIFF) // 2
    near_pairs = [(i, i ^ 1) for i in range(tiles) if i ^ 1 < tiles]
    far_pairs = [pair for i in range(1, tiles - 1, 2) for pair in ((i, i + 1), (i + 1, i))]
    pad = pltpu.VMEM((8, 128), F32)

    def edges(near):
        (value,) = call(
            functools.partial(edge_kernel, near, rows, levels),
            [("h", bands), ("h", members), ("h", increment), ("h", s_high), ("h", s_low)],
            [(owned, lanes, DIFF * levels, 128)],
            [
                pltpu.VMEM((1, levels), jnp.int32),
                pltpu.VMEM((owned, levels, 8, width), jnp.bfloat16),
                pltpu.VMEM((levels, 8, width), F32),
                pltpu.VMEM((width, width), jnp.bfloat16),
                pltpu.VMEM((width, width), jnp.bfloat16),
                pltpu.VMEM((lanes, deep * 8, 128), F32),
                pad,
                pltpu.SemaphoreType.DMA((owned + 4,)),
            ],
            limit=EDGE_LIMIT if near else VMEM_LIMIT,
        )
        return value

    near_edge = edges(True)
    near_halo = lax.ppermute(near_edge, "tile", near_pairs)
    far_edge = edges(False)
    members, far_edge = lax.optimization_barrier((members, far_edge))
    mem = members.reshape(owned, levels * rows, width)
    far_halo = lax.ppermute(far_edge, "tile", far_pairs)

    piece, four = (part, tall, width), (DIFF, tall, width)
    mine, theirs, cov_near, cov_far, mem_near, mem_far, inc_t, prev_t = call(
        functools.partial(own_kernel, rows, levels, tiles),
        [("v", bands), ("s", diffusion_steps), ("v", mem), ("v", inc), ("v", prev)]
        + [("v", s_high), ("v", s_low), ("v", waves)],
        [piece, piece, four, four, edge, edge, (rows, tall, width), (rows, tall, width)],
        [pltpu.VMEM((lanes, deep * rows, 128), F32)] * 2
        + [pltpu.VMEM((rows, tall, width), F32)] * 2
        + [pltpu.VMEM((DIFF, 3, 8, width), F32), pad],
        (200_000_000, 10_000_000),
    )
    bits = [1 << k for k in range(1, mems.bit_length() - 1)]
    mine = mine + lax.ppermute(theirs, "mem", flipped("mem", 1))
    for bit in bits:
        mine = mine + lax.ppermute(mine, "mem", flipped("mem", bit))
    other = lax.ppermute(mine, "mem", flipped("mem", 1))

    def edge_sum(near, halo, mem_rows, cov, outs):
        return call(
            functools.partial(halo_kernel, near, levels, tiles),
            [("s", diffusion_steps), ("v", halo), ("v", mem_rows), ("v", cov)]
            + [("v", s_high), ("v", s_low), ("v", waves)],
            outs,
            [pltpu.VMEM(four, F32), pltpu.VMEM((DIFF, 2, 8, width), F32)],
        )

    (near_sum,) = edge_sum(True, near_halo, mem_near, cov_near, [four])
    for bit in [1] + bits[:-1]:
        near_sum = near_sum + lax.ppermute(near_sum, "mem", flipped("mem", bit))
    near_other = lax.ppermute(near_sum, "mem", flipped("mem", bits[-1]))
    w_rest, sums = call(
        functools.partial(bulk_kernel, rows, levels, inverse),
        [("s", beta_prev), ("v", mine), ("v", other), ("v", near_sum), ("v", near_other)]
        + [("v", inc_t), ("v", prev_t)],
        [(lanes, levels * rows, 128), (8, 128)],
        [pltpu.VMEM((rows - DIFF, tall, width), F32)],
    )
    two = (DIFF // 2, tall, width)
    far_mine, far_theirs = edge_sum(False, far_halo, mem_far, cov_far, [two, two])
    far_mine = far_mine + lax.ppermute(far_theirs, "mem", flipped("mem", 1))
    for bit in bits:
        far_mine = far_mine + lax.ppermute(far_mine, "mem", flipped("mem", bit))
    far_other = lax.ppermute(far_mine, "mem", flipped("mem", 1))
    w_far, sums = call(
        functools.partial(last_kernel, inverse),
        [("s", beta_prev), ("v", sums), ("v", far_mine), ("v", far_other), ("v", inc_t), ("v", prev_t)],
        [four, (8, 128)],
    )
    digit = 1
    stages = radices(tiles)
    for index, radix in enumerate(stages):
        parts = [sums] + [lax.ppermute(sums, "tile", rotated("tile", digit, radix, by)) for by in range(1, radix)]
        if index < len(stages) - 1:
            (sums,) = call(merge_kernel, [("v", value) for value in parts], [(8, 128)])
        digit *= radix
    out, coefficients = call(
        functools.partial(final_kernel, rows, levels, cells, len(parts)),
        [("v", value) for value in parts] + [("v", w_far), ("v", w_rest), ("v", inc_t), ("v", inc)],
        [("h", (levels * rows, width)), (1, 2)],
        [pltpu.VMEM((lanes, levels * rows, 128), F32), pltpu.SemaphoreType.DMA((4 * lanes,))],
    )
    return out.reshape(levels, rows, width), coefficients.reshape(2)


def solution(mesh):
    in_specs = (
        P(None, "tile", None),
        P(None, "tile", None),
        P(),
        P("mem", None, "tile", None),
        P(),
        P(),
    )
    out_specs = (P(None, "tile", None), P())
    return jax.shard_map(
        per_device, mesh=mesh, in_specs=in_specs, out_specs=out_specs, check_vma=False
    )
```

```python
import functools

import jax
import jax.numpy as jnp
import ml_dtypes
import numpy as np
from jax import lax
from jax.experimental import pallas as pl
from jax.experimental.pallas import tpu as pltpu
from jax.sharding import PartitionSpec as P

DIFF = 4
RATE = 0.24
F32 = jnp.float32
VMEM_LIMIT = 32 * 1024 * 1024
EDGE_LIMIT = 60 * 1024 * 1024


def up_to(value, unit):
    return -(-value // unit) * unit


def grid_row(tile, row, rows):
    return jnp.where(tile % 2 == 0, row, rows - 1 - row)


def put_flat(ref, value):
    for piece in range(ref.shape[0]):
        ref[piece, : value.shape[0], :] = value[:, piece * 128 : (piece + 1) * 128]


def strided(ref, start, count, stride):
    pieces = [ref[piece, pl.ds(start, count, stride=stride), :] for piece in range(ref.shape[0])]
    return jnp.concatenate(pieces, axis=1)


def sweep_counts(steps_ref, tile, tiles):
    even = tile % 2 == 0
    near = jnp.where(even, tile + 1, tile - 1)
    far = jnp.where(even, tile - 1, tile + 1)

    def count(index):
        inside = (index >= 0) & (index < tiles)
        return jnp.where(inside, steps_ref[jnp.clip(index, 0, tiles - 1)], 0)

    return count(tile), count(near), count(far)


def coefficient(sweep, count):
    return jnp.where(sweep < count, F32(RATE), F32(0.0))


def build_vertical(bands_ref, pad_ref, levels):
    pad_ref[...] = jnp.ones(pad_ref.shape, F32)
    pad_ref[0:1, 0:levels] = bands_ref[...].astype(F32)
    across = jnp.broadcast_to(pad_ref[0:1, :], (128, 128))
    down = across.T
    i = lax.broadcasted_iota(jnp.int32, (128, 128), 0)
    j = lax.broadcasted_iota(jnp.int32, (128, 128), 1)
    apart = (i - j).astype(F32)
    weight = jnp.exp(-(apart * apart) / (down * across))
    keep = (jnp.abs(apart) <= jnp.minimum(down, across)) & (i < levels) & (j < levels)
    full = jnp.where(keep, weight, F32(0.0))[: up_to(levels, 8), : up_to(levels, 16)]
    high = full.astype(jnp.bfloat16)
    return high, (full - high.astype(F32)).astype(jnp.bfloat16)


def apply_vertical(vertical, field):
    v_high, v_low = vertical
    high = field.astype(jnp.bfloat16)
    low = (field - high.astype(F32)).astype(jnp.bfloat16)
    dot = functools.partial(jnp.dot, preferred_element_type=F32)
    return dot(v_high, high) + dot(v_high, low) + dot(v_low, high)


def sine_matrix(width):
    mode = np.arange(1, width + 1)
    full = np.sqrt(2.0 / (width + 1)) * np.sin(np.pi * np.outer(mode, mode) / (width + 1))
    high = full.astype(ml_dtypes.bfloat16)
    low = (full - high.astype(np.float64)).astype(ml_dtypes.bfloat16)
    waves = np.broadcast_to(2.0 * np.cos(np.pi * mode / (width + 1)), (8, width)).astype(np.float32)
    return jnp.asarray(high), jnp.asarray(low), jnp.asarray(waves)


def transform(field, s_high, s_low):
    high = field.astype(jnp.bfloat16)
    low = (field - high.astype(F32)).astype(jnp.bfloat16)
    dot = functools.partial(jnp.dot, preferred_element_type=F32)
    return dot(high, s_high) + dot(low, s_high) + dot(high, s_low)


def advance(field, rates, bases):
    new = {}
    for p, rate in rates.items():
        near = [field[p + d] for d in (-1, 1) if p + d in field]
        value = None
        if near:
            value = rate * (near[0] + near[1] if len(near) == 2 else near[0])
        if p in field:
            here = bases[p] * field[p]
            value = here if value is None else here + value
        if value is not None:
            new[p] = value
    return new


def base_of(rate, waves):
    return (1.0 - 4.0 * rate) + rate * waves


def edge_kernel(
    near, rows, levels,
    bands_hbm, members_hbm, inc_hbm, s_high_hbm, s_low_hbm, out_ref,
    bands_ref, mem_ref, inc_ref, s_high_ref, s_low_ref, prod_ref, pad_ref, sems,
):
    tile = lax.axis_index("tile")
    high_end = (tile % 2 == 0) == near
    start = pl.multiple_of(jnp.where(high_end, rows - 8, 0), 8)
    owned = members_hbm.shape[0]
    pairs = [(bands_hbm, bands_ref), (inc_hbm.at[:, pl.ds(start, 8), :], inc_ref)]
    pairs += [(members_hbm.at[m, :, pl.ds(start, 8), :], mem_ref.at[m]) for m in range(owned)]
    pairs += [(s_high_hbm, s_high_ref), (s_low_hbm, s_low_ref)]
    copies = [pltpu.make_async_copy(source, target, sems.at[k]) for k, (source, target) in enumerate(pairs)]
    for copy in copies:
        copy.start()
    width = inc_ref.shape[-1]
    deep, tall = up_to(levels, 16), up_to(levels, 8)
    for piece in range(width // 128):
        prod_ref[piece, levels * 8 :, :] = jnp.zeros((prod_ref.shape[1] - levels * 8, 128), F32)
    copies[0].wait()
    vertical = build_vertical(bands_ref, pad_ref, levels)
    copies[1].wait()
    for m in range(owned):
        copies[2 + m].wait()
        product = mem_ref[m].astype(F32) * inc_ref[...]
        put_flat(prod_ref, product.reshape(levels * 8, width))
        local = []
        for q in range(DIFF):
            row = jnp.where(high_end, 7 - q, q)
            local.append(apply_vertical(vertical, strided(prod_ref, row, deep, 8)))
        if m == 0:
            copies[2 + owned].wait()
            copies[3 + owned].wait()
        waves = transform(jnp.concatenate(local, axis=0), s_high_ref[...], s_low_ref[...])
        for q in range(DIFF):
            for piece in range(width // 128):
                part = waves[q * tall : q * tall + levels, piece * 128 : (piece + 1) * 128]
                out_ref[m, piece, pl.ds(q, levels, stride=DIFF), :] = part


def turn_kernel(rows, levels, inc_ref, prev_ref, inc_t_ref, prev_t_ref, flat_ref):
    tile = lax.axis_index("tile")
    for piece in range(flat_ref.shape[0]):
        flat_ref[piece, rows * levels :, :] = jnp.zeros((flat_ref.shape[1] - rows * levels, 128), F32)
    for source, target in ((inc_ref, inc_t_ref), (prev_ref, prev_t_ref)):
        put_flat(flat_ref, source[...])
        for row in range(rows):
            target[row] = strided(flat_ref, grid_row(tile, row, rows), target.shape[1], rows)


def own_kernel(
    rows, levels, tiles,
    bands_ref, steps_ref, members_ref, inc_ref, s_high_ref, s_low_ref, waves_ref,
    mine_ref, theirs_ref, cov_near_ref, cov_far_ref, mem_near_ref, mem_far_ref,
    prod_ref, memf_ref, spec_ref, acc_ref, base_ref, pad_ref,
):
    tile = lax.axis_index("tile")
    half = lax.axis_index("mem") % 2
    counts = sweep_counts(steps_ref, tile, tiles)
    vertical = build_vertical(bands_ref, pad_ref, levels)
    deep, tall = up_to(levels, 16), up_to(levels, 8)
    total = rows * levels
    width = inc_ref.shape[-1]
    for ref in (prod_ref, memf_ref):
        for piece in range(width // 128):
            ref[piece, total:, :] = jnp.zeros((ref.shape[1] - total, 128), F32)

    def row_of(ref, row, count):
        return strided(ref, grid_row(tile, row, rows), count, rows)

    rate = [[coefficient(k, count) for count in counts] for k in range(DIFF)]
    for k in range(DIFF):
        for side in range(3):
            base_ref[k, side] = base_of(rate[k][side], waves_ref[...])

    def side_of(p):
        return 2 if p < 0 else 1 if p >= rows else 0

    for m in range(members_ref.shape[0]):
        as_float = members_ref[m].astype(F32)
        put_flat(memf_ref, as_float)
        put_flat(prod_ref, transform(as_float * inc_ref[...], s_high_ref[...], s_low_ref[...]))
        for row in range(rows):
            spec_ref[row] = apply_vertical(vertical, row_of(prod_ref, row, deep))

        def chunk(index, _):
            at = pl.ds(pl.multiple_of(index * 8, 8), 8)
            field = {p: spec_ref[p, at, :] for p in range(rows)}
            for k in range(DIFF):
                out = min(k + 1, DIFF - 1 - k)
                kept = range(-out, rows + out)
                bases = {p: base_ref[k, side_of(p)] for p in kept}
                field = advance(field, {p: rate[k][side_of(p)] for p in kept}, bases)
            for p in range(rows):
                spec_ref[p, at, :] = field[p]
            return 0

        lax.fori_loop(0, tall // 8, chunk, 0)
        group = 4
        for first in range(0, rows, group):
            block = spec_ref[first : first + group].reshape(group * tall, width)
            block = transform(block, s_high_ref[...], s_low_ref[...])
            for k in range(group):
                row = first + k
                member = row_of(memf_ref, row, tall)
                if row < DIFF:
                    mem_far_ref[m, row] = member
                if row >= rows - DIFF:
                    mem_near_ref[m, rows - 1 - row] = member
                value = member * block[k * tall : (k + 1) * tall]
                acc_ref[row] = value if m == 0 else acc_ref[row] + value
    part = (rows - 2 * DIFF) // 2
    for q in range(DIFF):
        cov_far_ref[q] = acc_ref[q]
        cov_near_ref[q] = acc_ref[rows - 1 - q]
    for q in range(part):
        mine_ref[q] = acc_ref[DIFF + half * part + q]
        theirs_ref[q] = acc_ref[DIFF + (1 - half) * part + q]


def halo_kernel(
    near, levels, tiles,
    steps_ref, halo_ref, mem_ref, cov_ref, s_high_ref, s_low_ref, waves_ref, *refs,
):
    out_refs, (spec_ref, base_ref) = refs[:-2], refs[-2:]
    counts = sweep_counts(steps_ref, lax.axis_index("tile"), tiles)
    owned, tall, width = halo_ref.shape[0], cov_ref.shape[1], cov_ref.shape[2]
    rate = [[coefficient(k, counts[0]), coefficient(k, counts[1 if near else 2])] for k in range(DIFF)]
    for k in range(DIFF):
        for side in range(2):
            base_ref[k, side] = base_of(rate[k][side], waves_ref[...])
    sums = [cov_ref[q] for q in range(DIFF)]
    for m in range(owned):
        for at in range(0, levels, 8):
            size = min(8, levels - at)
            field = {q: strided(halo_ref.at[m], q + DIFF * at, size, DIFF) for q in range(DIFF)}
            for k in range(DIFF):
                kept = range(-1 - k, DIFF - 1 - k)
                bases = {p: base_ref[k, 0 if p < 0 else 1][:size] for p in kept}
                field = advance(field, {p: rate[k][0 if p < 0 else 1] for p in kept}, bases)
            for q in range(DIFF):
                spec_ref[q, at : at + size, :] = field[-1 - q]
        if levels < tall:
            for q in range(DIFF):
                spec_ref[q, levels:, :] = jnp.zeros((tall - levels, width), F32)
        block = spec_ref[...].reshape(DIFF * tall, width)
        block = transform(block, s_high_ref[...], s_low_ref[...])
        for q in range(DIFF):
            sums[q] = sums[q] + mem_ref[m, q] * block[q * tall : (q + 1) * tall]
    part = DIFF // 2
    half = lax.axis_index("mem") % 2
    for q in range(DIFF):

        @pl.when(half == q // part)
        def _(q=q):
            out_refs[0][q % part] = sums[q]

        @pl.when(half != q // part)
        def _(q=q):
            out_refs[1][q % part] = sums[q]


def reduced(value):
    return jnp.sum(value, axis=(0, 1), keepdims=True)


def folded(value):
    return jnp.sum(value.reshape(value.shape[0] // 8, 8, value.shape[1]), axis=0)


def ratio(top, bottom):
    some = bottom != 0.0
    return jnp.where(some, top / jnp.where(some, bottom, F32(1.0)), F32(0.0))


def put_row(ref, row, rows, value):
    for piece in range(ref.shape[0]):
        part = value[:, piece * 128 : (piece + 1) * 128]
        ref[piece, pl.ds(row, value.shape[0], stride=rows), :] = part


def bulk_kernel(
    rows, levels, inverse,
    beta_ref, mine_ref, other_ref, near_mine_ref, near_other_ref, inc_ref, prev_ref,
    w_ref, sums_ref, keep_ref,
):
    beta = beta_ref[0]
    tile = lax.axis_index("tile")
    part = (rows - 2 * DIFF) // 2
    own_half = lax.axis_index("mem") % 2
    zero = jnp.zeros((8, inc_ref.shape[-1]), F32)

    def covariance(row):
        if row >= rows - DIFF:
            which, q = divmod(rows - 1 - row, DIFF // 2)
            return jnp.where(own_half == which, near_mine_ref[q], near_other_ref[q])
        which, q = divmod(row - DIFF, part)
        return jnp.where(own_half == which, mine_ref[q], other_ref[q])

    square, cross = zero, zero
    for row in range(DIFF, rows):
        inc = inc_ref[row]
        scaled = inverse * covariance(row)
        square = square + folded(inc * inc)
        cross = cross + folded(inc * scaled)
        value = scaled - beta * prev_ref[row]
        keep_ref[row - DIFF] = value
        put_row(w_ref, grid_row(tile, row, rows), rows, value[:levels])
    square, cross = reduced(square), reduced(cross)
    pivot = ratio(cross, square)
    mixed, rest = zero, zero
    for row in range(DIFF, rows):
        inc = inc_ref[row]
        apart = keep_ref[row - DIFF] - pivot * inc
        mixed = mixed + folded(apart * inc)
        rest = rest + folded(apart * apart)
    store_sums(sums_ref, square, cross, reduced(mixed), reduced(rest), pivot)


def store_sums(ref, *values):
    sub = lax.broadcasted_iota(jnp.int32, ref.shape, 0)
    out = jnp.zeros(ref.shape, F32)
    for index, value in enumerate(values):
        out = jnp.where(sub == index, value, out)
    ref[...] = out


def load_sums(ref):
    return [ref[index : index + 1, :] for index in range(5)]


def last_kernel(inverse, beta_ref, sums_ref, mine_ref, other_ref, inc_ref, prev_ref, w_ref, out_ref):
    own_half = lax.axis_index("mem") % 2
    part = DIFF // 2
    beta = beta_ref[0]
    square0, cross0, mixed0, rest0, pivot0 = [value[:, 0:1] for value in load_sums(sums_ref)]
    zero = jnp.zeros((8, inc_ref.shape[-1]), F32)
    square, cross, mixed, rest = zero, zero, zero, zero
    for q in range(DIFF):
        inc = inc_ref[q]
        which, index = divmod(q, part)
        scaled = inverse * jnp.where(own_half == which, mine_ref[index], other_ref[index])
        value = scaled - beta * prev_ref[q]
        w_ref[q] = value
        apart = value - pivot0 * inc
        square = square + folded(inc * inc)
        cross = cross + folded(inc * scaled)
        mixed = mixed + folded(apart * inc)
        rest = rest + folded(apart * apart)
    store_sums(
        out_ref,
        square0 + reduced(square), cross0 + reduced(cross), mixed0 + reduced(mixed), rest0 + reduced(rest), pivot0,
    )


def merged(parts):
    square = sum(part[0] for part in parts)
    cross = sum(part[1] for part in parts)
    pivot = ratio(cross, square)
    mixed, rest = F32(0.0), F32(0.0)
    for part in parts:
        shift = part[4] - pivot
        mixed = mixed + part[2] + shift * part[0]
        rest = rest + part[3] + 2.0 * shift * part[2] + shift * shift * part[0]
    return square, cross, mixed, rest, pivot


def merge_kernel(*refs):
    store_sums(refs[-1], *merged([load_sums(ref) for ref in refs[:-1]]))


def final_kernel(rows, levels, cells, count, *refs):
    sums_refs = refs[:count]
    w_far_ref, w_ref, inc_t_ref, inc_ref, out_hbm, coef_ref, out_ref, sems = refs[count:]
    tile = lax.axis_index("tile")
    _, _, _, rest, pivot = merged([load_sums(ref) for ref in sums_refs])
    scale = jnp.sqrt(rest / cells + 1e-6)
    lane = lax.broadcasted_iota(jnp.int32, scale.shape, 1)
    coef_ref[...] = jnp.where(lane == 0, 1.0 + pivot, scale)[:, :2]
    over = 1.0 / scale
    wide_pivot, wide_over = (jnp.concatenate([value] * w_ref.shape[0], axis=1) for value in (pivot, over))
    step = up_to(up_to(levels, 8) // 4, 8)
    copies = []
    for low in range(0, levels, step):
        high = min(levels, low + step)
        span = slice(low * rows, high * rows)
        for piece in range(w_ref.shape[0]):
            lanes = slice(piece * 128, (piece + 1) * 128)
            out_ref[piece, span, :] = (w_ref[piece, span, :] - pivot * inc_ref[span, lanes]) * over
        for q in range(DIFF):
            value = (w_far_ref[q, low:high] - wide_pivot * inc_t_ref[q, low:high]) * wide_over
            put_row(out_ref, grid_row(tile, q, rows) + low * rows, rows, value)
        for piece in range(w_ref.shape[0]):
            lanes = slice(piece * 128, (piece + 1) * 128)
            source, target = out_ref.at[piece, span, :], out_hbm.at[span, lanes]
            copies.append(pltpu.make_async_copy(source, target, sems.at[len(copies)]))
            copies[-1].start()
    for copy in copies:
        copy.wait()


def call(kernel, ins, outs, scratch=(), cost=None, limit=VMEM_LIMIT):
    spaces = {"s": pltpu.SMEM, "v": pltpu.VMEM, "h": pltpu.HBM}
    outs = [out if isinstance(out[0], str) else ("v", out) for out in outs]
    estimate = None
    if cost is not None:
        estimate = pl.CostEstimate(flops=cost[0], bytes_accessed=cost[1], transcendentals=0)
    return pl.pallas_call(
        kernel,
        out_shape=tuple(jax.ShapeDtypeStruct(shape, F32) for _, shape in outs),
        in_specs=[pl.BlockSpec(memory_space=spaces[kind]) for kind, _ in ins],
        out_specs=tuple(pl.BlockSpec(memory_space=spaces[kind]) for kind, _ in outs),
        scratch_shapes=scratch,
        compiler_params=pltpu.CompilerParams(vmem_limit_bytes=limit),
        cost_estimate=estimate,
    )(*(value for _, value in ins))


def flipped(axis, bit):
    count = lax.axis_size(axis)
    return [(i, i ^ bit) for i in range(count)]


def rotated(axis, digit, radix, by):
    count = lax.axis_size(axis)

    def target(i):
        value = i // digit % radix
        return i + ((value + by) % radix - value) * digit

    return [(i, target(i)) for i in range(count)]


def radices(count):
    out = [] if count % 2 else [2]
    rest = count // 2 if out else count
    factor = 4
    while rest > 1:
        while factor > 1 and rest % factor:
            factor -= 1
        if factor == 1:
            factor = rest
        out.append(factor)
        rest //= factor
        factor = min(factor, 4)
    return out


def per_device(increment, previous, beta_prev, members, band_widths, diffusion_steps):
    levels, rows, width = increment.shape
    tiles, mems = lax.axis_size("tile"), lax.axis_size("mem")
    owned = members.shape[0]
    tall, deep = up_to(levels, 8), up_to(levels, 16)
    inverse = 1.0 / (owned * mems - 1)
    cells = levels * rows * tiles * width
    lanes = width // 128
    inc = increment.reshape(levels * rows, width)
    prev = previous.reshape(levels * rows, width)
    bands = band_widths.reshape(1, levels)
    s_high, s_low, waves = sine_matrix(width)
    edge = (owned, DIFF, tall, width)
    part = (rows - 2 * DIFF) // 2
    near_pairs = [(i, i ^ 1) for i in range(tiles) if i ^ 1 < tiles]
    far_pairs = [pair for i in range(1, tiles - 1, 2) for pair in ((i, i + 1), (i + 1, i))]
    pad = pltpu.VMEM((8, 128), F32)

    def edges(near):
        (value,) = call(
            functools.partial(edge_kernel, near, rows, levels),
            [("h", bands), ("h", members), ("h", increment), ("h", s_high), ("h", s_low)],
            [(owned, lanes, DIFF * levels, 128)],
            [
                pltpu.VMEM((1, levels), jnp.int32),
                pltpu.VMEM((owned, levels, 8, width), jnp.bfloat16),
                pltpu.VMEM((levels, 8, width), F32),
                pltpu.VMEM((width, width), jnp.bfloat16),
                pltpu.VMEM((width, width), jnp.bfloat16),
                pltpu.VMEM((lanes, deep * 8, 128), F32),
                pad,
                pltpu.SemaphoreType.DMA((owned + 4,)),
            ],
            limit=EDGE_LIMIT if near else VMEM_LIMIT,
        )
        return value

    near_edge = edges(True)
    near_halo = lax.ppermute(near_edge, "tile", near_pairs)
    far_edge = edges(False)
    members, far_edge = lax.optimization_barrier((members, far_edge))
    mem = members.reshape(owned, levels * rows, width)

    piece, four = (part, tall, width), (DIFF, tall, width)
    mine, theirs, cov_near, cov_far, mem_near, mem_far = call(
        functools.partial(own_kernel, rows, levels, tiles),
        [("v", bands), ("s", diffusion_steps), ("v", mem), ("v", inc)]
        + [("v", s_high), ("v", s_low), ("v", waves)],
        [piece, piece, four, four, edge, edge],
        [pltpu.VMEM((lanes, deep * rows, 128), F32)] * 2
        + [pltpu.VMEM((rows, tall, width), F32)] * 2
        + [pltpu.VMEM((DIFF, 3, 8, width), F32), pad],
        (200_000_000, 10_000_000),
    )
    prev, _ = lax.optimization_barrier((prev, theirs))
    inc_t, prev_t = call(
        functools.partial(turn_kernel, rows, levels),
        [("v", inc), ("v", prev)],
        [(rows, tall, width), (rows, tall, width)],
        [pltpu.VMEM((lanes, tall * rows, 128), F32)],
    )
    theirs, far_edge = lax.optimization_barrier((theirs, far_edge))
    far_halo = lax.ppermute(far_edge, "tile", far_pairs)
    bits = [1 << k for k in range(1, mems.bit_length() - 1)]
    mine = mine + lax.ppermute(theirs, "mem", flipped("mem", 1))
    for bit in bits:
        mine = mine + lax.ppermute(mine, "mem", flipped("mem", bit))
    other = lax.ppermute(mine, "mem", flipped("mem", 1))

    def edge_sum(near, halo, mem_rows, cov, outs):
        return call(
            functools.partial(halo_kernel, near, levels, tiles),
            [("s", diffusion_steps), ("v", halo), ("v", mem_rows), ("v", cov)]
            + [("v", s_high), ("v", s_low), ("v", waves)],
            outs,
            [pltpu.VMEM(four, F32), pltpu.VMEM((DIFF, 2, 8, width), F32)],
        )

    two = (DIFF // 2, tall, width)
    near_mine, near_theirs = edge_sum(True, near_halo, mem_near, cov_near, [two, two])
    near_mine = near_mine + lax.ppermute(near_theirs, "mem", flipped("mem", 1))
    for bit in bits:
        near_mine = near_mine + lax.ppermute(near_mine, "mem", flipped("mem", bit))
    near_other = lax.ppermute(near_mine, "mem", flipped("mem", 1))
    cov_far, near_mine, inc_t = lax.optimization_barrier((cov_far, near_mine, inc_t))
    w_rest, sums = call(
        functools.partial(bulk_kernel, rows, levels, inverse),
        [("s", beta_prev), ("v", mine), ("v", other), ("v", near_mine), ("v", near_other)]
        + [("v", inc_t), ("v", prev_t)],
        [(lanes, levels * rows, 128), (8, 128)],
        [pltpu.VMEM((rows - DIFF, tall, width), F32)],
    )
    far_mine, far_theirs = edge_sum(False, far_halo, mem_far, cov_far, [two, two])
    far_mine = far_mine + lax.ppermute(far_theirs, "mem", flipped("mem", 1))
    for bit in bits:
        far_mine = far_mine + lax.ppermute(far_mine, "mem", flipped("mem", bit))
    far_other = lax.ppermute(far_mine, "mem", flipped("mem", 1))
    w_far, sums = call(
        functools.partial(last_kernel, inverse),
        [("s", beta_prev), ("v", sums), ("v", far_mine), ("v", far_other), ("v", inc_t), ("v", prev_t)],
        [four, (8, 128)],
    )
    digit = 1
    stages = radices(tiles)
    for index, radix in enumerate(stages):
        parts = [sums] + [lax.ppermute(sums, "tile", rotated("tile", digit, radix, by)) for by in range(1, radix)]
        if index < len(stages) - 1:
            (sums,) = call(merge_kernel, [("v", value) for value in parts], [(8, 128)])
        digit *= radix
    out, coefficients = call(
        functools.partial(final_kernel, rows, levels, cells, len(parts)),
        [("v", value) for value in parts] + [("v", w_far), ("v", w_rest), ("v", inc_t), ("v", inc)],
        [("h", (levels * rows, width)), (1, 2)],
        [pltpu.VMEM((lanes, levels * rows, 128), F32), pltpu.SemaphoreType.DMA((4 * lanes,))],
    )
    return out.reshape(levels, rows, width), coefficients.reshape(2)


def solution(mesh):
    in_specs = (
        P(None, "tile", None),
        P(None, "tile", None),
        P(),
        P("mem", None, "tile", None),
        P(),
        P(),
    )
    out_specs = (P(None, "tile", None), P())
    return jax.shard_map(
        per_device, mesh=mesh, in_specs=in_specs, out_specs=out_specs, check_vma=False
    )
```

```python
import functools

import jax
import jax.numpy as jnp
import ml_dtypes
import numpy as np
from jax import lax
from jax.experimental import pallas as pl
from jax.experimental.pallas import tpu as pltpu
from jax.sharding import PartitionSpec as P

DIFF = 4
RATE = 0.24
F32 = jnp.float32
VMEM_LIMIT = 32 * 1024 * 1024
EDGE_LIMIT = 60 * 1024 * 1024


def up_to(value, unit):
    return -(-value // unit) * unit


def grid_row(tile, row, rows):
    return jnp.where(tile % 2 == 0, row, rows - 1 - row)


def put_flat(ref, value):
    for piece in range(ref.shape[0]):
        ref[piece, : value.shape[0], :] = value[:, piece * 128 : (piece + 1) * 128]


def strided(ref, start, count, stride):
    pieces = [ref[piece, pl.ds(start, count, stride=stride), :] for piece in range(ref.shape[0])]
    return jnp.concatenate(pieces, axis=1)


def sweep_counts(steps_ref, tile, tiles):
    even = tile % 2 == 0
    near = jnp.where(even, tile + 1, tile - 1)
    far = jnp.where(even, tile - 1, tile + 1)

    def count(index):
        inside = (index >= 0) & (index < tiles)
        return jnp.where(inside, steps_ref[jnp.clip(index, 0, tiles - 1)], 0)

    return count(tile), count(near), count(far)


def coefficient(sweep, count):
    return jnp.where(sweep < count, F32(RATE), F32(0.0))


def build_vertical(bands_ref, pad_ref, levels):
    pad_ref[...] = jnp.ones(pad_ref.shape, F32)
    pad_ref[0:1, 0:levels] = bands_ref[...].astype(F32)
    across = jnp.broadcast_to(pad_ref[0:1, :], (128, 128))
    down = across.T
    i = lax.broadcasted_iota(jnp.int32, (128, 128), 0)
    j = lax.broadcasted_iota(jnp.int32, (128, 128), 1)
    apart = (i - j).astype(F32)
    weight = jnp.exp(-(apart * apart) / (down * across))
    keep = (jnp.abs(apart) <= jnp.minimum(down, across)) & (i < levels) & (j < levels)
    full = jnp.where(keep, weight, F32(0.0))[: up_to(levels, 8)]
    high = full.astype(jnp.bfloat16).astype(F32)
    blank = jnp.zeros(full.shape, F32)
    deep = up_to(levels, 16)
    high, low = jnp.concatenate([high, blank], axis=1), jnp.concatenate([full - high, blank], axis=1)
    stacked = high + pltpu.roll(high, deep, 1) + pltpu.roll(low, 2 * deep, 1)
    return stacked.astype(jnp.bfloat16)


def apply_vertical(vertical, field):
    high = field.astype(jnp.bfloat16)
    low = (field - high.astype(F32)).astype(jnp.bfloat16)
    blank = jnp.zeros((vertical.shape[1] - 3 * field.shape[0], field.shape[1]), jnp.bfloat16)
    stacked = jnp.concatenate([high, low, high, blank], axis=0)
    return jnp.dot(vertical, stacked, preferred_element_type=F32)


def sine_matrix(width):
    mode = np.arange(1, width + 1)
    full = np.sqrt(2.0 / (width + 1)) * np.sin(np.pi * np.outer(mode, mode) / (width + 1))
    high = full.astype(ml_dtypes.bfloat16)
    low = (full - high.astype(np.float64)).astype(ml_dtypes.bfloat16)
    waves = np.broadcast_to(2.0 * np.cos(np.pi * mode / (width + 1)), (8, width)).astype(np.float32)
    return jnp.asarray(high), jnp.asarray(low), jnp.asarray(waves)


def transform(field, s_high, s_low):
    high = field.astype(jnp.bfloat16)
    low = (field - high.astype(F32)).astype(jnp.bfloat16)
    dot = functools.partial(jnp.dot, preferred_element_type=F32)
    return dot(high, s_high) + dot(low, s_high) + dot(high, s_low)


def advance(field, rates, bases):
    new = {}
    for p, rate in rates.items():
        near = [field[p + d] for d in (-1, 1) if p + d in field]
        value = None
        if near:
            value = rate * (near[0] + near[1] if len(near) == 2 else near[0])
        if p in field:
            here = bases[p] * field[p]
            value = here if value is None else here + value
        if value is not None:
            new[p] = value
    return new


def base_of(rate, waves):
    return (1.0 - 4.0 * rate) + rate * waves


def edge_kernel(
    near, rows, levels,
    bands_hbm, members_hbm, inc_hbm, s_high_hbm, s_low_hbm, out_ref,
    bands_ref, mem_ref, inc_ref, s_high_ref, s_low_ref, prod_ref, pad_ref, sems,
):
    tile = lax.axis_index("tile")
    high_end = (tile % 2 == 0) == near
    start = pl.multiple_of(jnp.where(high_end, rows - 8, 0), 8)
    owned = members_hbm.shape[0]
    pairs = [(bands_hbm, bands_ref), (inc_hbm.at[:, pl.ds(start, 8), :], inc_ref)]
    pairs += [(members_hbm.at[m, :, pl.ds(start, 8), :], mem_ref.at[m]) for m in range(owned)]
    pairs += [(s_high_hbm, s_high_ref), (s_low_hbm, s_low_ref)]
    copies = [pltpu.make_async_copy(source, target, sems.at[k]) for k, (source, target) in enumerate(pairs)]
    for copy in copies:
        copy.start()
    width = inc_ref.shape[-1]
    deep, tall = up_to(levels, 16), up_to(levels, 8)
    for piece in range(width // 128):
        prod_ref[piece, levels * 8 :, :] = jnp.zeros((prod_ref.shape[1] - levels * 8, 128), F32)
    copies[0].wait()
    vertical = build_vertical(bands_ref, pad_ref, levels)
    copies[1].wait()
    for m in range(owned):
        copies[2 + m].wait()
        product = mem_ref[m].astype(F32) * inc_ref[...]
        put_flat(prod_ref, product.reshape(levels * 8, width))
        local = []
        for q in range(DIFF):
            row = jnp.where(high_end, 7 - q, q)
            local.append(apply_vertical(vertical, strided(prod_ref, row, deep, 8)))
        if m == 0:
            copies[2 + owned].wait()
            copies[3 + owned].wait()
        waves = transform(jnp.concatenate(local, axis=0), s_high_ref[...], s_low_ref[...])
        for q in range(DIFF):
            for piece in range(width // 128):
                part = waves[q * tall : q * tall + levels, piece * 128 : (piece + 1) * 128]
                out_ref[m, piece, pl.ds(q, levels, stride=DIFF), :] = part


def turn_kernel(rows, levels, inc_ref, prev_ref, inc_t_ref, prev_t_ref, flat_ref):
    tile = lax.axis_index("tile")
    for piece in range(flat_ref.shape[0]):
        flat_ref[piece, rows * levels :, :] = jnp.zeros((flat_ref.shape[1] - rows * levels, 128), F32)
    for source, target in ((inc_ref, inc_t_ref), (prev_ref, prev_t_ref)):
        put_flat(flat_ref, source[...])
        for row in range(rows):
            target[row] = strided(flat_ref, grid_row(tile, row, rows), target.shape[1], rows)


def own_kernel(
    rows, levels, tiles,
    bands_ref, steps_ref, members_ref, inc_ref, s_high_ref, s_low_ref, waves_ref,
    mine_ref, theirs_ref, cov_near_ref, cov_far_ref, mem_near_ref, mem_far_ref,
    prod_ref, memf_ref, spec_ref, acc_ref, base_ref, pad_ref,
):
    tile = lax.axis_index("tile")
    half = lax.axis_index("mem") % 2
    counts = sweep_counts(steps_ref, tile, tiles)
    vertical = build_vertical(bands_ref, pad_ref, levels)
    deep, tall = up_to(levels, 16), up_to(levels, 8)
    total = rows * levels
    width = inc_ref.shape[-1]
    for ref in (prod_ref, memf_ref):
        for piece in range(width // 128):
            ref[piece, total:, :] = jnp.zeros((ref.shape[1] - total, 128), F32)

    def row_of(ref, row, count):
        return strided(ref, grid_row(tile, row, rows), count, rows)

    rate = [[coefficient(k, count) for count in counts] for k in range(DIFF)]
    for k in range(DIFF):
        for side in range(3):
            base_ref[k, side] = base_of(rate[k][side], waves_ref[...])

    def side_of(p):
        return 2 if p < 0 else 1 if p >= rows else 0

    for m in range(members_ref.shape[0]):
        as_float = members_ref[m].astype(F32)
        put_flat(memf_ref, as_float)
        put_flat(prod_ref, transform(as_float * inc_ref[...], s_high_ref[...], s_low_ref[...]))
        for row in range(rows):
            spec_ref[row] = apply_vertical(vertical, row_of(prod_ref, row, deep))

        def chunk(index, _):
            at = pl.ds(pl.multiple_of(index * 8, 8), 8)
            field = {p: spec_ref[p, at, :] for p in range(rows)}
            for k in range(DIFF):
                out = min(k + 1, DIFF - 1 - k)
                kept = range(-out, rows + out)
                bases = {p: base_ref[k, side_of(p)] for p in kept}
                field = advance(field, {p: rate[k][side_of(p)] for p in kept}, bases)
            for p in range(rows):
                spec_ref[p, at, :] = field[p]
            return 0

        lax.fori_loop(0, tall // 8, chunk, 0)
        group = 4
        for first in range(0, rows, group):
            block = spec_ref[first : first + group].reshape(group * tall, width)
            block = transform(block, s_high_ref[...], s_low_ref[...])
            for k in range(group):
                row = first + k
                member = row_of(memf_ref, row, tall)
                if row < DIFF:
                    mem_far_ref[m, row] = member
                if row >= rows - DIFF:
                    mem_near_ref[m, rows - 1 - row] = member
                value = member * block[k * tall : (k + 1) * tall]
                acc_ref[row] = value if m == 0 else acc_ref[row] + value
    part = (rows - 2 * DIFF) // 2
    for q in range(DIFF):
        cov_far_ref[q] = acc_ref[q]
        cov_near_ref[q] = acc_ref[rows - 1 - q]
    for q in range(part):
        mine_ref[q] = acc_ref[DIFF + half * part + q]
        theirs_ref[q] = acc_ref[DIFF + (1 - half) * part + q]


def halo_kernel(
    near, levels, tiles,
    steps_ref, halo_ref, mem_ref, cov_ref, s_high_ref, s_low_ref, waves_ref, *refs,
):
    out_refs, (spec_ref, base_ref) = refs[:-2], refs[-2:]
    counts = sweep_counts(steps_ref, lax.axis_index("tile"), tiles)
    owned, tall, width = halo_ref.shape[0], cov_ref.shape[1], cov_ref.shape[2]
    rate = [[coefficient(k, counts[0]), coefficient(k, counts[1 if near else 2])] for k in range(DIFF)]
    for k in range(DIFF):
        for side in range(2):
            base_ref[k, side] = base_of(rate[k][side], waves_ref[...])
    sums = [cov_ref[q] for q in range(DIFF)]
    for m in range(owned):
        for at in range(0, levels, 8):
            size = min(8, levels - at)
            field = {q: strided(halo_ref.at[m], q + DIFF * at, size, DIFF) for q in range(DIFF)}
            for k in range(DIFF):
                kept = range(-1 - k, DIFF - 1 - k)
                bases = {p: base_ref[k, 0 if p < 0 else 1][:size] for p in kept}
                field = advance(field, {p: rate[k][0 if p < 0 else 1] for p in kept}, bases)
            for q in range(DIFF):
                spec_ref[q, at : at + size, :] = field[-1 - q]
        if levels < tall:
            for q in range(DIFF):
                spec_ref[q, levels:, :] = jnp.zeros((tall - levels, width), F32)
        block = spec_ref[...].reshape(DIFF * tall, width)
        block = transform(block, s_high_ref[...], s_low_ref[...])
        for q in range(DIFF):
            sums[q] = sums[q] + mem_ref[m, q] * block[q * tall : (q + 1) * tall]
    part = DIFF // 2
    half = lax.axis_index("mem") % 2
    for q in range(DIFF):

        @pl.when(half == q // part)
        def _(q=q):
            out_refs[0][q % part] = sums[q]

        @pl.when(half != q // part)
        def _(q=q):
            out_refs[1][q % part] = sums[q]


def reduced(value):
    return jnp.sum(value, axis=(0, 1), keepdims=True)


def folded(value):
    return jnp.sum(value.reshape(value.shape[0] // 8, 8, value.shape[1]), axis=0)


def ratio(top, bottom):
    some = bottom != 0.0
    return jnp.where(some, top / jnp.where(some, bottom, F32(1.0)), F32(0.0))


def put_row(ref, row, rows, value):
    for piece in range(ref.shape[0]):
        part = value[:, piece * 128 : (piece + 1) * 128]
        ref[piece, pl.ds(row, value.shape[0], stride=rows), :] = part


def bulk_kernel(
    rows, levels, inverse,
    beta_ref, mine_ref, other_ref, near_mine_ref, near_other_ref, inc_ref, prev_ref,
    w_ref, sums_ref, keep_ref,
):
    beta = beta_ref[0]
    tile = lax.axis_index("tile")
    part = (rows - 2 * DIFF) // 2
    own_half = lax.axis_index("mem") % 2
    zero = jnp.zeros((8, inc_ref.shape[-1]), F32)

    def covariance(row):
        if row >= rows - DIFF:
            which, q = divmod(rows - 1 - row, DIFF // 2)
            return jnp.where(own_half == which, near_mine_ref[q], near_other_ref[q])
        which, q = divmod(row - DIFF, part)
        return jnp.where(own_half == which, mine_ref[q], other_ref[q])

    square, cross = zero, zero
    for row in range(DIFF, rows):
        inc = inc_ref[row]
        scaled = inverse * covariance(row)
        square = square + folded(inc * inc)
        cross = cross + folded(inc * scaled)
        value = scaled - beta * prev_ref[row]
        keep_ref[row - DIFF] = value
        put_row(w_ref, grid_row(tile, row, rows), rows, value[:levels])
    square, cross = reduced(square), reduced(cross)
    pivot = ratio(cross, square)
    mixed, rest = zero, zero
    for row in range(DIFF, rows):
        inc = inc_ref[row]
        apart = keep_ref[row - DIFF] - pivot * inc
        mixed = mixed + folded(apart * inc)
        rest = rest + folded(apart * apart)
    store_sums(sums_ref, square, cross, reduced(mixed), reduced(rest), pivot)


def store_sums(ref, *values):
    sub = lax.broadcasted_iota(jnp.int32, ref.shape, 0)
    out = jnp.zeros(ref.shape, F32)
    for index, value in enumerate(values):
        out = jnp.where(sub == index, value, out)
    ref[...] = out


def load_sums(ref):
    return [ref[index : index + 1, :] for index in range(5)]


def last_kernel(inverse, beta_ref, sums_ref, mine_ref, other_ref, inc_ref, prev_ref, w_ref, out_ref):
    own_half = lax.axis_index("mem") % 2
    part = DIFF // 2
    beta = beta_ref[0]
    square0, cross0, mixed0, rest0, pivot0 = [value[:, 0:1] for value in load_sums(sums_ref)]
    zero = jnp.zeros((8, inc_ref.shape[-1]), F32)
    square, cross, mixed, rest = zero, zero, zero, zero
    for q in range(DIFF):
        inc = inc_ref[q]
        which, index = divmod(q, part)
        scaled = inverse * jnp.where(own_half == which, mine_ref[index], other_ref[index])
        value = scaled - beta * prev_ref[q]
        w_ref[q] = value
        apart = value - pivot0 * inc
        square = square + folded(inc * inc)
        cross = cross + folded(inc * scaled)
        mixed = mixed + folded(apart * inc)
        rest = rest + folded(apart * apart)
    store_sums(
        out_ref,
        square0 + reduced(square), cross0 + reduced(cross), mixed0 + reduced(mixed), rest0 + reduced(rest), pivot0,
    )


def merged(parts):
    square = sum(part[0] for part in parts)
    cross = sum(part[1] for part in parts)
    pivot = ratio(cross, square)
    mixed, rest = F32(0.0), F32(0.0)
    for part in parts:
        shift = part[4] - pivot
        mixed = mixed + part[2] + shift * part[0]
        rest = rest + part[3] + 2.0 * shift * part[2] + shift * shift * part[0]
    return square, cross, mixed, rest, pivot


def merge_kernel(*refs):
    store_sums(refs[-1], *merged([load_sums(ref) for ref in refs[:-1]]))


def final_kernel(rows, levels, cells, count, *refs):
    sums_refs = refs[:count]
    w_far_ref, w_ref, inc_t_ref, inc_ref, out_hbm, coef_ref, out_ref, sems = refs[count:]
    tile = lax.axis_index("tile")
    _, _, _, rest, pivot = merged([load_sums(ref) for ref in sums_refs])
    scale = jnp.sqrt(rest / cells + 1e-6)
    lane = lax.broadcasted_iota(jnp.int32, scale.shape, 1)
    coef_ref[...] = jnp.where(lane == 0, 1.0 + pivot, scale)[:, :2]
    over = 1.0 / scale
    wide_pivot, wide_over = (jnp.concatenate([value] * w_ref.shape[0], axis=1) for value in (pivot, over))
    step = up_to(up_to(levels, 8) // 4, 8)
    copies = []
    for low in range(0, levels, step):
        high = min(levels, low + step)
        span = slice(low * rows, high * rows)
        for piece in range(w_ref.shape[0]):
            lanes = slice(piece * 128, (piece + 1) * 128)
            out_ref[piece, span, :] = (w_ref[piece, span, :] - pivot * inc_ref[span, lanes]) * over
        for q in range(DIFF):
            value = (w_far_ref[q, low:high] - wide_pivot * inc_t_ref[q, low:high]) * wide_over
            put_row(out_ref, grid_row(tile, q, rows) + low * rows, rows, value)
        for piece in range(w_ref.shape[0]):
            lanes = slice(piece * 128, (piece + 1) * 128)
            source, target = out_ref.at[piece, span, :], out_hbm.at[span, lanes]
            copies.append(pltpu.make_async_copy(source, target, sems.at[len(copies)]))
            copies[-1].start()
    for copy in copies:
        copy.wait()


def call(kernel, ins, outs, scratch=(), cost=None, limit=VMEM_LIMIT):
    spaces = {"s": pltpu.SMEM, "v": pltpu.VMEM, "h": pltpu.HBM}
    outs = [out if isinstance(out[0], str) else ("v", out) for out in outs]
    estimate = None
    if cost is not None:
        estimate = pl.CostEstimate(flops=cost[0], bytes_accessed=cost[1], transcendentals=0)
    return pl.pallas_call(
        kernel,
        out_shape=tuple(jax.ShapeDtypeStruct(shape, F32) for _, shape in outs),
        in_specs=[pl.BlockSpec(memory_space=spaces[kind]) for kind, _ in ins],
        out_specs=tuple(pl.BlockSpec(memory_space=spaces[kind]) for kind, _ in outs),
        scratch_shapes=scratch,
        compiler_params=pltpu.CompilerParams(vmem_limit_bytes=limit),
        cost_estimate=estimate,
    )(*(value for _, value in ins))


def flipped(axis, bit):
    count = lax.axis_size(axis)
    return [(i, i ^ bit) for i in range(count)]


def rotated(axis, digit, radix, by):
    count = lax.axis_size(axis)

    def target(i):
        value = i // digit % radix
        return i + ((value + by) % radix - value) * digit

    return [(i, target(i)) for i in range(count)]


def radices(count):
    out = [] if count % 2 else [2]
    rest = count // 2 if out else count
    factor = 4
    while rest > 1:
        while factor > 1 and rest % factor:
            factor -= 1
        if factor == 1:
            factor = rest
        out.append(factor)
        rest //= factor
        factor = min(factor, 4)
    return out


def per_device(increment, previous, beta_prev, members, band_widths, diffusion_steps):
    levels, rows, width = increment.shape
    tiles, mems = lax.axis_size("tile"), lax.axis_size("mem")
    owned = members.shape[0]
    tall, deep = up_to(levels, 8), up_to(levels, 16)
    inverse = 1.0 / (owned * mems - 1)
    cells = levels * rows * tiles * width
    lanes = width // 128
    inc = increment.reshape(levels * rows, width)
    prev = previous.reshape(levels * rows, width)
    bands = band_widths.reshape(1, levels)
    s_high, s_low, waves = sine_matrix(width)
    edge = (owned, DIFF, tall, width)
    part = (rows - 2 * DIFF) // 2
    near_pairs = [(i, i ^ 1) for i in range(tiles) if i ^ 1 < tiles]
    far_pairs = [pair for i in range(1, tiles - 1, 2) for pair in ((i, i + 1), (i + 1, i))]
    pad = pltpu.VMEM((8, 128), F32)

    def edges(near):
        (value,) = call(
            functools.partial(edge_kernel, near, rows, levels),
            [("h", bands), ("h", members), ("h", increment), ("h", s_high), ("h", s_low)],
            [(owned, lanes, DIFF * levels, 128)],
            [
                pltpu.VMEM((1, levels), jnp.int32),
                pltpu.VMEM((owned, levels, 8, width), jnp.bfloat16),
                pltpu.VMEM((levels, 8, width), F32),
                pltpu.VMEM((width, width), jnp.bfloat16),
                pltpu.VMEM((width, width), jnp.bfloat16),
                pltpu.VMEM((lanes, deep * 8, 128), F32),
                pad,
                pltpu.SemaphoreType.DMA((owned + 4,)),
            ],
            limit=EDGE_LIMIT if near else VMEM_LIMIT,
        )
        return value

    near_edge = edges(True)
    near_halo = lax.ppermute(near_edge, "tile", near_pairs)
    far_edge = edges(False)
    members, far_edge = lax.optimization_barrier((members, far_edge))
    mem = members.reshape(owned, levels * rows, width)

    piece, four = (part, tall, width), (DIFF, tall, width)
    mine, theirs, cov_near, cov_far, mem_near, mem_far = call(
        functools.partial(own_kernel, rows, levels, tiles),
        [("v", bands), ("s", diffusion_steps), ("v", mem), ("v", inc)]
        + [("v", s_high), ("v", s_low), ("v", waves)],
        [piece, piece, four, four, edge, edge],
        [pltpu.VMEM((lanes, deep * rows, 128), F32)] * 2
        + [pltpu.VMEM((rows, tall, width), F32)] * 2
        + [pltpu.VMEM((DIFF, 3, 8, width), F32), pad],
        (200_000_000, 10_000_000),
    )
    prev, _ = lax.optimization_barrier((prev, theirs))
    inc_t, prev_t = call(
        functools.partial(turn_kernel, rows, levels),
        [("v", inc), ("v", prev)],
        [(rows, tall, width), (rows, tall, width)],
        [pltpu.VMEM((lanes, tall * rows, 128), F32)],
    )
    theirs, far_edge = lax.optimization_barrier((theirs, far_edge))
    far_halo = lax.ppermute(far_edge, "tile", far_pairs)
    bits = [1 << k for k in range(1, mems.bit_length() - 1)]
    mine = mine + lax.ppermute(theirs, "mem", flipped("mem", 1))
    for bit in bits:
        mine = mine + lax.ppermute(mine, "mem", flipped("mem", bit))
    other = lax.ppermute(mine, "mem", flipped("mem", 1))

    def edge_sum(near, halo, mem_rows, cov, outs):
        return call(
            functools.partial(halo_kernel, near, levels, tiles),
            [("s", diffusion_steps), ("v", halo), ("v", mem_rows), ("v", cov)]
            + [("v", s_high), ("v", s_low), ("v", waves)],
            outs,
            [pltpu.VMEM(four, F32), pltpu.VMEM((DIFF, 2, 8, width), F32)],
        )

    two = (DIFF // 2, tall, width)
    near_mine, near_theirs = edge_sum(True, near_halo, mem_near, cov_near, [two, two])
    near_mine = near_mine + lax.ppermute(near_theirs, "mem", flipped("mem", 1))
    for bit in bits:
        near_mine = near_mine + lax.ppermute(near_mine, "mem", flipped("mem", bit))
    near_other = lax.ppermute(near_mine, "mem", flipped("mem", 1))
    cov_far, near_mine, inc_t = lax.optimization_barrier((cov_far, near_mine, inc_t))
    w_rest, sums = call(
        functools.partial(bulk_kernel, rows, levels, inverse),
        [("s", beta_prev), ("v", mine), ("v", other), ("v", near_mine), ("v", near_other)]
        + [("v", inc_t), ("v", prev_t)],
        [(lanes, levels * rows, 128), (8, 128)],
        [pltpu.VMEM((rows - DIFF, tall, width), F32)],
    )
    far_mine, far_theirs = edge_sum(False, far_halo, mem_far, cov_far, [two, two])
    far_mine = far_mine + lax.ppermute(far_theirs, "mem", flipped("mem", 1))
    for bit in bits:
        far_mine = far_mine + lax.ppermute(far_mine, "mem", flipped("mem", bit))
    far_other = lax.ppermute(far_mine, "mem", flipped("mem", 1))
    w_far, sums = call(
        functools.partial(last_kernel, inverse),
        [("s", beta_prev), ("v", sums), ("v", far_mine), ("v", far_other), ("v", inc_t), ("v", prev_t)],
        [four, (8, 128)],
    )
    digit = 1
    stages = radices(tiles)
    for index, radix in enumerate(stages):
        parts = [sums] + [lax.ppermute(sums, "tile", rotated("tile", digit, radix, by)) for by in range(1, radix)]
        if index < len(stages) - 1:
            (sums,) = call(merge_kernel, [("v", value) for value in parts], [(8, 128)])
        digit *= radix
    out, coefficients = call(
        functools.partial(final_kernel, rows, levels, cells, len(parts)),
        [("v", value) for value in parts] + [("v", w_far), ("v", w_rest), ("v", inc_t), ("v", inc)],
        [("h", (levels * rows, width)), (1, 2)],
        [pltpu.VMEM((lanes, levels * rows, 128), F32), pltpu.SemaphoreType.DMA((4 * lanes,))],
    )
    return out.reshape(levels, rows, width), coefficients.reshape(2)


def solution(mesh):
    in_specs = (
        P(None, "tile", None),
        P(None, "tile", None),
        P(),
        P("mem", None, "tile", None),
        P(),
        P(),
    )
    out_specs = (P(None, "tile", None), P())
    return jax.shard_map(
        per_device, mesh=mesh, in_specs=in_specs, out_specs=out_specs, check_vma=False
    )
```

```python
import functools

import jax
import jax.numpy as jnp
import ml_dtypes
import numpy as np
from jax import lax
from jax.experimental import pallas as pl
from jax.experimental.pallas import tpu as pltpu
from jax.sharding import PartitionSpec as P

DIFF = 4
RATE = 0.24
F32 = jnp.float32
VMEM_LIMIT = 32 * 1024 * 1024
EDGE_LIMIT = 60 * 1024 * 1024


def up_to(value, unit):
    return -(-value // unit) * unit


def grid_row(tile, row, rows):
    return jnp.where(tile % 2 == 0, row, rows - 1 - row)


def put_flat(ref, value):
    for piece in range(ref.shape[0]):
        ref[piece, : value.shape[0], :] = value[:, piece * 128 : (piece + 1) * 128]


def strided(ref, start, count, stride):
    pieces = [ref[piece, pl.ds(start, count, stride=stride), :] for piece in range(ref.shape[0])]
    return jnp.concatenate(pieces, axis=1)


def put_row(ref, row, rows, value):
    for piece in range(ref.shape[0]):
        part = value[:, piece * 128 : (piece + 1) * 128]
        ref[piece, pl.ds(row, value.shape[0], stride=rows), :] = part


def sweep_counts(steps_ref, tile, tiles):
    even = tile % 2 == 0
    near = jnp.where(even, tile + 1, tile - 1)
    far = jnp.where(even, tile - 1, tile + 1)

    def count(index):
        inside = (index >= 0) & (index < tiles)
        return jnp.where(inside, steps_ref[jnp.clip(index, 0, tiles - 1)], 0)

    return count(tile), count(near), count(far)


def coefficient(sweep, count):
    return jnp.where(sweep < count, F32(RATE), F32(0.0))


def build_vertical(bands_ref, pad_ref, levels):
    pad_ref[...] = jnp.ones(pad_ref.shape, F32)
    pad_ref[0:1, 0:levels] = bands_ref[...].astype(F32)
    across = jnp.broadcast_to(pad_ref[0:1, :], (128, 128))
    down = across.T
    i = lax.broadcasted_iota(jnp.int32, (128, 128), 0)
    j = lax.broadcasted_iota(jnp.int32, (128, 128), 1)
    apart = (i - j).astype(F32)
    weight = jnp.exp(-(apart * apart) / (down * across))
    keep = (jnp.abs(apart) <= jnp.minimum(down, across)) & (i < levels) & (j < levels)
    full = jnp.where(keep, weight, F32(0.0))[: up_to(levels, 8)]
    high = full.astype(jnp.bfloat16).astype(F32)
    blank = jnp.zeros(full.shape, F32)
    deep = up_to(levels, 16)
    high, low = jnp.concatenate([high, blank], axis=1), jnp.concatenate([full - high, blank], axis=1)
    stacked = high + pltpu.roll(high, deep, 1) + pltpu.roll(low, 2 * deep, 1)
    return stacked.astype(jnp.bfloat16)


def apply_vertical(vertical, field):
    high = field.astype(jnp.bfloat16)
    low = (field - high.astype(F32)).astype(jnp.bfloat16)
    blank = jnp.zeros((vertical.shape[1] - 3 * field.shape[0], field.shape[1]), jnp.bfloat16)
    stacked = jnp.concatenate([high, low, high, blank], axis=0)
    return jnp.dot(vertical, stacked, preferred_element_type=F32)


def sine_matrix(width):
    mode = np.arange(1, width + 1)
    full = np.sqrt(2.0 / (width + 1)) * np.sin(np.pi * np.outer(mode, mode) / (width + 1))
    high = full.astype(ml_dtypes.bfloat16)
    low = (full - high.astype(np.float64)).astype(ml_dtypes.bfloat16)
    waves = np.broadcast_to(2.0 * np.cos(np.pi * mode / (width + 1)), (8, width)).astype(np.float32)
    return jnp.asarray(high), jnp.asarray(low), jnp.asarray(waves)


def transform(field, s_high, s_low):
    high = field.astype(jnp.bfloat16)
    low = (field - high.astype(F32)).astype(jnp.bfloat16)
    dot = functools.partial(jnp.dot, preferred_element_type=F32)
    return dot(high, s_high) + dot(low, s_high) + dot(high, s_low)


def advance(field, rates, bases):
    new = {}
    for p, rate in rates.items():
        near = [field[p + d] for d in (-1, 1) if p + d in field]
        value = None
        if near:
            value = rate * (near[0] + near[1] if len(near) == 2 else near[0])
        if p in field:
            here = bases[p] * field[p]
            value = here if value is None else here + value
        if value is not None:
            new[p] = value
    return new


def base_of(rate, waves):
    return (1.0 - 4.0 * rate) + rate * waves


def product_kernel(rows, levels, members_hbm, inc_hbm, out_ref, mem_ref, inc_ref, prod_ref, sems):
    even = lax.axis_index("tile") % 2 == 0
    start = pl.multiple_of(jnp.where(even, rows - 8, 0), 8)
    owned, width = members_hbm.shape[0], inc_ref.shape[-1]
    pairs = [(inc_hbm.at[:, pl.ds(start, 8), :], inc_ref)]
    pairs += [(members_hbm.at[m, :, pl.ds(start, 8), :], mem_ref.at[m]) for m in range(owned)]
    copies = [pltpu.make_async_copy(source, target, sems.at[k]) for k, (source, target) in enumerate(pairs)]
    for copy in copies:
        copy.start()
    copies[0].wait()
    for m in range(owned):
        copies[1 + m].wait()
        put_flat(prod_ref, (mem_ref[m].astype(F32) * inc_ref[...]).reshape(levels * 8, width))
        for q in range(DIFF):
            put_row(out_ref.at[m], q, DIFF, strided(prod_ref, jnp.where(even, 7 - q, q), levels, 8))


def edge_kernel(
    rows, levels,
    bands_ref, members_ref, inc_ref, s_high_ref, s_low_ref, out_ref, prod_ref, pad_ref,
):
    tile = lax.axis_index("tile")
    deep, tall = up_to(levels, 16), up_to(levels, 8)
    total = rows * levels
    vertical = build_vertical(bands_ref, pad_ref, levels)
    for piece in range(prod_ref.shape[0]):
        prod_ref[piece, total:, :] = jnp.zeros((prod_ref.shape[1] - total, 128), F32)
    for m in range(members_ref.shape[0]):
        put_flat(prod_ref, members_ref[m].astype(F32) * inc_ref[...])
        local = [
            apply_vertical(vertical, strided(prod_ref, grid_row(tile, q, rows), deep, rows)) for q in range(DIFF)
        ]
        waves = transform(jnp.concatenate(local, axis=0), s_high_ref[...], s_low_ref[...])
        for q in range(DIFF):
            put_row(out_ref.at[m], q, DIFF, waves[q * tall : q * tall + levels])


def turn_kernel(rows, levels, inc_ref, prev_ref, inc_t_ref, prev_t_ref, flat_ref):
    tile = lax.axis_index("tile")
    for piece in range(flat_ref.shape[0]):
        flat_ref[piece, rows * levels :, :] = jnp.zeros((flat_ref.shape[1] - rows * levels, 128), F32)
    for source, target in ((inc_ref, inc_t_ref), (prev_ref, prev_t_ref)):
        put_flat(flat_ref, source[...])
        for row in range(rows):
            target[row] = strided(flat_ref, grid_row(tile, row, rows), target.shape[1], rows)


def own_kernel(
    rows, levels, tiles,
    bands_ref, steps_ref, members_ref, inc_ref, s_high_ref, s_low_ref, waves_ref,
    mine_ref, theirs_ref, cov_near_ref, cov_far_ref, mem_near_ref, mem_far_ref,
    prod_ref, memf_ref, spec_ref, acc_ref, base_ref, pad_ref,
):
    tile = lax.axis_index("tile")
    half = lax.axis_index("mem") % 2
    counts = sweep_counts(steps_ref, tile, tiles)
    vertical = build_vertical(bands_ref, pad_ref, levels)
    deep, tall = up_to(levels, 16), up_to(levels, 8)
    total = rows * levels
    width = inc_ref.shape[-1]
    for ref in (prod_ref, memf_ref):
        for piece in range(width // 128):
            ref[piece, total:, :] = jnp.zeros((ref.shape[1] - total, 128), F32)

    def row_of(ref, row, count):
        return strided(ref, grid_row(tile, row, rows), count, rows)

    rate = [[coefficient(k, count) for count in counts] for k in range(DIFF)]
    for k in range(DIFF):
        for side in range(3):
            base_ref[k, side] = base_of(rate[k][side], waves_ref[...])

    def side_of(p):
        return 2 if p < 0 else 1 if p >= rows else 0

    for m in range(members_ref.shape[0]):
        as_float = members_ref[m].astype(F32)
        put_flat(memf_ref, as_float)
        put_flat(prod_ref, transform(as_float * inc_ref[...], s_high_ref[...], s_low_ref[...]))
        for row in range(rows):
            spec_ref[row] = apply_vertical(vertical, row_of(prod_ref, row, deep))

        def chunk(index, _):
            at = pl.ds(pl.multiple_of(index * 8, 8), 8)
            field = {p: spec_ref[p, at, :] for p in range(rows)}
            for k in range(DIFF):
                out = min(k + 1, DIFF - 1 - k)
                kept = range(-out, rows + out)
                bases = {p: base_ref[k, side_of(p)] for p in kept}
                field = advance(field, {p: rate[k][side_of(p)] for p in kept}, bases)
            for p in range(rows):
                spec_ref[p, at, :] = field[p]
            return 0

        lax.fori_loop(0, tall // 8, chunk, 0)
        group = 4
        for first in range(0, rows, group):
            block = spec_ref[first : first + group].reshape(group * tall, width)
            block = transform(block, s_high_ref[...], s_low_ref[...])
            for k in range(group):
                row = first + k
                member = row_of(memf_ref, row, tall)
                if row < DIFF:
                    mem_far_ref[m, row] = member
                if row >= rows - DIFF:
                    mem_near_ref[m, rows - 1 - row] = member
                value = member * block[k * tall : (k + 1) * tall]
                acc_ref[row] = value if m == 0 else acc_ref[row] + value
    part = (rows - 2 * DIFF) // 2
    for q in range(DIFF):
        cov_far_ref[q] = acc_ref[q]
        cov_near_ref[q] = acc_ref[rows - 1 - q]
    for q in range(part):
        mine_ref[q] = acc_ref[DIFF + half * part + q]
        theirs_ref[q] = acc_ref[DIFF + (1 - half) * part + q]


def halo_kernel(
    near, levels, tiles,
    bands_ref, steps_ref, halo_ref, mem_ref, cov_ref, s_high_ref, s_low_ref, waves_ref, mine_ref, theirs_ref,
    spec_ref, base_ref, halo_row_ref, pad_ref,
):
    counts = sweep_counts(steps_ref, lax.axis_index("tile"), tiles)
    owned, tall, width = halo_ref.shape[0], cov_ref.shape[1], cov_ref.shape[2]
    rate = [[coefficient(k, counts[0]), coefficient(k, counts[1 if near else 2])] for k in range(DIFF)]
    for k in range(DIFF):
        for side in range(2):
            base_ref[k, side] = base_of(rate[k][side], waves_ref[...])
    if near:
        vertical = build_vertical(bands_ref, pad_ref, levels)
        halo_row_ref[levels:, :] = jnp.zeros((halo_row_ref.shape[0] - levels, width), F32)
    sums = [cov_ref[q] for q in range(DIFF)]
    for m in range(owned):
        if near:
            local = []
            for q in range(DIFF):
                halo_row_ref[:levels, :] = strided(halo_ref.at[m], q, levels, DIFF)
                local.append(apply_vertical(vertical, halo_row_ref[...]))
            waves = transform(jnp.concatenate(local, axis=0), s_high_ref[...], s_low_ref[...])
            for q in range(DIFF):
                spec_ref[q] = waves[q * tall : (q + 1) * tall]
        for at in range(0, levels, 8):
            size = min(8, levels - at)
            if near:
                field = {q: spec_ref[q, at : at + size, :] for q in range(DIFF)}
            else:
                field = {q: strided(halo_ref.at[m], q + DIFF * at, size, DIFF) for q in range(DIFF)}
            for k in range(DIFF):
                kept = range(-1 - k, DIFF - 1 - k)
                bases = {p: base_ref[k, 0 if p < 0 else 1][:size] for p in kept}
                field = advance(field, {p: rate[k][0 if p < 0 else 1] for p in kept}, bases)
            for q in range(DIFF):
                spec_ref[q, at : at + size, :] = field[-1 - q]
        if levels < tall:
            for q in range(DIFF):
                spec_ref[q, levels:, :] = jnp.zeros((tall - levels, width), F32)
        block = spec_ref[...].reshape(DIFF * tall, width)
        block = transform(block, s_high_ref[...], s_low_ref[...])
        for q in range(DIFF):
            sums[q] = sums[q] + mem_ref[m, q] * block[q * tall : (q + 1) * tall]
    part = DIFF // 2
    half = lax.axis_index("mem") % 2
    for q in range(DIFF):

        @pl.when(half == q // part)
        def _(q=q):
            mine_ref[q % part] = sums[q]

        @pl.when(half != q // part)
        def _(q=q):
            theirs_ref[q % part] = sums[q]


def reduced(value):
    return jnp.sum(value, axis=(0, 1), keepdims=True)


def folded(value):
    return jnp.sum(value.reshape(value.shape[0] // 8, 8, value.shape[1]), axis=0)


def ratio(top, bottom):
    some = bottom != 0.0
    return jnp.where(some, top / jnp.where(some, bottom, F32(1.0)), F32(0.0))


def bulk_kernel(
    rows, levels, inverse,
    beta_ref, mine_ref, other_ref, near_mine_ref, near_other_ref, inc_ref, prev_ref,
    w_ref, sums_ref, keep_ref,
):
    beta = beta_ref[0]
    tile = lax.axis_index("tile")
    part = (rows - 2 * DIFF) // 2
    own_half = lax.axis_index("mem") % 2
    zero = jnp.zeros((8, inc_ref.shape[-1]), F32)

    def covariance(row):
        if row >= rows - DIFF:
            which, q = divmod(rows - 1 - row, DIFF // 2)
            return jnp.where(own_half == which, near_mine_ref[q], near_other_ref[q])
        which, q = divmod(row - DIFF, part)
        return jnp.where(own_half == which, mine_ref[q], other_ref[q])

    square, cross = zero, zero
    for row in range(DIFF, rows):
        inc = inc_ref[row]
        scaled = inverse * covariance(row)
        square = square + folded(inc * inc)
        cross = cross + folded(inc * scaled)
        value = scaled - beta * prev_ref[row]
        keep_ref[row - DIFF] = value
        put_row(w_ref, grid_row(tile, row, rows), rows, value[:levels])
    square, cross = reduced(square), reduced(cross)
    pivot = ratio(cross, square)
    mixed, rest = zero, zero
    for row in range(DIFF, rows):
        inc = inc_ref[row]
        apart = keep_ref[row - DIFF] - pivot * inc
        mixed = mixed + folded(apart * inc)
        rest = rest + folded(apart * apart)
    store_sums(sums_ref, square, cross, reduced(mixed), reduced(rest), pivot)


def store_sums(ref, *values):
    sub = lax.broadcasted_iota(jnp.int32, ref.shape, 0)
    out = jnp.zeros(ref.shape, F32)
    for index, value in enumerate(values):
        out = jnp.where(sub == index, value, out)
    ref[...] = out


def load_sums(ref):
    return [ref[index : index + 1, :] for index in range(5)]


def last_kernel(inverse, beta_ref, sums_ref, *refs):
    mine_refs, other_refs, (inc_ref, prev_ref, w_ref, out_ref) = refs[:2], refs[2:4], refs[4:]
    own_half = lax.axis_index("mem") % 2
    part = DIFF // 2
    beta = beta_ref[0]
    square0, cross0, mixed0, rest0, pivot0 = [value[:, 0:1] for value in load_sums(sums_ref)]
    zero = jnp.zeros((8, inc_ref.shape[-1]), F32)
    square, cross, mixed, rest = zero, zero, zero, zero
    for q in range(DIFF):
        inc = inc_ref[q]
        which, index = divmod(q, part)
        mine, other = (refs[0][index] + refs[1][index] for refs in (mine_refs, other_refs))
        scaled = inverse * jnp.where(own_half == which, mine, other)
        value = scaled - beta * prev_ref[q]
        w_ref[q] = value
        apart = value - pivot0 * inc
        square = square + folded(inc * inc)
        cross = cross + folded(inc * scaled)
        mixed = mixed + folded(apart * inc)
        rest = rest + folded(apart * apart)
    store_sums(
        out_ref,
        square0 + reduced(square), cross0 + reduced(cross), mixed0 + reduced(mixed), rest0 + reduced(rest), pivot0,
    )


def merged(parts):
    square = sum(part[0] for part in parts)
    cross = sum(part[1] for part in parts)
    pivot = ratio(cross, square)
    mixed, rest = F32(0.0), F32(0.0)
    for part in parts:
        shift = part[4] - pivot
        mixed = mixed + part[2] + shift * part[0]
        rest = rest + part[3] + 2.0 * shift * part[2] + shift * shift * part[0]
    return square, cross, mixed, rest, pivot


def merge_kernel(*refs):
    store_sums(refs[-1], *merged([load_sums(ref) for ref in refs[:-1]]))


def final_kernel(rows, levels, cells, count, *refs):
    sums_refs = refs[:count]
    w_far_ref, w_ref, inc_t_ref, inc_ref, out_hbm, coef_ref, out_ref, sems = refs[count:]
    tile = lax.axis_index("tile")
    _, _, _, rest, pivot = merged([load_sums(ref) for ref in sums_refs])
    scale = jnp.sqrt(rest / cells + 1e-6)
    lane = lax.broadcasted_iota(jnp.int32, scale.shape, 1)
    coef_ref[...] = jnp.where(lane == 0, 1.0 + pivot, scale)[:, :2]
    over = 1.0 / scale
    wide_pivot, wide_over = (jnp.concatenate([value] * w_ref.shape[0], axis=1) for value in (pivot, over))
    step = up_to(up_to(levels, 8) // 4, 8)
    copies = []
    for low in range(0, levels, step):
        high = min(levels, low + step)
        span = slice(low * rows, high * rows)
        for piece in range(w_ref.shape[0]):
            lanes = slice(piece * 128, (piece + 1) * 128)
            out_ref[piece, span, :] = (w_ref[piece, span, :] - pivot * inc_ref[span, lanes]) * over
        for q in range(DIFF):
            value = (w_far_ref[q, low:high] - wide_pivot * inc_t_ref[q, low:high]) * wide_over
            put_row(out_ref, grid_row(tile, q, rows) + low * rows, rows, value)
        for piece in range(w_ref.shape[0]):
            lanes = slice(piece * 128, (piece + 1) * 128)
            source, target = out_ref.at[piece, span, :], out_hbm.at[span, lanes]
            copies.append(pltpu.make_async_copy(source, target, sems.at[len(copies)]))
            copies[-1].start()
    for copy in copies:
        copy.wait()


def call(kernel, ins, outs, scratch=(), cost=None, limit=VMEM_LIMIT):
    spaces = {"s": pltpu.SMEM, "v": pltpu.VMEM, "h": pltpu.HBM}
    outs = [out if isinstance(out[0], str) else ("v", out) for out in outs]
    estimate = None
    if cost is not None:
        estimate = pl.CostEstimate(flops=cost[0], bytes_accessed=cost[1], transcendentals=0)
    return pl.pallas_call(
        kernel,
        out_shape=tuple(jax.ShapeDtypeStruct(shape, F32) for _, shape in outs),
        in_specs=[pl.BlockSpec(memory_space=spaces[kind]) for kind, _ in ins],
        out_specs=tuple(pl.BlockSpec(memory_space=spaces[kind]) for kind, _ in outs),
        scratch_shapes=scratch,
        compiler_params=pltpu.CompilerParams(vmem_limit_bytes=limit),
        cost_estimate=estimate,
    )(*(value for _, value in ins))


def flipped(axis, bit):
    count = lax.axis_size(axis)
    return [(i, i ^ bit) for i in range(count)]


def rotated(axis, digit, radix, by):
    count = lax.axis_size(axis)

    def target(i):
        value = i // digit % radix
        return i + ((value + by) % radix - value) * digit

    return [(i, target(i)) for i in range(count)]


def radices(count):
    out = [] if count % 2 else [2]
    rest = count // 2 if out else count
    factor = 4
    while rest > 1:
        while factor > 1 and rest % factor:
            factor -= 1
        if factor == 1:
            factor = rest
        out.append(factor)
        rest //= factor
        factor = min(factor, 4)
    return out


def per_device(increment, previous, beta_prev, members, band_widths, diffusion_steps):
    levels, rows, width = increment.shape
    tiles, mems = lax.axis_size("tile"), lax.axis_size("mem")
    owned = members.shape[0]
    tall, deep = up_to(levels, 8), up_to(levels, 16)
    inverse = 1.0 / (owned * mems - 1)
    cells = levels * rows * tiles * width
    lanes = width // 128
    inc = increment.reshape(levels * rows, width)
    prev = previous.reshape(levels * rows, width)
    bands = band_widths.reshape(1, levels)
    s_high, s_low, waves = sine_matrix(width)
    edge = (owned, DIFF, tall, width)
    part = (rows - 2 * DIFF) // 2
    near_pairs = [(i, i ^ 1) for i in range(tiles) if i ^ 1 < tiles]
    far_pairs = [pair for i in range(1, tiles - 1, 2) for pair in ((i, i + 1), (i + 1, i))]
    pad = pltpu.VMEM((8, 128), F32)

    packed = (owned, lanes, DIFF * levels, 128)
    (near_edge,) = call(
        functools.partial(product_kernel, rows, levels),
        [("h", members), ("h", increment)],
        [packed],
        [
            pltpu.VMEM((owned, levels, 8, width), jnp.bfloat16),
            pltpu.VMEM((levels, 8, width), F32),
            pltpu.VMEM((lanes, levels * 8, 128), F32),
            pltpu.SemaphoreType.DMA((owned + 1,)),
        ],
        limit=EDGE_LIMIT,
    )
    near_halo = lax.ppermute(near_edge, "tile", near_pairs)
    mem = members.reshape(owned, levels * rows, width)
    (far_edge,) = call(
        functools.partial(edge_kernel, rows, levels),
        [("v", bands), ("v", mem), ("v", inc), ("v", s_high), ("v", s_low)],
        [packed],
        [pltpu.VMEM((lanes, deep * rows, 128), F32), pad],
    )
    members, far_edge = lax.optimization_barrier((members, far_edge))
    mem = members.reshape(owned, levels * rows, width)

    piece, four = (part, tall, width), (DIFF, tall, width)
    mine, theirs, cov_near, cov_far, mem_near, mem_far = call(
        functools.partial(own_kernel, rows, levels, tiles),
        [("v", bands), ("s", diffusion_steps), ("v", mem), ("v", inc)]
        + [("v", s_high), ("v", s_low), ("v", waves)],
        [piece, piece, four, four, edge, edge],
        [pltpu.VMEM((lanes, deep * rows, 128), F32)] * 2
        + [pltpu.VMEM((rows, tall, width), F32)] * 2
        + [pltpu.VMEM((DIFF, 3, 8, width), F32), pad],
        (200_000_000, 10_000_000),
    )
    prev, _ = lax.optimization_barrier((prev, theirs))
    inc_t, prev_t = call(
        functools.partial(turn_kernel, rows, levels),
        [("v", inc), ("v", prev)],
        [(rows, tall, width), (rows, tall, width)],
        [pltpu.VMEM((lanes, tall * rows, 128), F32)],
    )
    theirs, far_edge, inc_t = lax.optimization_barrier((theirs, far_edge, inc_t))
    far_halo = lax.ppermute(far_edge, "tile", far_pairs)
    bits = [1 << k for k in range(1, mems.bit_length() - 1)]
    mine = mine + lax.ppermute(theirs, "mem", flipped("mem", 1))
    for bit in bits:
        mine = mine + lax.ppermute(mine, "mem", flipped("mem", bit))
    other = lax.ppermute(mine, "mem", flipped("mem", 1))

    def edge_sum(near, halo, mem_rows, cov, outs):
        return call(
            functools.partial(halo_kernel, near, levels, tiles),
            [("v", bands), ("s", diffusion_steps), ("v", halo), ("v", mem_rows), ("v", cov)]
            + [("v", s_high), ("v", s_low), ("v", waves)],
            outs,
            [pltpu.VMEM(four, F32), pltpu.VMEM((DIFF, 2, 8, width), F32), pltpu.VMEM((deep, width), F32), pad],
        )

    two = (DIFF // 2, tall, width)
    near_mine, near_theirs = edge_sum(True, near_halo, mem_near, cov_near, [two, two])
    near_mine = near_mine + lax.ppermute(near_theirs, "mem", flipped("mem", 1))
    for bit in bits:
        near_mine = near_mine + lax.ppermute(near_mine, "mem", flipped("mem", bit))
    near_other = lax.ppermute(near_mine, "mem", flipped("mem", 1))
    cov_far, near_mine, inc_t = lax.optimization_barrier((cov_far, near_mine, inc_t))
    w_rest, sums = call(
        functools.partial(bulk_kernel, rows, levels, inverse),
        [("s", beta_prev), ("v", mine), ("v", other), ("v", near_mine), ("v", near_other)]
        + [("v", inc_t), ("v", prev_t)],
        [(lanes, levels * rows, 128), (8, 128)],
        [pltpu.VMEM((rows - DIFF, tall, width), F32)],
    )
    far_mine, far_theirs = edge_sum(False, far_halo, mem_far, cov_far, [two, two])
    far_mine = far_mine + lax.ppermute(far_theirs, "mem", flipped("mem", 1))
    for bit in bits[:-1]:
        far_mine = far_mine + lax.ppermute(far_mine, "mem", flipped("mem", bit))
    far_sums = [far_mine, lax.ppermute(far_mine, "mem", flipped("mem", bits[-1]))]
    far_others = [lax.ppermute(value, "mem", flipped("mem", 1)) for value in far_sums]
    w_far, sums = call(
        functools.partial(last_kernel, inverse),
        [("s", beta_prev), ("v", sums)]
        + [("v", value) for value in far_sums + far_others + [inc_t, prev_t]],
        [four, (8, 128)],
    )
    digit = 1
    stages = radices(tiles)
    for index, radix in enumerate(stages):
        parts = [sums] + [lax.ppermute(sums, "tile", rotated("tile", digit, radix, by)) for by in range(1, radix)]
        if index < len(stages) - 1:
            (sums,) = call(merge_kernel, [("v", value) for value in parts], [(8, 128)])
        digit *= radix
    out, coefficients = call(
        functools.partial(final_kernel, rows, levels, cells, len(parts)),
        [("v", value) for value in parts] + [("v", w_far), ("v", w_rest), ("v", inc_t), ("v", inc)],
        [("h", (levels * rows, width)), (1, 2)],
        [pltpu.VMEM((lanes, levels * rows, 128), F32), pltpu.SemaphoreType.DMA((4 * lanes,))],
    )
    return out.reshape(levels, rows, width), coefficients.reshape(2)


def solution(mesh):
    in_specs = (
        P(None, "tile", None),
        P(None, "tile", None),
        P(),
        P("mem", None, "tile", None),
        P(),
        P(),
    )
    out_specs = (P(None, "tile", None), P())
    return jax.shard_map(
        per_device, mesh=mesh, in_specs=in_specs, out_specs=out_specs, check_vma=False
    )
```

```python
import functools

import jax
import jax.numpy as jnp
import ml_dtypes
import numpy as np
from jax import lax
from jax.experimental import pallas as pl
from jax.experimental.pallas import tpu as pltpu
from jax.sharding import PartitionSpec as P

DIFF = 4
RATE = 0.24
F32 = jnp.float32
VMEM_LIMIT = 32 * 1024 * 1024
EDGE_LIMIT = 60 * 1024 * 1024


def up_to(value, unit):
    return -(-value // unit) * unit


def grid_row(tile, row, rows):
    return jnp.where(tile % 2 == 0, row, rows - 1 - row)


def put_flat(ref, value):
    for piece in range(ref.shape[0]):
        ref[piece, : value.shape[0], :] = value[:, piece * 128 : (piece + 1) * 128]


def strided(ref, start, count, stride):
    pieces = [ref[piece, pl.ds(start, count, stride=stride), :] for piece in range(ref.shape[0])]
    return jnp.concatenate(pieces, axis=1)


def put_row(ref, row, rows, value):
    for piece in range(ref.shape[0]):
        part = value[:, piece * 128 : (piece + 1) * 128]
        ref[piece, pl.ds(row, value.shape[0], stride=rows), :] = part


def sweep_counts(steps_ref, tile, tiles):
    even = tile % 2 == 0
    near = jnp.where(even, tile + 1, tile - 1)
    far = jnp.where(even, tile - 1, tile + 1)

    def count(index):
        inside = (index >= 0) & (index < tiles)
        return jnp.where(inside, steps_ref[jnp.clip(index, 0, tiles - 1)], 0)

    return count(tile), count(near), count(far)


def coefficient(sweep, count):
    return jnp.where(sweep < count, F32(RATE), F32(0.0))


def build_vertical(bands_ref, pad_ref, levels):
    pad_ref[...] = jnp.ones(pad_ref.shape, F32)
    pad_ref[0:1, 0:levels] = bands_ref[...].astype(F32)
    across = jnp.broadcast_to(pad_ref[0:1, :], (128, 128))
    down = across.T
    i = lax.broadcasted_iota(jnp.int32, (128, 128), 0)
    j = lax.broadcasted_iota(jnp.int32, (128, 128), 1)
    apart = (i - j).astype(F32)
    weight = jnp.exp(-(apart * apart) / (down * across))
    keep = (jnp.abs(apart) <= jnp.minimum(down, across)) & (i < levels) & (j < levels)
    full = jnp.where(keep, weight, F32(0.0))[: up_to(levels, 8)]
    high = full.astype(jnp.bfloat16).astype(F32)
    blank = jnp.zeros(full.shape, F32)
    deep = up_to(levels, 16)
    high, low = jnp.concatenate([high, blank], axis=1), jnp.concatenate([full - high, blank], axis=1)
    stacked = high + pltpu.roll(high, deep, 1) + pltpu.roll(low, 2 * deep, 1)
    return stacked.astype(jnp.bfloat16)


def apply_vertical(vertical, field):
    high = field.astype(jnp.bfloat16)
    low = (field - high.astype(F32)).astype(jnp.bfloat16)
    blank = jnp.zeros((vertical.shape[1] - 3 * field.shape[0], field.shape[1]), jnp.bfloat16)
    stacked = jnp.concatenate([high, low, high, blank], axis=0)
    return jnp.dot(vertical, stacked, preferred_element_type=F32)


def sine_matrix(width):
    mode = np.arange(1, width + 1)
    full = np.sqrt(2.0 / (width + 1)) * np.sin(np.pi * np.outer(mode, mode) / (width + 1))
    high = full.astype(ml_dtypes.bfloat16)
    low = (full - high.astype(np.float64)).astype(ml_dtypes.bfloat16)
    waves = np.broadcast_to(2.0 * np.cos(np.pi * mode / (width + 1)), (8, width)).astype(np.float32)
    return jnp.asarray(high), jnp.asarray(low), jnp.asarray(waves)


def transform(field, s_high, s_low):
    high = field.astype(jnp.bfloat16)
    low = (field - high.astype(F32)).astype(jnp.bfloat16)
    dot = functools.partial(jnp.dot, preferred_element_type=F32)
    return dot(high, s_high) + dot(low, s_high) + dot(high, s_low)


def advance(field, rates, bases):
    new = {}
    for p, rate in rates.items():
        near = [field[p + d] for d in (-1, 1) if p + d in field]
        value = None
        if near:
            value = rate * (near[0] + near[1] if len(near) == 2 else near[0])
        if p in field:
            here = bases[p] * field[p]
            value = here if value is None else here + value
        if value is not None:
            new[p] = value
    return new


def base_of(rate, waves):
    return (1.0 - 4.0 * rate) + rate * waves


def product_kernel(rows, levels, members_hbm, inc_hbm, out_ref, mem_ref, inc_ref, prod_ref, sems):
    even = lax.axis_index("tile") % 2 == 0
    start = pl.multiple_of(jnp.where(even, rows - 8, 0), 8)
    owned, width = members_hbm.shape[0], inc_ref.shape[-1]
    pairs = [(inc_hbm.at[:, pl.ds(start, 8), :], inc_ref)]
    pairs += [(members_hbm.at[m, :, pl.ds(start, 8), :], mem_ref.at[m]) for m in range(owned)]
    copies = [pltpu.make_async_copy(source, target, sems.at[k]) for k, (source, target) in enumerate(pairs)]
    for copy in copies:
        copy.start()
    copies[0].wait()
    for m in range(owned):
        copies[1 + m].wait()
        put_flat(prod_ref, (mem_ref[m].astype(F32) * inc_ref[...]).reshape(levels * 8, width))
        for q in range(DIFF):
            put_row(out_ref.at[m], q, DIFF, strided(prod_ref, jnp.where(even, 7 - q, q), levels, 8))


def half_span(levels):
    return up_to(-(-levels // 2), 2)


def core():
    return lax.axis_index("mem") % 2


def edge_kernel(
    rows, levels,
    bands_ref, members_ref, inc_ref, s_high_ref, s_low_ref,
    far_own_ref, far_other_ref, mem_own_ref, mem_other_ref, prod_ref, pad_ref, wave_ref, pack_ref,
):
    tile = lax.axis_index("tile")
    deep, tall = up_to(levels, 16), up_to(levels, 8)
    total = rows * levels
    vertical = build_vertical(bands_ref, pad_ref, levels)
    for piece in range(prod_ref.shape[0]):
        prod_ref[piece, total:, :] = jnp.zeros((prod_ref.shape[1] - total, 128), F32)
    for m in range(members_ref.shape[0]):
        member = members_ref[m].astype(F32)
        put_flat(prod_ref, member * inc_ref[...])
        local = [
            apply_vertical(vertical, strided(prod_ref, grid_row(tile, q, rows), deep, rows)) for q in range(DIFF)
        ]
        waves = transform(jnp.concatenate(local, axis=0), s_high_ref[...], s_low_ref[...])
        put_flat(prod_ref, member)
        for q in range(DIFF):
            put_row(wave_ref.at[m], q, DIFF, waves[q * tall : q * tall + levels])
            put_row(pack_ref.at[m], q, DIFF, strided(prod_ref, grid_row(tile, q, rows), levels, rows))
    size = half_span(levels)
    for pack, own_ref, other_ref in ((wave_ref, far_own_ref, far_other_ref), (pack_ref, mem_own_ref, mem_other_ref)):
        for part, ref in ((core(), own_ref), (1 - core(), other_ref)):
            low = pl.multiple_of(part * (levels - size) * DIFF, 8)
            ref[...] = pack[:, :, pl.ds(low, size * DIFF), :]


def turn_kernel(rows, levels, inc_ref, prev_ref, inc_t_ref, prev_t_ref, flat_ref):
    tile = lax.axis_index("tile")
    for piece in range(flat_ref.shape[0]):
        flat_ref[piece, rows * levels :, :] = jnp.zeros((flat_ref.shape[1] - rows * levels, 128), F32)
    for source, target in ((inc_ref, inc_t_ref), (prev_ref, prev_t_ref)):
        put_flat(flat_ref, source[...])
        for row in range(rows):
            target[row] = strided(flat_ref, grid_row(tile, row, rows), target.shape[1], rows)


def own_kernel(
    rows, levels, tiles,
    bands_ref, steps_ref, members_ref, inc_ref, s_high_ref, s_low_ref, waves_ref,
    mine_ref, theirs_ref, cov_near_ref, cov_far_ref, cov_other_ref, mem_near_ref,
    prod_ref, memf_ref, spec_ref, acc_ref, base_ref, pad_ref,
):
    tile = lax.axis_index("tile")
    half = lax.axis_index("mem") % 2
    counts = sweep_counts(steps_ref, tile, tiles)
    vertical = build_vertical(bands_ref, pad_ref, levels)
    deep, tall = up_to(levels, 16), up_to(levels, 8)
    total = rows * levels
    width = inc_ref.shape[-1]
    for ref in (prod_ref, memf_ref):
        for piece in range(width // 128):
            ref[piece, total:, :] = jnp.zeros((ref.shape[1] - total, 128), F32)

    def row_of(ref, row, count):
        return strided(ref, grid_row(tile, row, rows), count, rows)

    rate = [[coefficient(k, count) for count in counts] for k in range(DIFF)]
    for k in range(DIFF):
        for side in range(3):
            base_ref[k, side] = base_of(rate[k][side], waves_ref[...])

    def side_of(p):
        return 2 if p < 0 else 1 if p >= rows else 0

    for m in range(members_ref.shape[0]):
        as_float = members_ref[m].astype(F32)
        put_flat(memf_ref, as_float)
        put_flat(prod_ref, transform(as_float * inc_ref[...], s_high_ref[...], s_low_ref[...]))
        for row in range(rows):
            spec_ref[row] = apply_vertical(vertical, row_of(prod_ref, row, deep))

        def chunk(index, _):
            at = pl.ds(pl.multiple_of(index * 8, 8), 8)
            field = {p: spec_ref[p, at, :] for p in range(rows)}
            for k in range(DIFF):
                out = min(k + 1, DIFF - 1 - k)
                kept = range(-out, rows + out)
                bases = {p: base_ref[k, side_of(p)] for p in kept}
                field = advance(field, {p: rate[k][side_of(p)] for p in kept}, bases)
            for p in range(rows):
                spec_ref[p, at, :] = field[p]
            return 0

        lax.fori_loop(0, tall // 8, chunk, 0)
        group = 4
        for first in range(0, rows, group):
            block = spec_ref[first : first + group].reshape(group * tall, width)
            block = transform(block, s_high_ref[...], s_low_ref[...])
            for k in range(group):
                row = first + k
                member = row_of(memf_ref, row, tall)
                if row >= rows - DIFF:
                    mem_near_ref[m, rows - 1 - row] = member
                value = member * block[k * tall : (k + 1) * tall]
                acc_ref[row] = value if m == 0 else acc_ref[row] + value
    part = (rows - 2 * DIFF) // 2
    size = half_span(levels)
    blank = jnp.zeros((cov_far_ref.shape[1] - size, width), F32)
    for q in range(DIFF):
        cov_near_ref[q] = acc_ref[rows - 1 - q]
        halves = (acc_ref[q, :size], acc_ref[q, levels - size : levels])
        for ref, first in ((cov_far_ref, half == 0), (cov_other_ref, half == 1)):
            ref[q, :size] = jnp.where(first, halves[0], halves[1])
            ref[q, size:] = blank
    for q in range(part):
        mine_ref[q] = acc_ref[DIFF + half * part + q]
        theirs_ref[q] = acc_ref[DIFF + (1 - half) * part + q]


def settle(field, rates, base_ref, size):
    for k in range(DIFF):
        kept = range(-1 - k, DIFF - 1 - k)
        bases = {p: base_ref[k, 0 if p < 0 else 1][:size] for p in kept}
        field = advance(field, {p: rates[k][0 if p < 0 else 1] for p in kept}, bases)
    return [field[-1 - q] for q in range(DIFF)]


def side_rates(near, tiles, steps_ref, waves_ref, base_ref):
    counts = sweep_counts(steps_ref, lax.axis_index("tile"), tiles)
    rates = [[coefficient(k, counts[0]), coefficient(k, counts[1 if near else 2])] for k in range(DIFF)]
    for k in range(DIFF):
        for side in range(2):
            base_ref[k, side] = base_of(rates[k][side], waves_ref[...])
    return rates


def near_kernel(
    levels, tiles,
    bands_ref, steps_ref, halo_ref, mem_ref, cov_ref, s_high_ref, s_low_ref, waves_ref, mine_ref, theirs_ref,
    spec_ref, base_ref, halo_row_ref, pad_ref,
):
    rates = side_rates(True, tiles, steps_ref, waves_ref, base_ref)
    tall, width = spec_ref.shape[1:]
    vertical = build_vertical(bands_ref, pad_ref, levels)
    halo_row_ref[levels:, :] = jnp.zeros((halo_row_ref.shape[0] - levels, width), F32)
    sums = [cov_ref[q] for q in range(DIFF)]
    for m in range(halo_ref.shape[0]):
        local = []
        for q in range(DIFF):
            halo_row_ref[:levels, :] = strided(halo_ref.at[m], q, levels, DIFF)
            local.append(apply_vertical(vertical, halo_row_ref[...]))
        waves = transform(jnp.concatenate(local, axis=0), s_high_ref[...], s_low_ref[...])
        for q in range(DIFF):
            spec_ref[q] = waves[q * tall : (q + 1) * tall]
        for at in range(0, tall, 8):
            field = {q: spec_ref[q, at : at + 8, :] for q in range(DIFF)}
            for q, value in enumerate(settle(field, rates, base_ref, 8)):
                spec_ref[q, at : at + 8, :] = value
        block = spec_ref[...].reshape(DIFF * tall, width)
        block = transform(block, s_high_ref[...], s_low_ref[...])
        for q in range(DIFF):
            sums[q] = sums[q] + mem_ref[m, q] * block[q * tall : (q + 1) * tall]
    part = DIFF // 2
    for q in range(DIFF):

        @pl.when(core() == q // part)
        def _(q=q):
            mine_ref[q % part] = sums[q]

        @pl.when(core() != q // part)
        def _(q=q):
            theirs_ref[q % part] = sums[q]


def far_kernel(
    levels, tiles,
    steps_ref, halo_ref, mem_ref, mem_other_ref, cov_ref, cov_other_ref, s_high_ref, s_low_ref, waves_ref,
    out_ref, spec_ref, base_ref,
):
    rates = side_rates(False, tiles, steps_ref, waves_ref, base_ref)
    tall, width = spec_ref.shape[2:]
    size = half_span(levels)
    owned = mem_ref.shape[0]
    for m in range(2 * owned):
        for q in range(DIFF):
            spec_ref[m, q, size:, :] = jnp.zeros((tall - size, width), F32)
        for at in range(0, size, 8):
            count = min(8, size - at)
            field = {q: strided(halo_ref.at[m], q + DIFF * at, count, DIFF) for q in range(DIFF)}
            for q, value in enumerate(settle(field, rates, base_ref, count)):
                spec_ref[m, q, at : at + count, :] = value
    block = spec_ref[...].reshape(2 * owned * DIFF * tall, width)
    spec_ref[...] = transform(block, s_high_ref[...], s_low_ref[...]).reshape(spec_ref.shape)
    for q in range(DIFF):
        out_ref[q, size:] = jnp.zeros((tall - size, width), F32)
        for at in range(0, size, 8):
            span = slice(at, min(at + 8, size))
            total = cov_ref[q, span] + cov_other_ref[q, span]
            for m in range(2 * owned):
                member_ref = (mem_ref if m < owned else mem_other_ref).at[m % owned]
                total = total + strided(member_ref, q + DIFF * at, span.stop - at, DIFF) * spec_ref[m, q, span]
            out_ref[q, span] = total


def reduced(value):
    return jnp.sum(value, axis=(0, 1), keepdims=True)


def folded(value):
    return jnp.sum(value.reshape(value.shape[0] // 8, 8, value.shape[1]), axis=0)


def ratio(top, bottom):
    some = bottom != 0.0
    return jnp.where(some, top / jnp.where(some, bottom, F32(1.0)), F32(0.0))


def bulk_kernel(
    rows, levels, inverse,
    beta_ref, mine_ref, other_ref, near_mine_ref, near_other_ref, inc_ref, prev_ref,
    w_ref, sums_ref, keep_ref,
):
    beta = beta_ref[0]
    tile = lax.axis_index("tile")
    part = (rows - 2 * DIFF) // 2
    own_half = lax.axis_index("mem") % 2
    zero = jnp.zeros((8, inc_ref.shape[-1]), F32)

    def covariance(row):
        if row >= rows - DIFF:
            which, q = divmod(rows - 1 - row, DIFF // 2)
            return jnp.where(own_half == which, near_mine_ref[q], near_other_ref[q])
        which, q = divmod(row - DIFF, part)
        return jnp.where(own_half == which, mine_ref[q], other_ref[q])

    square, cross = zero, zero
    for row in range(DIFF, rows):
        inc = inc_ref[row]
        scaled = inverse * covariance(row)
        square = square + folded(inc * inc)
        cross = cross + folded(inc * scaled)
        value = scaled - beta * prev_ref[row]
        keep_ref[row - DIFF] = value
        put_row(w_ref, grid_row(tile, row, rows), rows, value[:levels])
    square, cross = reduced(square), reduced(cross)
    pivot = ratio(cross, square)
    mixed, rest = zero, zero
    for row in range(DIFF, rows):
        inc = inc_ref[row]
        apart = keep_ref[row - DIFF] - pivot * inc
        mixed = mixed + folded(apart * inc)
        rest = rest + folded(apart * apart)
    store_sums(sums_ref, square, cross, reduced(mixed), reduced(rest), pivot)


def store_sums(ref, *values):
    sub = lax.broadcasted_iota(jnp.int32, ref.shape, 0)
    out = jnp.zeros(ref.shape, F32)
    for index, value in enumerate(values):
        out = jnp.where(sub == index, value, out)
    ref[...] = out


def load_sums(ref):
    return [ref[index : index + 1, :] for index in range(5)]


def last_kernel(inverse, levels, beta_ref, sums_ref, *refs):
    mine_refs, other_refs, (inc_ref, prev_ref, w_ref, out_ref, cov_ref) = refs[:2], refs[2:4], refs[4:]
    beta = beta_ref[0]
    square0, cross0, mixed0, rest0, pivot0 = [value[:, 0:1] for value in load_sums(sums_ref)]
    zero = jnp.zeros((8, inc_ref.shape[-1]), F32)
    square, cross, mixed, rest = zero, zero, zero, zero
    size = half_span(levels)
    for q in range(DIFF):
        mine, other = (first[q, :size] + second[q, :size] for first, second in (mine_refs, other_refs))
        cov_ref[levels:, :] = jnp.zeros((cov_ref.shape[0] - levels, cov_ref.shape[1]), F32)
        cov_ref[levels - size : levels, :] = jnp.where(core() == 1, mine, other)
        cov_ref[:size, :] = jnp.where(core() == 0, mine, other)
        inc = inc_ref[q]
        scaled = inverse * cov_ref[...]
        value = scaled - beta * prev_ref[q]
        w_ref[q] = value
        apart = value - pivot0 * inc
        square = square + folded(inc * inc)
        cross = cross + folded(inc * scaled)
        mixed = mixed + folded(apart * inc)
        rest = rest + folded(apart * apart)
    store_sums(
        out_ref,
        square0 + reduced(square), cross0 + reduced(cross), mixed0 + reduced(mixed), rest0 + reduced(rest), pivot0,
    )


def merged(parts):
    square = sum(part[0] for part in parts)
    cross = sum(part[1] for part in parts)
    pivot = ratio(cross, square)
    mixed, rest = F32(0.0), F32(0.0)
    for part in parts:
        shift = part[4] - pivot
        mixed = mixed + part[2] + shift * part[0]
        rest = rest + part[3] + 2.0 * shift * part[2] + shift * shift * part[0]
    return square, cross, mixed, rest, pivot


def merge_kernel(*refs):
    store_sums(refs[-1], *merged([load_sums(ref) for ref in refs[:-1]]))


def final_kernel(rows, levels, cells, count, *refs):
    sums_refs = refs[:count]
    w_far_ref, w_ref, inc_t_ref, inc_ref, out_hbm, coef_ref, out_ref, sems = refs[count:]
    tile = lax.axis_index("tile")
    _, _, _, rest, pivot = merged([load_sums(ref) for ref in sums_refs])
    scale = jnp.sqrt(rest / cells + 1e-6)
    lane = lax.broadcasted_iota(jnp.int32, scale.shape, 1)
    coef_ref[...] = jnp.where(lane == 0, 1.0 + pivot, scale)[:, :2]
    over = 1.0 / scale
    wide_pivot, wide_over = (jnp.concatenate([value] * w_ref.shape[0], axis=1) for value in (pivot, over))
    step = up_to(up_to(levels, 8) // 4, 8)
    copies = []
    for low in range(0, levels, step):
        high = min(levels, low + step)
        span = slice(low * rows, high * rows)
        for piece in range(w_ref.shape[0]):
            lanes = slice(piece * 128, (piece + 1) * 128)
            out_ref[piece, span, :] = (w_ref[piece, span, :] - pivot * inc_ref[span, lanes]) * over
        for q in range(DIFF):
            value = (w_far_ref[q, low:high] - wide_pivot * inc_t_ref[q, low:high]) * wide_over
            put_row(out_ref, grid_row(tile, q, rows) + low * rows, rows, value)
        for piece in range(w_ref.shape[0]):
            lanes = slice(piece * 128, (piece + 1) * 128)
            source, target = out_ref.at[piece, span, :], out_hbm.at[span, lanes]
            copies.append(pltpu.make_async_copy(source, target, sems.at[len(copies)]))
            copies[-1].start()
    for copy in copies:
        copy.wait()


def call(kernel, ins, outs, scratch=(), cost=None, limit=VMEM_LIMIT):
    spaces = {"s": pltpu.SMEM, "v": pltpu.VMEM, "h": pltpu.HBM}
    outs = [out if isinstance(out[0], str) else ("v", out) for out in outs]
    estimate = None
    if cost is not None:
        estimate = pl.CostEstimate(flops=cost[0], bytes_accessed=cost[1], transcendentals=0)
    return pl.pallas_call(
        kernel,
        out_shape=tuple(jax.ShapeDtypeStruct(shape, F32) for _, shape in outs),
        in_specs=[pl.BlockSpec(memory_space=spaces[kind]) for kind, _ in ins],
        out_specs=tuple(pl.BlockSpec(memory_space=spaces[kind]) for kind, _ in outs),
        scratch_shapes=scratch,
        compiler_params=pltpu.CompilerParams(vmem_limit_bytes=limit),
        cost_estimate=estimate,
    )(*(value for _, value in ins))


def flipped(axis, bit):
    count = lax.axis_size(axis)
    return [(i, i ^ bit) for i in range(count)]


def rotated(axis, digit, radix, by):
    count = lax.axis_size(axis)

    def target(i):
        value = i // digit % radix
        other = value ^ by if radix & (radix - 1) == 0 else (value + by) % radix
        return i + (other - value) * digit

    return [(i, target(i)) for i in range(count)]


def radices(count):
    out = [] if count % 2 else [2]
    rest = count // 2 if out else count
    factor = 4
    while rest > 1:
        while factor > 1 and rest % factor:
            factor -= 1
        if factor == 1:
            factor = rest
        out.append(factor)
        rest //= factor
        factor = min(factor, 4)
    return out


def per_device(increment, previous, beta_prev, members, band_widths, diffusion_steps):
    levels, rows, width = increment.shape
    tiles, mems = lax.axis_size("tile"), lax.axis_size("mem")
    owned = members.shape[0]
    tall, deep = up_to(levels, 8), up_to(levels, 16)
    inverse = 1.0 / (owned * mems - 1)
    cells = levels * rows * tiles * width
    lanes = width // 128
    inc = increment.reshape(levels * rows, width)
    prev = previous.reshape(levels * rows, width)
    bands = band_widths.reshape(1, levels)
    s_high, s_low, waves = sine_matrix(width)
    edge = (owned, DIFF, tall, width)
    part = (rows - 2 * DIFF) // 2
    near_pairs = [(i, i ^ 1) for i in range(tiles) if i ^ 1 < tiles]
    far_pairs = [pair for i in range(1, tiles - 1, 2) for pair in ((i, i + 1), (i + 1, i))]
    pad = pltpu.VMEM((8, 128), F32)

    packed = (owned, lanes, DIFF * levels, 128)
    (near_edge,) = call(
        functools.partial(product_kernel, rows, levels),
        [("h", members), ("h", increment)],
        [packed],
        [
            pltpu.VMEM((owned, levels, 8, width), jnp.bfloat16),
            pltpu.VMEM((levels, 8, width), F32),
            pltpu.VMEM((lanes, levels * 8, 128), F32),
            pltpu.SemaphoreType.DMA((owned + 1,)),
        ],
        limit=EDGE_LIMIT,
    )
    mem = members.reshape(owned, levels * rows, width)
    bands, near_edge = lax.optimization_barrier((bands, near_edge))
    near_halo = lax.ppermute(near_edge, "tile", near_pairs)
    size = half_span(levels)
    half_packed = (owned, lanes, DIFF * size, 128)
    pair = flipped("mem", 1)
    far_edge, far_edge_other, mem_far, mem_far_other = call(
        functools.partial(edge_kernel, rows, levels),
        [("v", bands), ("v", mem), ("v", inc), ("v", s_high), ("v", s_low)],
        [half_packed] * 4,
        [pltpu.VMEM((lanes, deep * rows, 128), F32), pad, pltpu.VMEM(packed, F32), pltpu.VMEM(packed, F32)],
    )
    far_edge_other = lax.ppermute(far_edge_other, "mem", pair)
    mem_far_other = lax.ppermute(mem_far_other, "mem", pair)
    members, far_edge = lax.optimization_barrier((members, far_edge))
    mem = members.reshape(owned, levels * rows, width)

    piece, four = (part, tall, width), (DIFF, tall, width)
    short = (DIFF, up_to(size, 8), width)
    mine, theirs, cov_near, cov_far, cov_far_other, mem_near = call(
        functools.partial(own_kernel, rows, levels, tiles),
        [("v", bands), ("s", diffusion_steps), ("v", mem), ("v", inc)]
        + [("v", s_high), ("v", s_low), ("v", waves)],
        [piece, piece, four, short, short, edge],
        [pltpu.VMEM((lanes, deep * rows, 128), F32)] * 2
        + [pltpu.VMEM((rows, tall, width), F32)] * 2
        + [pltpu.VMEM((DIFF, 3, 8, width), F32), pad],
        (20_000_000, 1_000_000),
    )
    prev, _ = lax.optimization_barrier((prev, theirs))
    inc_t, prev_t = call(
        functools.partial(turn_kernel, rows, levels),
        [("v", inc), ("v", prev)],
        [(rows, tall, width), (rows, tall, width)],
        [pltpu.VMEM((lanes, tall * rows, 128), F32)],
    )
    theirs, far_edge_other = lax.optimization_barrier((theirs, far_edge_other))
    far_edge = jnp.concatenate([far_edge, far_edge_other])
    far_halo = lax.ppermute(far_edge, "tile", far_pairs)
    bits = [1 << k for k in range(1, mems.bit_length() - 1)]
    mine = mine + lax.ppermute(theirs, "mem", flipped("mem", 1))
    for bit in bits:
        mine = mine + lax.ppermute(mine, "mem", flipped("mem", bit))
    other = lax.ppermute(mine, "mem", flipped("mem", 1))

    cov_far_other = lax.ppermute(cov_far_other, "mem", pair)
    two = (DIFF // 2, tall, width)
    near_mine, near_theirs = call(
        functools.partial(near_kernel, levels, tiles),
        [("v", bands), ("s", diffusion_steps), ("v", near_halo), ("v", mem_near), ("v", cov_near)]
        + [("v", s_high), ("v", s_low), ("v", waves)],
        [two, two],
        [pltpu.VMEM(four, F32), pltpu.VMEM((DIFF, 2, 8, width), F32), pltpu.VMEM((deep, width), F32), pad],
    )
    near_mine = near_mine + lax.ppermute(near_theirs, "mem", flipped("mem", 1))
    for bit in bits:
        near_mine = near_mine + lax.ppermute(near_mine, "mem", flipped("mem", bit))
    near_other = lax.ppermute(near_mine, "mem", flipped("mem", 1))
    cov_far, near_other, inc_t = lax.optimization_barrier((cov_far, near_other, inc_t))
    w_rest, sums = call(
        functools.partial(bulk_kernel, rows, levels, inverse),
        [("s", beta_prev), ("v", mine), ("v", other), ("v", near_mine), ("v", near_other)]
        + [("v", inc_t), ("v", prev_t)],
        [(lanes, levels * rows, 128), (8, 128)],
        [pltpu.VMEM((rows - DIFF, tall, width), F32)],
    )
    (cov,) = call(
        functools.partial(far_kernel, levels, tiles),
        [("s", diffusion_steps), ("v", far_halo), ("v", mem_far), ("v", mem_far_other)]
        + [("v", cov_far), ("v", cov_far_other), ("v", s_high), ("v", s_low), ("v", waves)],
        [short],
        [pltpu.VMEM((2 * owned, *short), F32), pltpu.VMEM((DIFF, 2, 8, width), F32)],
    )
    for bit in bits[:-1]:
        cov = cov + lax.ppermute(cov, "mem", flipped("mem", bit))
    far_sums = [cov, lax.ppermute(cov, "mem", flipped("mem", bits[-1]))]
    far_others = [lax.ppermute(value, "mem", pair) for value in far_sums]
    w_far, sums = call(
        functools.partial(last_kernel, inverse, levels),
        [("s", beta_prev), ("v", sums)]
        + [("v", value) for value in far_sums + far_others + [inc_t, prev_t]],
        [four, (8, 128)],
        [pltpu.VMEM((tall, width), F32)],
    )
    digit = 1
    stages = radices(tiles)
    for index, radix in enumerate(stages):
        parts = [sums] + [lax.ppermute(sums, "tile", rotated("tile", digit, radix, by)) for by in range(1, radix)]
        if index < len(stages) - 1:
            (sums,) = call(merge_kernel, [("v", value) for value in parts], [(8, 128)])
        digit *= radix
    out, coefficients = call(
        functools.partial(final_kernel, rows, levels, cells, len(parts)),
        [("v", value) for value in parts] + [("v", w_far), ("v", w_rest), ("v", inc_t), ("v", inc)],
        [("h", (levels * rows, width)), (1, 2)],
        [pltpu.VMEM((lanes, levels * rows, 128), F32), pltpu.SemaphoreType.DMA((4 * lanes,))],
    )
    return out.reshape(levels, rows, width), coefficients.reshape(2)


def solution(mesh):
    in_specs = (
        P(None, "tile", None),
        P(None, "tile", None),
        P(),
        P("mem", None, "tile", None),
        P(),
        P(),
    )
    out_specs = (P(None, "tile", None), P())
    return jax.shard_map(
        per_device, mesh=mesh, in_specs=in_specs, out_specs=out_specs, check_vma=False
    )
```

```python
import functools

import jax
import jax.numpy as jnp
import ml_dtypes
import numpy as np
from jax import lax
from jax.experimental import pallas as pl
from jax.experimental.pallas import tpu as pltpu
from jax.sharding import PartitionSpec as P

DIFF = 4
RATE = 0.24
F32 = jnp.float32
VMEM_LIMIT = 32 * 1024 * 1024
EDGE_LIMIT = 60 * 1024 * 1024


def up_to(value, unit):
    return -(-value // unit) * unit


def grid_row(tile, row, rows):
    return jnp.where(tile % 2 == 0, row, rows - 1 - row)


def put_flat(ref, value):
    for piece in range(ref.shape[0]):
        ref[piece, : value.shape[0], :] = value[:, piece * 128 : (piece + 1) * 128]


def strided(ref, start, count, stride):
    pieces = [ref[piece, pl.ds(start, count, stride=stride), :] for piece in range(ref.shape[0])]
    return jnp.concatenate(pieces, axis=1)


def put_row(ref, row, rows, value):
    for piece in range(ref.shape[0]):
        part = value[:, piece * 128 : (piece + 1) * 128]
        ref[piece, pl.ds(row, value.shape[0], stride=rows), :] = part


def sweep_counts(steps_ref, tile, tiles):
    even = tile % 2 == 0
    near = jnp.where(even, tile + 1, tile - 1)
    far = jnp.where(even, tile - 1, tile + 1)

    def count(index):
        inside = (index >= 0) & (index < tiles)
        return jnp.where(inside, steps_ref[jnp.clip(index, 0, tiles - 1)], 0)

    return count(tile), count(near), count(far)


def coefficient(sweep, count):
    return jnp.where(sweep < count, F32(RATE), F32(0.0))


def build_vertical(bands_ref, pad_ref, levels):
    pad_ref[...] = jnp.ones(pad_ref.shape, F32)
    pad_ref[0:1, 0:levels] = bands_ref[...].astype(F32)
    across = jnp.broadcast_to(pad_ref[0:1, :], (128, 128))
    down = across.T
    i = lax.broadcasted_iota(jnp.int32, (128, 128), 0)
    j = lax.broadcasted_iota(jnp.int32, (128, 128), 1)
    apart = (i - j).astype(F32)
    weight = jnp.exp(-(apart * apart) / (down * across))
    keep = (jnp.abs(apart) <= jnp.minimum(down, across)) & (i < levels) & (j < levels)
    full = jnp.where(keep, weight, F32(0.0))[: up_to(levels, 8)]
    high = full.astype(jnp.bfloat16).astype(F32)
    blank = jnp.zeros(full.shape, F32)
    deep = up_to(levels, 16)
    high, low = jnp.concatenate([high, blank], axis=1), jnp.concatenate([full - high, blank], axis=1)
    stacked = high + pltpu.roll(high, deep, 1) + pltpu.roll(low, 2 * deep, 1)
    return stacked.astype(jnp.bfloat16)


def apply_vertical(vertical, field):
    high = field.astype(jnp.bfloat16)
    low = (field - high.astype(F32)).astype(jnp.bfloat16)
    blank = jnp.zeros((vertical.shape[1] - 3 * field.shape[0], field.shape[1]), jnp.bfloat16)
    stacked = jnp.concatenate([high, low, high, blank], axis=0)
    return jnp.dot(vertical, stacked, preferred_element_type=F32)


def sine_matrix(width):
    mode = np.arange(1, width + 1)
    full = np.sqrt(2.0 / (width + 1)) * np.sin(np.pi * np.outer(mode, mode) / (width + 1))
    high = full.astype(ml_dtypes.bfloat16)
    low = (full - high.astype(np.float64)).astype(ml_dtypes.bfloat16)
    waves = np.broadcast_to(2.0 * np.cos(np.pi * mode / (width + 1)), (8, width)).astype(np.float32)
    return jnp.asarray(high), jnp.asarray(low), jnp.asarray(waves)


def transform(field, s_high, s_low):
    high = field.astype(jnp.bfloat16)
    low = (field - high.astype(F32)).astype(jnp.bfloat16)
    dot = functools.partial(jnp.dot, preferred_element_type=F32)
    return dot(high, s_high) + dot(low, s_high) + dot(high, s_low)


def advance(field, rates, bases):
    new = {}
    for p, rate in rates.items():
        near = [field[p + d] for d in (-1, 1) if p + d in field]
        value = None
        if near:
            value = rate * (near[0] + near[1] if len(near) == 2 else near[0])
        if p in field:
            here = bases[p] * field[p]
            value = here if value is None else here + value
        if value is not None:
            new[p] = value
    return new


def base_of(rate, waves):
    return (1.0 - 4.0 * rate) + rate * waves


def product_kernel(rows, levels, members_hbm, inc_hbm, out_ref, mem_ref, inc_ref, prod_ref, sems):
    even = lax.axis_index("tile") % 2 == 0
    start = pl.multiple_of(jnp.where(even, rows - 8, 0), 8)
    owned, width = members_hbm.shape[0], inc_ref.shape[-1]
    pairs = [(inc_hbm.at[:, pl.ds(start, 8), :], inc_ref)]
    pairs += [(members_hbm.at[m, :, pl.ds(start, 8), :], mem_ref.at[m]) for m in range(owned)]
    copies = [pltpu.make_async_copy(source, target, sems.at[k]) for k, (source, target) in enumerate(pairs)]
    for copy in copies:
        copy.start()
    copies[0].wait()
    for m in range(owned):
        copies[1 + m].wait()
        put_flat(prod_ref, (mem_ref[m].astype(F32) * inc_ref[...]).reshape(levels * 8, width))
        for q in range(DIFF):
            put_row(out_ref.at[m], q, DIFF, strided(prod_ref, jnp.where(even, 7 - q, q), levels, 8))


def half_span(levels):
    return up_to(-(-levels // 2), 2)


def core():
    return lax.axis_index("mem") % 2


def put_parts(ref, own_ref, other_ref, levels):
    size = half_span(levels)
    for part, target in ((core(), own_ref), (1 - core(), other_ref)):
        low = pl.multiple_of(part * (levels - size) * DIFF, 8)
        target[...] = ref[:, :, pl.ds(low, size * DIFF), :]


def edge_kernel(
    rows, levels,
    bands_ref, members_ref, inc_ref, s_high_ref, s_low_ref,
    far_own_ref, far_other_ref, prod_ref, pad_ref, wave_ref,
):
    tile = lax.axis_index("tile")
    deep, tall = up_to(levels, 16), up_to(levels, 8)
    total = rows * levels
    vertical = build_vertical(bands_ref, pad_ref, levels)
    for piece in range(prod_ref.shape[0]):
        prod_ref[piece, total:, :] = jnp.zeros((prod_ref.shape[1] - total, 128), F32)
    for m in range(members_ref.shape[0]):
        put_flat(prod_ref, members_ref[m].astype(F32) * inc_ref[...])
        local = [
            apply_vertical(vertical, strided(prod_ref, grid_row(tile, q, rows), deep, rows)) for q in range(DIFF)
        ]
        waves = transform(jnp.concatenate(local, axis=0), s_high_ref[...], s_low_ref[...])
        for q in range(DIFF):
            put_row(wave_ref.at[m], q, DIFF, waves[q * tall : q * tall + levels])
    put_parts(wave_ref, far_own_ref, far_other_ref, levels)


def turn_kernel(
    rows, levels,
    inc_ref, prev_ref, members_ref, inc_t_ref, prev_t_ref, mem_own_ref, mem_other_ref, flat_ref, pack_ref,
):
    tile = lax.axis_index("tile")
    for piece in range(flat_ref.shape[0]):
        flat_ref[piece, rows * levels :, :] = jnp.zeros((flat_ref.shape[1] - rows * levels, 128), F32)
    for m in range(members_ref.shape[0]):
        put_flat(flat_ref, members_ref[m].astype(F32))
        for q in range(DIFF):
            put_row(pack_ref.at[m], q, DIFF, strided(flat_ref, grid_row(tile, q, rows), levels, rows))
    put_parts(pack_ref, mem_own_ref, mem_other_ref, levels)
    for source, target in ((inc_ref, inc_t_ref), (prev_ref, prev_t_ref)):
        put_flat(flat_ref, source[...])
        for row in range(rows):
            target[row] = strided(flat_ref, grid_row(tile, row, rows), target.shape[1], rows)


def own_kernel(
    rows, levels, tiles,
    bands_ref, steps_ref, members_ref, inc_ref, s_high_ref, s_low_ref, waves_ref,
    mine_ref, theirs_ref, cov_near_ref, cov_far_ref, cov_other_ref, mem_near_ref,
    prod_ref, memf_ref, spec_ref, acc_ref, base_ref, pad_ref,
):
    tile = lax.axis_index("tile")
    half = lax.axis_index("mem") % 2
    counts = sweep_counts(steps_ref, tile, tiles)
    vertical = build_vertical(bands_ref, pad_ref, levels)
    deep, tall = up_to(levels, 16), up_to(levels, 8)
    total = rows * levels
    width = inc_ref.shape[-1]
    for ref in (prod_ref, memf_ref):
        for piece in range(width // 128):
            ref[piece, total:, :] = jnp.zeros((ref.shape[1] - total, 128), F32)

    def row_of(ref, row, count):
        return strided(ref, grid_row(tile, row, rows), count, rows)

    rate = [[coefficient(k, count) for count in counts] for k in range(DIFF)]
    for k in range(DIFF):
        for side in range(3):
            base_ref[k, side] = base_of(rate[k][side], waves_ref[...])

    def side_of(p):
        return 2 if p < 0 else 1 if p >= rows else 0

    for m in range(members_ref.shape[0]):
        as_float = members_ref[m].astype(F32)
        put_flat(memf_ref, as_float)
        put_flat(prod_ref, transform(as_float * inc_ref[...], s_high_ref[...], s_low_ref[...]))
        for row in range(rows):
            spec_ref[row] = apply_vertical(vertical, row_of(prod_ref, row, deep))

        def chunk(index, _):
            at = pl.ds(pl.multiple_of(index * 8, 8), 8)
            field = {p: spec_ref[p, at, :] for p in range(rows)}
            for k in range(DIFF):
                out = min(k + 1, DIFF - 1 - k)
                kept = range(-out, rows + out)
                bases = {p: base_ref[k, side_of(p)] for p in kept}
                field = advance(field, {p: rate[k][side_of(p)] for p in kept}, bases)
            for p in range(rows):
                spec_ref[p, at, :] = field[p]
            return 0

        lax.fori_loop(0, tall // 8, chunk, 0)
        group = 4
        for first in range(0, rows, group):
            block = spec_ref[first : first + group].reshape(group * tall, width)
            block = transform(block, s_high_ref[...], s_low_ref[...])
            for k in range(group):
                row = first + k
                member = row_of(memf_ref, row, tall)
                if row >= rows - DIFF:
                    mem_near_ref[m, rows - 1 - row] = member
                value = member * block[k * tall : (k + 1) * tall]
                acc_ref[row] = value if m == 0 else acc_ref[row] + value
    part = (rows - 2 * DIFF) // 2
    size = half_span(levels)
    blank = jnp.zeros((cov_far_ref.shape[1] - size, width), F32)
    for q in range(DIFF):
        cov_near_ref[q] = acc_ref[rows - 1 - q]
        halves = (acc_ref[q, :size], acc_ref[q, levels - size : levels])
        for ref, first in ((cov_far_ref, half == 0), (cov_other_ref, half == 1)):
            ref[q, :size] = jnp.where(first, halves[0], halves[1])
            ref[q, size:] = blank
    for q in range(part):
        mine_ref[q] = acc_ref[DIFF + half * part + q]
        theirs_ref[q] = acc_ref[DIFF + (1 - half) * part + q]


def settle(field, rates, base_ref, size):
    for k in range(DIFF):
        kept = range(-1 - k, DIFF - 1 - k)
        bases = {p: base_ref[k, 0 if p < 0 else 1][:size] for p in kept}
        field = advance(field, {p: rates[k][0 if p < 0 else 1] for p in kept}, bases)
    return [field[-1 - q] for q in range(DIFF)]


def side_rates(near, tiles, steps_ref, waves_ref, base_ref):
    counts = sweep_counts(steps_ref, lax.axis_index("tile"), tiles)
    rates = [[coefficient(k, counts[0]), coefficient(k, counts[1 if near else 2])] for k in range(DIFF)]
    for k in range(DIFF):
        for side in range(2):
            base_ref[k, side] = base_of(rates[k][side], waves_ref[...])
    return rates


def near_kernel(
    levels, tiles,
    bands_ref, steps_ref, halo_ref, mem_ref, cov_ref, s_high_ref, s_low_ref, waves_ref, mine_ref, theirs_ref,
    spec_ref, base_ref, halo_row_ref, pad_ref,
):
    rates = side_rates(True, tiles, steps_ref, waves_ref, base_ref)
    tall, width = spec_ref.shape[1:]
    vertical = build_vertical(bands_ref, pad_ref, levels)
    halo_row_ref[levels:, :] = jnp.zeros((halo_row_ref.shape[0] - levels, width), F32)
    sums = [cov_ref[q] for q in range(DIFF)]
    for m in range(halo_ref.shape[0]):
        local = []
        for q in range(DIFF):
            halo_row_ref[:levels, :] = strided(halo_ref.at[m], q, levels, DIFF)
            local.append(apply_vertical(vertical, halo_row_ref[...]))
        waves = transform(jnp.concatenate(local, axis=0), s_high_ref[...], s_low_ref[...])
        for q in range(DIFF):
            spec_ref[q] = waves[q * tall : (q + 1) * tall]
        for at in range(0, tall, 8):
            field = {q: spec_ref[q, at : at + 8, :] for q in range(DIFF)}
            for q, value in enumerate(settle(field, rates, base_ref, 8)):
                spec_ref[q, at : at + 8, :] = value
        block = spec_ref[...].reshape(DIFF * tall, width)
        block = transform(block, s_high_ref[...], s_low_ref[...])
        for q in range(DIFF):
            sums[q] = sums[q] + mem_ref[m, q] * block[q * tall : (q + 1) * tall]
    part = DIFF // 2
    for q in range(DIFF):

        @pl.when(core() == q // part)
        def _(q=q):
            mine_ref[q % part] = sums[q]

        @pl.when(core() != q // part)
        def _(q=q):
            theirs_ref[q % part] = sums[q]


def far_kernel(
    levels, tiles,
    steps_ref, halo_ref, mem_ref, mem_other_ref, cov_ref, cov_other_ref, s_high_ref, s_low_ref, waves_ref,
    out_ref, spec_ref, base_ref,
):
    rates = side_rates(False, tiles, steps_ref, waves_ref, base_ref)
    tall, width = spec_ref.shape[2:]
    size = half_span(levels)
    owned = mem_ref.shape[0]
    for m in range(2 * owned):
        for q in range(DIFF):
            spec_ref[m, q, size:, :] = jnp.zeros((tall - size, width), F32)
        for at in range(0, size, 8):
            count = min(8, size - at)
            field = {q: strided(halo_ref.at[m], q + DIFF * at, count, DIFF) for q in range(DIFF)}
            for q, value in enumerate(settle(field, rates, base_ref, count)):
                spec_ref[m, q, at : at + count, :] = value
    block = spec_ref[...].reshape(2 * owned * DIFF * tall, width)
    spec_ref[...] = transform(block, s_high_ref[...], s_low_ref[...]).reshape(spec_ref.shape)
    for q in range(DIFF):
        out_ref[q, size:] = jnp.zeros((tall - size, width), F32)
        for at in range(0, size, 8):
            span = slice(at, min(at + 8, size))
            total = cov_ref[q, span] + cov_other_ref[q, span]
            for m in range(2 * owned):
                member_ref = (mem_ref if m < owned else mem_other_ref).at[m % owned]
                total = total + strided(member_ref, q + DIFF * at, span.stop - at, DIFF) * spec_ref[m, q, span]
            out_ref[q, span] = total


def reduced(value):
    return jnp.sum(value, axis=(0, 1), keepdims=True)


def folded(value):
    return jnp.sum(value.reshape(value.shape[0] // 8, 8, value.shape[1]), axis=0)


def ratio(top, bottom):
    some = bottom != 0.0
    return jnp.where(some, top / jnp.where(some, bottom, F32(1.0)), F32(0.0))


def bulk_kernel(
    rows, levels, inverse,
    beta_ref, mine_ref, other_ref, near_mine_ref, near_other_ref, inc_ref, prev_ref,
    w_ref, sums_ref, keep_ref,
):
    beta = beta_ref[0]
    tile = lax.axis_index("tile")
    part = (rows - 2 * DIFF) // 2
    own_half = lax.axis_index("mem") % 2
    zero = jnp.zeros((8, inc_ref.shape[-1]), F32)

    def covariance(row):
        if row >= rows - DIFF:
            which, q = divmod(rows - 1 - row, DIFF // 2)
            return jnp.where(own_half == which, near_mine_ref[q], near_other_ref[q])
        which, q = divmod(row - DIFF, part)
        return jnp.where(own_half == which, mine_ref[q], other_ref[q])

    square, cross = zero, zero
    for row in range(DIFF, rows):
        inc = inc_ref[row]
        scaled = inverse * covariance(row)
        square = square + folded(inc * inc)
        cross = cross + folded(inc * scaled)
        value = scaled - beta * prev_ref[row]
        keep_ref[row - DIFF] = value
        put_row(w_ref, grid_row(tile, row, rows), rows, value[:levels])
    square, cross = reduced(square), reduced(cross)
    pivot = ratio(cross, square)
    mixed, rest = zero, zero
    for row in range(DIFF, rows):
        inc = inc_ref[row]
        apart = keep_ref[row - DIFF] - pivot * inc
        mixed = mixed + folded(apart * inc)
        rest = rest + folded(apart * apart)
    store_sums(sums_ref, square, cross, reduced(mixed), reduced(rest), pivot)


def store_sums(ref, *values):
    sub = lax.broadcasted_iota(jnp.int32, ref.shape, 0)
    out = jnp.zeros(ref.shape, F32)
    for index, value in enumerate(values):
        out = jnp.where(sub == index, value, out)
    ref[...] = out


def load_sums(ref):
    return [ref[index : index + 1, :] for index in range(5)]


def last_kernel(inverse, levels, beta_ref, sums_ref, *refs):
    mine_refs, other_refs, (inc_ref, prev_ref, w_ref, out_ref, cov_ref) = refs[:2], refs[2:4], refs[4:]
    beta = beta_ref[0]
    square0, cross0, mixed0, rest0, pivot0 = [value[:, 0:1] for value in load_sums(sums_ref)]
    zero = jnp.zeros((8, inc_ref.shape[-1]), F32)
    square, cross, mixed, rest = zero, zero, zero, zero
    size = half_span(levels)
    for q in range(DIFF):
        mine, other = (first[q, :size] + second[q, :size] for first, second in (mine_refs, other_refs))
        cov_ref[levels:, :] = jnp.zeros((cov_ref.shape[0] - levels, cov_ref.shape[1]), F32)
        cov_ref[levels - size : levels, :] = jnp.where(core() == 1, mine, other)
        cov_ref[:size, :] = jnp.where(core() == 0, mine, other)
        inc = inc_ref[q]
        scaled = inverse * cov_ref[...]
        value = scaled - beta * prev_ref[q]
        w_ref[q] = value
        apart = value - pivot0 * inc
        square = square + folded(inc * inc)
        cross = cross + folded(inc * scaled)
        mixed = mixed + folded(apart * inc)
        rest = rest + folded(apart * apart)
    store_sums(
        out_ref,
        square0 + reduced(square), cross0 + reduced(cross), mixed0 + reduced(mixed), rest0 + reduced(rest), pivot0,
    )


def merged(parts):
    square = sum(part[0] for part in parts)
    cross = sum(part[1] for part in parts)
    pivot = ratio(cross, square)
    mixed, rest = F32(0.0), F32(0.0)
    for part in parts:
        shift = part[4] - pivot
        mixed = mixed + part[2] + shift * part[0]
        rest = rest + part[3] + 2.0 * shift * part[2] + shift * shift * part[0]
    return square, cross, mixed, rest, pivot


def merge_kernel(*refs):
    store_sums(refs[-1], *merged([load_sums(ref) for ref in refs[:-1]]))


def final_kernel(rows, levels, cells, count, *refs):
    sums_refs = refs[:count]
    w_far_ref, w_ref, inc_t_ref, inc_ref, out_hbm, coef_ref, out_ref, sems = refs[count:]
    tile = lax.axis_index("tile")
    _, _, _, rest, pivot = merged([load_sums(ref) for ref in sums_refs])
    scale = jnp.sqrt(rest / cells + 1e-6)
    lane = lax.broadcasted_iota(jnp.int32, scale.shape, 1)
    coef_ref[...] = jnp.where(lane == 0, 1.0 + pivot, scale)[:, :2]
    over = 1.0 / scale
    wide_pivot, wide_over = (jnp.concatenate([value] * w_ref.shape[0], axis=1) for value in (pivot, over))
    step = up_to(up_to(levels, 8) // 4, 8)
    copies = []
    for low in range(0, levels, step):
        high = min(levels, low + step)
        span = slice(low * rows, high * rows)
        for piece in range(w_ref.shape[0]):
            lanes = slice(piece * 128, (piece + 1) * 128)
            out_ref[piece, span, :] = (w_ref[piece, span, :] - pivot * inc_ref[span, lanes]) * over
        for q in range(DIFF):
            value = (w_far_ref[q, low:high] - wide_pivot * inc_t_ref[q, low:high]) * wide_over
            put_row(out_ref, grid_row(tile, q, rows) + low * rows, rows, value)
        for piece in range(w_ref.shape[0]):
            lanes = slice(piece * 128, (piece + 1) * 128)
            source, target = out_ref.at[piece, span, :], out_hbm.at[span, lanes]
            copies.append(pltpu.make_async_copy(source, target, sems.at[len(copies)]))
            copies[-1].start()
    for copy in copies:
        copy.wait()


def call(kernel, ins, outs, scratch=(), cost=None, limit=VMEM_LIMIT):
    spaces = {"s": pltpu.SMEM, "v": pltpu.VMEM, "h": pltpu.HBM}
    outs = [out if isinstance(out[0], str) else ("v", out) for out in outs]
    estimate = None
    if cost is not None:
        estimate = pl.CostEstimate(flops=cost[0], bytes_accessed=cost[1], transcendentals=0)
    return pl.pallas_call(
        kernel,
        out_shape=tuple(jax.ShapeDtypeStruct(shape, F32) for _, shape in outs),
        in_specs=[pl.BlockSpec(memory_space=spaces[kind]) for kind, _ in ins],
        out_specs=tuple(pl.BlockSpec(memory_space=spaces[kind]) for kind, _ in outs),
        scratch_shapes=scratch,
        compiler_params=pltpu.CompilerParams(vmem_limit_bytes=limit),
        cost_estimate=estimate,
    )(*(value for _, value in ins))


def flipped(axis, bit):
    count = lax.axis_size(axis)
    return [(i, i ^ bit) for i in range(count)]


def rotated(axis, digit, radix, by):
    count = lax.axis_size(axis)

    def target(i):
        value = i // digit % radix
        other = value ^ by if radix & (radix - 1) == 0 else (value + by) % radix
        return i + (other - value) * digit

    return [(i, target(i)) for i in range(count)]


def partners(radix):
    return [2, 3, 1] if radix == 4 else range(radix - 1, 0, -1)


def radices(count):
    out = [] if count % 2 else [2]
    rest = count // 2 if out else count
    factor = 4
    while rest > 1:
        while factor > 1 and rest % factor:
            factor -= 1
        if factor == 1:
            factor = rest
        out.append(factor)
        rest //= factor
        factor = min(factor, 4)
    return out


def per_device(increment, previous, beta_prev, members, band_widths, diffusion_steps):
    levels, rows, width = increment.shape
    tiles, mems = lax.axis_size("tile"), lax.axis_size("mem")
    owned = members.shape[0]
    tall, deep = up_to(levels, 8), up_to(levels, 16)
    inverse = 1.0 / (owned * mems - 1)
    cells = levels * rows * tiles * width
    lanes = width // 128
    inc = increment.reshape(levels * rows, width)
    prev = previous.reshape(levels * rows, width)
    bands = band_widths.reshape(1, levels)
    s_high, s_low, waves = sine_matrix(width)
    edge = (owned, DIFF, tall, width)
    part = (rows - 2 * DIFF) // 2
    near_pairs = [(i, i ^ 1) for i in range(tiles) if i ^ 1 < tiles]
    far_pairs = [pair for i in range(1, tiles - 1, 2) for pair in ((i, i + 1), (i + 1, i))]
    pad = pltpu.VMEM((8, 128), F32)

    packed = (owned, lanes, DIFF * levels, 128)
    (near_edge,) = call(
        functools.partial(product_kernel, rows, levels),
        [("h", members), ("h", increment)],
        [packed],
        [
            pltpu.VMEM((owned, levels, 8, width), jnp.bfloat16),
            pltpu.VMEM((levels, 8, width), F32),
            pltpu.VMEM((lanes, levels * 8, 128), F32),
            pltpu.SemaphoreType.DMA((owned + 1,)),
        ],
        limit=EDGE_LIMIT,
    )
    mem = members.reshape(owned, levels * rows, width)
    bands, near_edge = lax.optimization_barrier((bands, near_edge))
    near_halo = lax.ppermute(near_edge, "tile", near_pairs)
    size = half_span(levels)
    half_packed = (owned, lanes, DIFF * size, 128)
    pair = flipped("mem", 1)
    far_edge, far_edge_other = call(
        functools.partial(edge_kernel, rows, levels),
        [("v", bands), ("v", mem), ("v", inc), ("v", s_high), ("v", s_low)],
        [half_packed] * 2,
        [pltpu.VMEM((lanes, deep * rows, 128), F32), pad, pltpu.VMEM(packed, F32)],
    )
    far_edge_other = lax.ppermute(far_edge_other, "mem", pair)
    members, far_edge = lax.optimization_barrier((members, far_edge))
    mem = members.reshape(owned, levels * rows, width)

    piece, four = (part, tall, width), (DIFF, tall, width)
    short = (DIFF, up_to(size, 8), width)
    mine, theirs, cov_near, cov_far, cov_far_other, mem_near = call(
        functools.partial(own_kernel, rows, levels, tiles),
        [("v", bands), ("s", diffusion_steps), ("v", mem), ("v", inc)]
        + [("v", s_high), ("v", s_low), ("v", waves)],
        [piece, piece, four, short, short, edge],
        [pltpu.VMEM((lanes, deep * rows, 128), F32)] * 2
        + [pltpu.VMEM((rows, tall, width), F32)] * 2
        + [pltpu.VMEM((DIFF, 3, 8, width), F32), pad],
        (20_000_000, 1_000_000),
    )
    prev, _ = lax.optimization_barrier((prev, theirs))
    inc_t, prev_t, mem_far, mem_far_other = call(
        functools.partial(turn_kernel, rows, levels),
        [("v", inc), ("v", prev), ("v", mem)],
        [(rows, tall, width)] * 2 + [half_packed] * 2,
        [pltpu.VMEM((lanes, tall * rows, 128), F32), pltpu.VMEM(packed, F32)],
    )
    mem_far_other = lax.ppermute(mem_far_other, "mem", pair)
    theirs, far_edge_other = lax.optimization_barrier((theirs, far_edge_other))
    far_edge = jnp.concatenate([far_edge, far_edge_other])
    far_halo = lax.ppermute(far_edge, "tile", far_pairs)
    bits = [1 << k for k in range(1, mems.bit_length() - 1)]
    mine = mine + lax.ppermute(theirs, "mem", flipped("mem", 1))
    for bit in bits:
        mine = mine + lax.ppermute(mine, "mem", flipped("mem", bit))
    other = lax.ppermute(mine, "mem", flipped("mem", 1))

    cov_far_other = lax.ppermute(cov_far_other, "mem", pair)
    two = (DIFF // 2, tall, width)
    near_mine, near_theirs = call(
        functools.partial(near_kernel, levels, tiles),
        [("v", bands), ("s", diffusion_steps), ("v", near_halo), ("v", mem_near), ("v", cov_near)]
        + [("v", s_high), ("v", s_low), ("v", waves)],
        [two, two],
        [pltpu.VMEM(four, F32), pltpu.VMEM((DIFF, 2, 8, width), F32), pltpu.VMEM((deep, width), F32), pad],
    )
    near_mine = near_mine + lax.ppermute(near_theirs, "mem", flipped("mem", 1))
    for bit in bits:
        near_mine = near_mine + lax.ppermute(near_mine, "mem", flipped("mem", bit))
    near_other = lax.ppermute(near_mine, "mem", flipped("mem", 1))
    cov_far, near_other, inc_t = lax.optimization_barrier((cov_far, near_other, inc_t))
    w_rest, sums = call(
        functools.partial(bulk_kernel, rows, levels, inverse),
        [("s", beta_prev), ("v", mine), ("v", other), ("v", near_mine), ("v", near_other)]
        + [("v", inc_t), ("v", prev_t)],
        [(lanes, levels * rows, 128), (8, 128)],
        [pltpu.VMEM((rows - DIFF, tall, width), F32)],
    )
    (cov,) = call(
        functools.partial(far_kernel, levels, tiles),
        [("s", diffusion_steps), ("v", far_halo), ("v", mem_far), ("v", mem_far_other)]
        + [("v", cov_far), ("v", cov_far_other), ("v", s_high), ("v", s_low), ("v", waves)],
        [short],
        [pltpu.VMEM((2 * owned, *short), F32), pltpu.VMEM((DIFF, 2, 8, width), F32)],
    )
    for bit in bits[:-1]:
        cov = cov + lax.ppermute(cov, "mem", flipped("mem", bit))
    far_sums = [cov, lax.ppermute(cov, "mem", flipped("mem", bits[-1]))]
    far_others = [lax.ppermute(value, "mem", pair) for value in far_sums]
    w_far, sums = call(
        functools.partial(last_kernel, inverse, levels),
        [("s", beta_prev), ("v", sums)]
        + [("v", value) for value in far_sums + far_others + [inc_t, prev_t]],
        [four, (8, 128)],
        [pltpu.VMEM((tall, width), F32)],
    )
    digit = 1
    stages = radices(tiles)
    for index, radix in enumerate(stages):
        parts = [sums] + [lax.ppermute(sums, "tile", rotated("tile", digit, radix, by)) for by in partners(radix)]
        if index < len(stages) - 1:
            (sums,) = call(merge_kernel, [("v", value) for value in parts], [(8, 128)])
        digit *= radix
    out, coefficients = call(
        functools.partial(final_kernel, rows, levels, cells, len(parts)),
        [("v", value) for value in parts] + [("v", w_far), ("v", w_rest), ("v", inc_t), ("v", inc)],
        [("h", (levels * rows, width)), (1, 2)],
        [pltpu.VMEM((lanes, levels * rows, 128), F32), pltpu.SemaphoreType.DMA((4 * lanes,))],
    )
    return out.reshape(levels, rows, width), coefficients.reshape(2)


def solution(mesh):
    in_specs = (
        P(None, "tile", None),
        P(None, "tile", None),
        P(),
        P("mem", None, "tile", None),
        P(),
        P(),
    )
    out_specs = (P(None, "tile", None), P())
    return jax.shard_map(
        per_device, mesh=mesh, in_specs=in_specs, out_specs=out_specs, check_vma=False
    )
```

```python
import functools

import jax
import jax.numpy as jnp
import ml_dtypes
import numpy as np
from jax import lax
from jax.experimental import pallas as pl
from jax.experimental.pallas import tpu as pltpu
from jax.sharding import PartitionSpec as P

DIFF = 4
RATE = 0.24
F32 = jnp.float32
VMEM_LIMIT = 32 * 1024 * 1024
EDGE_LIMIT = 53 * 1024 * 1024


def up_to(value, unit):
    return -(-value // unit) * unit


def grid_row(tile, row, rows):
    return jnp.where(tile % 2 == 0, row, rows - 1 - row)


def put_flat(ref, value):
    for piece in range(ref.shape[0]):
        ref[piece, : value.shape[0], :] = value[:, piece * 128 : (piece + 1) * 128]


def strided(ref, start, count, stride):
    pieces = [ref[piece, pl.ds(start, count, stride=stride), :] for piece in range(ref.shape[0])]
    return jnp.concatenate(pieces, axis=1)


def put_row(ref, row, rows, value):
    for piece in range(ref.shape[0]):
        part = value[:, piece * 128 : (piece + 1) * 128]
        ref[piece, pl.ds(row, value.shape[0], stride=rows), :] = part


def sweep_counts(steps_ref, tile, tiles):
    even = tile % 2 == 0
    near = jnp.where(even, tile + 1, tile - 1)
    far = jnp.where(even, tile - 1, tile + 1)

    def count(index):
        inside = (index >= 0) & (index < tiles)
        return jnp.where(inside, steps_ref[jnp.clip(index, 0, tiles - 1)], 0)

    return count(tile), count(near), count(far)


def coefficient(sweep, count):
    return jnp.where(sweep < count, F32(RATE), F32(0.0))


def build_vertical(bands_ref, pad_ref, levels):
    pad_ref[...] = jnp.ones(pad_ref.shape, F32)
    pad_ref[0:1, 0:levels] = bands_ref[...].astype(F32)
    across = jnp.broadcast_to(pad_ref[0:1, :], (128, 128))
    down = across.T
    i = lax.broadcasted_iota(jnp.int32, (128, 128), 0)
    j = lax.broadcasted_iota(jnp.int32, (128, 128), 1)
    apart = (i - j).astype(F32)
    weight = jnp.exp(-(apart * apart) / (down * across))
    keep = (jnp.abs(apart) <= jnp.minimum(down, across)) & (i < levels) & (j < levels)
    full = jnp.where(keep, weight, F32(0.0))[: up_to(levels, 8)]
    high = full.astype(jnp.bfloat16).astype(F32)
    blank = jnp.zeros(full.shape, F32)
    deep = up_to(levels, 16)
    high, low = jnp.concatenate([high, blank], axis=1), jnp.concatenate([full - high, blank], axis=1)
    stacked = high + pltpu.roll(high, deep, 1) + pltpu.roll(low, 2 * deep, 1)
    return stacked.astype(jnp.bfloat16)


def apply_vertical(vertical, field):
    high = field.astype(jnp.bfloat16)
    low = (field - high.astype(F32)).astype(jnp.bfloat16)
    blank = jnp.zeros((vertical.shape[1] - 3 * field.shape[0], field.shape[1]), jnp.bfloat16)
    stacked = jnp.concatenate([high, low, high, blank], axis=0)
    return jnp.dot(vertical, stacked, preferred_element_type=F32)


def sine_matrix(width):
    mode = np.arange(1, width + 1)
    full = np.sqrt(2.0 / (width + 1)) * np.sin(np.pi * np.outer(mode, mode) / (width + 1))
    high = full.astype(ml_dtypes.bfloat16)
    low = (full - high.astype(np.float64)).astype(ml_dtypes.bfloat16)
    waves = np.broadcast_to(2.0 * np.cos(np.pi * mode / (width + 1)), (8, width)).astype(np.float32)
    return jnp.asarray(high), jnp.asarray(low), jnp.asarray(waves)


def transform(field, s_high, s_low):
    high = field.astype(jnp.bfloat16)
    low = (field - high.astype(F32)).astype(jnp.bfloat16)
    dot = functools.partial(jnp.dot, preferred_element_type=F32)
    return dot(high, s_high) + dot(low, s_high) + dot(high, s_low)


def advance(field, rates, bases):
    new = {}
    for p, rate in rates.items():
        near = [field[p + d] for d in (-1, 1) if p + d in field]
        value = None
        if near:
            value = rate * (near[0] + near[1] if len(near) == 2 else near[0])
        if p in field:
            here = bases[p] * field[p]
            value = here if value is None else here + value
        if value is not None:
            new[p] = value
    return new


def base_of(rate, waves):
    return (1.0 - 4.0 * rate) + rate * waves


def product_kernel(rows, levels, members_hbm, inc_hbm, out_ref, mem_ref, inc_ref, prod_ref, sems):
    even = lax.axis_index("tile") % 2 == 0
    start = pl.multiple_of(jnp.where(even, rows - 8, 0), 8)
    owned, width = members_hbm.shape[0], inc_ref.shape[-1]
    pairs = [(inc_hbm.at[:, pl.ds(start, 8), :], inc_ref)]
    pairs += [(members_hbm.at[m, :, pl.ds(start, 8), :], mem_ref.at[m]) for m in range(owned)]
    copies = [pltpu.make_async_copy(source, target, sems.at[k]) for k, (source, target) in enumerate(pairs)]
    for copy in copies:
        copy.start()
    copies[0].wait()
    for m in range(owned):
        copies[1 + m].wait()
        put_flat(prod_ref, (mem_ref[m].astype(F32) * inc_ref[...]).reshape(levels * 8, width))
        for q in range(DIFF):
            put_row(out_ref.at[m], q, DIFF, strided(prod_ref, jnp.where(even, 7 - q, q), levels, 8))


def half_span(levels):
    return up_to(-(-levels // 2), 2)


def core():
    return lax.axis_index("mem") % 2


def put_parts(ref, own_ref, other_ref, levels):
    size = half_span(levels)
    for part, target in ((core(), own_ref), (1 - core(), other_ref)):
        low = pl.multiple_of(part * (levels - size) * DIFF, 8)
        target[...] = ref[:, :, pl.ds(low, size * DIFF), :]


def edge_kernel(
    rows, levels,
    bands_ref, members_ref, inc_ref, s_high_ref, s_low_ref,
    far_own_ref, far_other_ref, prod_ref, pad_ref, wave_ref,
):
    tile = lax.axis_index("tile")
    deep, tall = up_to(levels, 16), up_to(levels, 8)
    total = rows * levels
    vertical = build_vertical(bands_ref, pad_ref, levels)
    for piece in range(prod_ref.shape[0]):
        prod_ref[piece, total:, :] = jnp.zeros((prod_ref.shape[1] - total, 128), F32)
    for m in range(members_ref.shape[0]):
        put_flat(prod_ref, members_ref[m].astype(F32) * inc_ref[...])
        local = [
            apply_vertical(vertical, strided(prod_ref, grid_row(tile, q, rows), deep, rows)) for q in range(DIFF)
        ]
        waves = transform(jnp.concatenate(local, axis=0), s_high_ref[...], s_low_ref[...])
        for q in range(DIFF):
            put_row(wave_ref.at[m], q, DIFF, waves[q * tall : q * tall + levels])
    put_parts(wave_ref, far_own_ref, far_other_ref, levels)


def turn_kernel(
    rows, levels,
    inc_ref, prev_ref, members_ref, inc_t_ref, prev_t_ref, mem_own_ref, mem_other_ref, flat_ref, pack_ref,
):
    tile = lax.axis_index("tile")
    for piece in range(flat_ref.shape[0]):
        flat_ref[piece, rows * levels :, :] = jnp.zeros((flat_ref.shape[1] - rows * levels, 128), F32)
    for m in range(members_ref.shape[0]):
        put_flat(flat_ref, members_ref[m].astype(F32))
        for q in range(DIFF):
            put_row(pack_ref.at[m], q, DIFF, strided(flat_ref, grid_row(tile, q, rows), levels, rows))
    put_parts(pack_ref, mem_own_ref, mem_other_ref, levels)
    for source, target in ((inc_ref, inc_t_ref), (prev_ref, prev_t_ref)):
        put_flat(flat_ref, source[...])
        for row in range(rows):
            target[row] = strided(flat_ref, grid_row(tile, row, rows), target.shape[1], rows)


def own_kernel(
    rows, levels, tiles,
    bands_ref, steps_ref, members_ref, inc_ref, s_high_ref, s_low_ref, waves_ref,
    mine_ref, theirs_ref, cov_near_ref, cov_far_ref, cov_other_ref, mem_near_ref,
    prod_ref, memf_ref, spec_ref, acc_ref, base_ref, pad_ref,
):
    tile = lax.axis_index("tile")
    half = lax.axis_index("mem") % 2
    counts = sweep_counts(steps_ref, tile, tiles)
    vertical = build_vertical(bands_ref, pad_ref, levels)
    deep, tall = up_to(levels, 16), up_to(levels, 8)
    total = rows * levels
    width = inc_ref.shape[-1]
    for ref in (prod_ref, memf_ref):
        for piece in range(width // 128):
            ref[piece, total:, :] = jnp.zeros((ref.shape[1] - total, 128), F32)

    def row_of(ref, row, count):
        return strided(ref, grid_row(tile, row, rows), count, rows)

    rate = [[coefficient(k, count) for count in counts] for k in range(DIFF)]
    for k in range(DIFF):
        for side in range(3):
            base_ref[k, side] = base_of(rate[k][side], waves_ref[...])

    def side_of(p):
        return 2 if p < 0 else 1 if p >= rows else 0

    for m in range(members_ref.shape[0]):
        as_float = members_ref[m].astype(F32)
        put_flat(memf_ref, as_float)
        put_flat(prod_ref, transform(as_float * inc_ref[...], s_high_ref[...], s_low_ref[...]))
        for row in range(rows):
            spec_ref[row] = apply_vertical(vertical, row_of(prod_ref, row, deep))

        def chunk(index, _):
            at = pl.ds(pl.multiple_of(index * 8, 8), 8)
            field = {p: spec_ref[p, at, :] for p in range(rows)}
            for k in range(DIFF):
                out = min(k + 1, DIFF - 1 - k)
                kept = range(-out, rows + out)
                bases = {p: base_ref[k, side_of(p)] for p in kept}
                field = advance(field, {p: rate[k][side_of(p)] for p in kept}, bases)
            for p in range(rows):
                spec_ref[p, at, :] = field[p]
            return 0

        lax.fori_loop(0, tall // 8, chunk, 0)
        group = 4
        for first in range(0, rows, group):
            block = spec_ref[first : first + group].reshape(group * tall, width)
            block = transform(block, s_high_ref[...], s_low_ref[...])
            for k in range(group):
                row = first + k
                member = row_of(memf_ref, row, tall)
                if row >= rows - DIFF:
                    mem_near_ref[m, rows - 1 - row] = member
                value = member * block[k * tall : (k + 1) * tall]
                acc_ref[row] = value if m == 0 else acc_ref[row] + value
    part = (rows - 2 * DIFF) // 2
    size = half_span(levels)
    blank = jnp.zeros((cov_far_ref.shape[1] - size, width), F32)
    for q in range(DIFF):
        cov_near_ref[q] = acc_ref[rows - 1 - q]
        halves = (acc_ref[q, :size], acc_ref[q, levels - size : levels])
        for ref, first in ((cov_far_ref, half == 0), (cov_other_ref, half == 1)):
            ref[q, :size] = jnp.where(first, halves[0], halves[1])
            ref[q, size:] = blank
    for q in range(part):
        mine_ref[q] = acc_ref[DIFF + half * part + q]
        theirs_ref[q] = acc_ref[DIFF + (1 - half) * part + q]


def settle(field, rates, base_ref, size):
    for k in range(DIFF):
        kept = range(-1 - k, DIFF - 1 - k)
        bases = {p: base_ref[k, 0 if p < 0 else 1][:size] for p in kept}
        field = advance(field, {p: rates[k][0 if p < 0 else 1] for p in kept}, bases)
    return [field[-1 - q] for q in range(DIFF)]


def side_rates(near, tiles, steps_ref, waves_ref, base_ref):
    counts = sweep_counts(steps_ref, lax.axis_index("tile"), tiles)
    rates = [[coefficient(k, counts[0]), coefficient(k, counts[1 if near else 2])] for k in range(DIFF)]
    for k in range(DIFF):
        for side in range(2):
            base_ref[k, side] = base_of(rates[k][side], waves_ref[...])
    return rates


def near_kernel(
    levels, tiles,
    bands_ref, steps_ref, halo_ref, mem_ref, cov_ref, s_high_ref, s_low_ref, waves_ref, mine_ref, theirs_ref,
    spec_ref, base_ref, halo_row_ref, pad_ref,
):
    rates = side_rates(True, tiles, steps_ref, waves_ref, base_ref)
    tall, width = spec_ref.shape[1:]
    vertical = build_vertical(bands_ref, pad_ref, levels)
    halo_row_ref[levels:, :] = jnp.zeros((halo_row_ref.shape[0] - levels, width), F32)
    sums = [cov_ref[q] for q in range(DIFF)]
    for m in range(halo_ref.shape[0]):
        local = []
        for q in range(DIFF):
            halo_row_ref[:levels, :] = strided(halo_ref.at[m], q, levels, DIFF)
            local.append(apply_vertical(vertical, halo_row_ref[...]))
        waves = transform(jnp.concatenate(local, axis=0), s_high_ref[...], s_low_ref[...])
        for q in range(DIFF):
            spec_ref[q] = waves[q * tall : (q + 1) * tall]
        for at in range(0, tall, 8):
            field = {q: spec_ref[q, at : at + 8, :] for q in range(DIFF)}
            for q, value in enumerate(settle(field, rates, base_ref, 8)):
                spec_ref[q, at : at + 8, :] = value
        block = spec_ref[...].reshape(DIFF * tall, width)
        block = transform(block, s_high_ref[...], s_low_ref[...])
        for q in range(DIFF):
            sums[q] = sums[q] + mem_ref[m, q] * block[q * tall : (q + 1) * tall]
    part = DIFF // 2
    for q in range(DIFF):

        @pl.when(core() == q // part)
        def _(q=q):
            mine_ref[q % part] = sums[q]

        @pl.when(core() != q // part)
        def _(q=q):
            theirs_ref[q % part] = sums[q]


def far_kernel(
    levels, tiles,
    steps_ref, halo_ref, mem_ref, mem_other_ref, cov_ref, cov_other_ref, s_high_ref, s_low_ref, waves_ref,
    out_ref, spec_ref, base_ref,
):
    rates = side_rates(False, tiles, steps_ref, waves_ref, base_ref)
    tall, width = spec_ref.shape[2:]
    size = half_span(levels)
    owned = mem_ref.shape[0]
    for m in range(2 * owned):
        for q in range(DIFF):
            spec_ref[m, q, size:, :] = jnp.zeros((tall - size, width), F32)
        for at in range(0, size, 8):
            count = min(8, size - at)
            field = {q: strided(halo_ref.at[m], q + DIFF * at, count, DIFF) for q in range(DIFF)}
            for q, value in enumerate(settle(field, rates, base_ref, count)):
                spec_ref[m, q, at : at + count, :] = value
    block = spec_ref[...].reshape(2 * owned * DIFF * tall, width)
    spec_ref[...] = transform(block, s_high_ref[...], s_low_ref[...]).reshape(spec_ref.shape)
    for q in range(DIFF):
        out_ref[q, size:] = jnp.zeros((tall - size, width), F32)
        for at in range(0, size, 8):
            span = slice(at, min(at + 8, size))
            total = cov_ref[q, span] + cov_other_ref[q, span]
            for m in range(2 * owned):
                member_ref = (mem_ref if m < owned else mem_other_ref).at[m % owned]
                total = total + strided(member_ref, q + DIFF * at, span.stop - at, DIFF) * spec_ref[m, q, span]
            out_ref[q, span] = total


def reduced(value):
    return jnp.sum(value, axis=(0, 1), keepdims=True)


def folded(value):
    return jnp.sum(value.reshape(value.shape[0] // 8, 8, value.shape[1]), axis=0)


def ratio(top, bottom):
    some = bottom != 0.0
    return jnp.where(some, top / jnp.where(some, bottom, F32(1.0)), F32(0.0))


def bulk_kernel(
    rows, levels, inverse,
    beta_ref, mine_ref, other_ref, near_mine_ref, near_other_ref, inc_ref, prev_ref,
    w_ref, sums_ref, keep_ref,
):
    beta = beta_ref[0]
    tile = lax.axis_index("tile")
    part = (rows - 2 * DIFF) // 2
    own_half = lax.axis_index("mem") % 2
    zero = jnp.zeros((8, inc_ref.shape[-1]), F32)

    def covariance(row):
        if row >= rows - DIFF:
            which, q = divmod(rows - 1 - row, DIFF // 2)
            return jnp.where(own_half == which, near_mine_ref[q], near_other_ref[q])
        which, q = divmod(row - DIFF, part)
        return jnp.where(own_half == which, mine_ref[q], other_ref[q])

    square, cross = zero, zero
    for row in range(DIFF, rows):
        inc = inc_ref[row]
        scaled = inverse * covariance(row)
        square = square + folded(inc * inc)
        cross = cross + folded(inc * scaled)
        value = scaled - beta * prev_ref[row]
        keep_ref[row - DIFF] = value
        put_row(w_ref, grid_row(tile, row, rows), rows, value[:levels])
    square, cross = reduced(square), reduced(cross)
    pivot = ratio(cross, square)
    mixed, rest = zero, zero
    for row in range(DIFF, rows):
        inc = inc_ref[row]
        apart = keep_ref[row - DIFF] - pivot * inc
        mixed = mixed + folded(apart * inc)
        rest = rest + folded(apart * apart)
    store_sums(sums_ref, square, cross, reduced(mixed), reduced(rest), pivot)


def store_sums(ref, *values):
    sub = lax.broadcasted_iota(jnp.int32, ref.shape, 0)
    out = jnp.zeros(ref.shape, F32)
    for index, value in enumerate(values):
        out = jnp.where(sub == index, value, out)
    ref[...] = out


def load_sums(ref):
    return [ref[index : index + 1, :] for index in range(5)]


def last_kernel(inverse, levels, beta_ref, sums_ref, *refs):
    mine_refs, other_refs, (inc_ref, prev_ref, w_ref, out_ref, cov_ref) = refs[:2], refs[2:4], refs[4:]
    beta = beta_ref[0]
    square0, cross0, mixed0, rest0, pivot0 = [value[:, 0:1] for value in load_sums(sums_ref)]
    zero = jnp.zeros((8, inc_ref.shape[-1]), F32)
    square, cross, mixed, rest = zero, zero, zero, zero
    size = half_span(levels)
    for q in range(DIFF):
        mine, other = (first[q, :size] + second[q, :size] for first, second in (mine_refs, other_refs))
        cov_ref[levels:, :] = jnp.zeros((cov_ref.shape[0] - levels, cov_ref.shape[1]), F32)
        cov_ref[levels - size : levels, :] = jnp.where(core() == 1, mine, other)
        cov_ref[:size, :] = jnp.where(core() == 0, mine, other)
        inc = inc_ref[q]
        scaled = inverse * cov_ref[...]
        value = scaled - beta * prev_ref[q]
        w_ref[q] = value
        apart = value - pivot0 * inc
        square = square + folded(inc * inc)
        cross = cross + folded(inc * scaled)
        mixed = mixed + folded(apart * inc)
        rest = rest + folded(apart * apart)
    store_sums(
        out_ref,
        square0 + reduced(square), cross0 + reduced(cross), mixed0 + reduced(mixed), rest0 + reduced(rest), pivot0,
    )


def merged(parts):
    square = sum(part[0] for part in parts)
    cross = sum(part[1] for part in parts)
    pivot = ratio(cross, square)
    mixed, rest = F32(0.0), F32(0.0)
    for part in parts:
        shift = part[4] - pivot
        mixed = mixed + part[2] + shift * part[0]
        rest = rest + part[3] + 2.0 * shift * part[2] + shift * shift * part[0]
    return square, cross, mixed, rest, pivot


def merge_kernel(*refs):
    store_sums(refs[-1], *merged([load_sums(ref) for ref in refs[:-1]]))


def final_kernel(rows, levels, cells, count, *refs):
    sums_refs = refs[:count]
    w_far_ref, w_ref, inc_t_ref, inc_ref, out_hbm, coef_ref, out_ref, sems = refs[count:]
    tile = lax.axis_index("tile")
    _, _, _, rest, pivot = merged([load_sums(ref) for ref in sums_refs])
    scale = jnp.sqrt(rest / cells + 1e-6)
    lane = lax.broadcasted_iota(jnp.int32, scale.shape, 1)
    coef_ref[...] = jnp.where(lane == 0, 1.0 + pivot, scale)[:, :2]
    over = 1.0 / scale
    wide_pivot, wide_over = (jnp.concatenate([value] * w_ref.shape[0], axis=1) for value in (pivot, over))
    step = up_to(up_to(levels, 8) // 4, 8)
    copies = []
    for low in range(0, levels, step):
        high = min(levels, low + step)
        span = slice(low * rows, high * rows)
        for piece in range(w_ref.shape[0]):
            lanes = slice(piece * 128, (piece + 1) * 128)
            out_ref[piece, span, :] = (w_ref[piece, span, :] - pivot * inc_ref[span, lanes]) * over
        for q in range(DIFF):
            value = (w_far_ref[q, low:high] - wide_pivot * inc_t_ref[q, low:high]) * wide_over
            put_row(out_ref, grid_row(tile, q, rows) + low * rows, rows, value)
        for piece in range(w_ref.shape[0]):
            lanes = slice(piece * 128, (piece + 1) * 128)
            source, target = out_ref.at[piece, span, :], out_hbm.at[span, lanes]
            copies.append(pltpu.make_async_copy(source, target, sems.at[len(copies)]))
            copies[-1].start()
    for copy in copies:
        copy.wait()


def call(kernel, ins, outs, scratch=(), cost=None, limit=VMEM_LIMIT):
    spaces = {"s": pltpu.SMEM, "v": pltpu.VMEM, "h": pltpu.HBM}
    outs = [out if isinstance(out[0], str) else ("v", out) for out in outs]
    estimate = None
    if cost is not None:
        estimate = pl.CostEstimate(flops=cost[0], bytes_accessed=cost[1], transcendentals=0)
    return pl.pallas_call(
        kernel,
        out_shape=tuple(jax.ShapeDtypeStruct(shape, F32) for _, shape in outs),
        in_specs=[pl.BlockSpec(memory_space=spaces[kind]) for kind, _ in ins],
        out_specs=tuple(pl.BlockSpec(memory_space=spaces[kind]) for kind, _ in outs),
        scratch_shapes=scratch,
        compiler_params=pltpu.CompilerParams(vmem_limit_bytes=limit),
        cost_estimate=estimate,
    )(*(value for _, value in ins))


def flipped(axis, bit):
    count = lax.axis_size(axis)
    return [(i, i ^ bit) for i in range(count)]


def rotated(axis, digit, radix, by):
    count = lax.axis_size(axis)

    def target(i):
        value = i // digit % radix
        other = value ^ by if radix & (radix - 1) == 0 else (value + by) % radix
        return i + (other - value) * digit

    return [(i, target(i)) for i in range(count)]


def partners(radix):
    return [2, 3, 1] if radix == 4 else range(radix - 1, 0, -1)


def radices(count):
    out = [] if count % 2 else [2]
    rest = count // 2 if out else count
    factor = 4
    while rest > 1:
        while factor > 1 and rest % factor:
            factor -= 1
        if factor == 1:
            factor = rest
        out.append(factor)
        rest //= factor
        factor = min(factor, 4)
    return out


def per_device(increment, previous, beta_prev, members, band_widths, diffusion_steps):
    levels, rows, width = increment.shape
    tiles, mems = lax.axis_size("tile"), lax.axis_size("mem")
    owned = members.shape[0]
    tall, deep = up_to(levels, 8), up_to(levels, 16)
    inverse = 1.0 / (owned * mems - 1)
    cells = levels * rows * tiles * width
    lanes = width // 128
    inc = increment.reshape(levels * rows, width)
    prev = previous.reshape(levels * rows, width)
    bands = band_widths.reshape(1, levels)
    s_high, s_low, waves = sine_matrix(width)
    edge = (owned, DIFF, tall, width)
    part = (rows - 2 * DIFF) // 2
    near_pairs = [(i, i ^ 1) for i in range(tiles) if i ^ 1 < tiles]
    far_pairs = [pair for i in range(1, tiles - 1, 2) for pair in ((i, i + 1), (i + 1, i))]
    pad = pltpu.VMEM((8, 128), F32)

    packed = (owned, lanes, DIFF * levels, 128)
    (near_edge,) = call(
        functools.partial(product_kernel, rows, levels),
        [("h", members), ("h", increment)],
        [packed],
        [
            pltpu.VMEM((owned, levels, 8, width), jnp.bfloat16),
            pltpu.VMEM((levels, 8, width), F32),
            pltpu.VMEM((lanes, levels * 8, 128), F32),
            pltpu.SemaphoreType.DMA((owned + 1,)),
        ],
        limit=EDGE_LIMIT,
    )
    mem = members.reshape(owned, levels * rows, width)
    bands, near_edge = lax.optimization_barrier((bands, near_edge))
    near_halo = lax.ppermute(near_edge, "tile", near_pairs)
    size = half_span(levels)
    half_packed = (owned, lanes, DIFF * size, 128)
    pair = flipped("mem", 1)
    far_edge, far_edge_other = call(
        functools.partial(edge_kernel, rows, levels),
        [("v", bands), ("v", mem), ("v", inc), ("v", s_high), ("v", s_low)],
        [half_packed] * 2,
        [pltpu.VMEM((lanes, deep * rows, 128), F32), pad, pltpu.VMEM(packed, F32)],
    )
    far_edge_other = lax.ppermute(far_edge_other, "mem", pair)
    members, far_edge = lax.optimization_barrier((members, far_edge))
    mem = members.reshape(owned, levels * rows, width)

    piece, four = (part, tall, width), (DIFF, tall, width)
    short = (DIFF, up_to(size, 8), width)
    mine, theirs, cov_near, cov_far, cov_far_other, mem_near = call(
        functools.partial(own_kernel, rows, levels, tiles),
        [("v", bands), ("s", diffusion_steps), ("v", mem), ("v", inc)]
        + [("v", s_high), ("v", s_low), ("v", waves)],
        [piece, piece, four, short, short, edge],
        [pltpu.VMEM((lanes, deep * rows, 128), F32)] * 2
        + [pltpu.VMEM((rows, tall, width), F32)] * 2
        + [pltpu.VMEM((DIFF, 3, 8, width), F32), pad],
        (20_000_000, 1_000_000),
    )
    prev, _ = lax.optimization_barrier((prev, theirs))
    inc_t, prev_t, mem_far, mem_far_other = call(
        functools.partial(turn_kernel, rows, levels),
        [("v", inc), ("v", prev), ("v", mem)],
        [(rows, tall, width)] * 2 + [half_packed] * 2,
        [pltpu.VMEM((lanes, tall * rows, 128), F32), pltpu.VMEM(packed, F32)],
    )
    mem_far_other = lax.ppermute(mem_far_other, "mem", pair)
    theirs, far_edge_other = lax.optimization_barrier((theirs, far_edge_other))
    far_edge = jnp.concatenate([far_edge, far_edge_other])
    far_halo = lax.ppermute(far_edge, "tile", far_pairs)
    bits = [1 << k for k in range(1, mems.bit_length() - 1)]
    mine = mine + lax.ppermute(theirs, "mem", flipped("mem", 1))
    for bit in bits:
        mine = mine + lax.ppermute(mine, "mem", flipped("mem", bit))
    other = lax.ppermute(mine, "mem", flipped("mem", 1))

    cov_far_other = lax.ppermute(cov_far_other, "mem", pair)
    two = (DIFF // 2, tall, width)
    near_mine, near_theirs = call(
        functools.partial(near_kernel, levels, tiles),
        [("v", bands), ("s", diffusion_steps), ("v", near_halo), ("v", mem_near), ("v", cov_near)]
        + [("v", s_high), ("v", s_low), ("v", waves)],
        [two, two],
        [pltpu.VMEM(four, F32), pltpu.VMEM((DIFF, 2, 8, width), F32), pltpu.VMEM((deep, width), F32), pad],
    )
    near_mine = near_mine + lax.ppermute(near_theirs, "mem", flipped("mem", 1))
    for bit in bits:
        near_mine = near_mine + lax.ppermute(near_mine, "mem", flipped("mem", bit))
    near_other = lax.ppermute(near_mine, "mem", flipped("mem", 1))
    cov_far, near_other, inc_t = lax.optimization_barrier((cov_far, near_other, inc_t))
    w_rest, sums = call(
        functools.partial(bulk_kernel, rows, levels, inverse),
        [("s", beta_prev), ("v", mine), ("v", other), ("v", near_mine), ("v", near_other)]
        + [("v", inc_t), ("v", prev_t)],
        [(lanes, levels * rows, 128), (8, 128)],
        [pltpu.VMEM((rows - DIFF, tall, width), F32)],
    )
    (cov,) = call(
        functools.partial(far_kernel, levels, tiles),
        [("s", diffusion_steps), ("v", far_halo), ("v", mem_far), ("v", mem_far_other)]
        + [("v", cov_far), ("v", cov_far_other), ("v", s_high), ("v", s_low), ("v", waves)],
        [short],
        [pltpu.VMEM((2 * owned, *short), F32), pltpu.VMEM((DIFF, 2, 8, width), F32)],
    )
    for bit in bits[:-1]:
        cov = cov + lax.ppermute(cov, "mem", flipped("mem", bit))
    far_sums = [cov, lax.ppermute(cov, "mem", flipped("mem", bits[-1]))]
    far_others = [lax.ppermute(value, "mem", pair) for value in far_sums]
    w_far, sums = call(
        functools.partial(last_kernel, inverse, levels),
        [("s", beta_prev), ("v", sums)]
        + [("v", value) for value in far_sums + far_others + [inc_t, prev_t]],
        [four, (8, 128)],
        [pltpu.VMEM((tall, width), F32)],
    )
    digit = 1
    stages = radices(tiles)
    for index, radix in enumerate(stages):
        parts = [sums] + [lax.ppermute(sums, "tile", rotated("tile", digit, radix, by)) for by in partners(radix)]
        if index < len(stages) - 1:
            (sums,) = call(merge_kernel, [("v", value) for value in parts], [(8, 128)])
        digit *= radix
    out, coefficients = call(
        functools.partial(final_kernel, rows, levels, cells, len(parts)),
        [("v", value) for value in parts] + [("v", w_far), ("v", w_rest), ("v", inc_t), ("v", inc)],
        [("h", (levels * rows, width)), (1, 2)],
        [pltpu.VMEM((lanes, levels * rows, 128), F32), pltpu.SemaphoreType.DMA((4 * lanes,))],
    )
    return out.reshape(levels, rows, width), coefficients.reshape(2)


def solution(mesh):
    in_specs = (
        P(None, "tile", None),
        P(None, "tile", None),
        P(),
        P("mem", None, "tile", None),
        P(),
        P(),
    )
    out_specs = (P(None, "tile", None), P())
    return jax.shard_map(
        per_device, mesh=mesh, in_specs=in_specs, out_specs=out_specs, check_vma=False
    )
```
